32 devices in a mesh: bin: 8 (over z, y), sky: 4 (over x, core).
Axes of the slice: x: 2, y: 2, z: 4, core: 2. Of those that a mesh axis runs over, the one named last changes fastest.
Arguments:
- lensing_maps: bfloat16 [8, 32, 8192], P('bin', 'sky')
- filter_taps: float32 [5, 17], replicated, may hold values from -1.5 to 1.5
- survey_mask: int32 [4, 64], P('sky'), may hold values 0 or 1
- bin_pairs: int32 [36, 2], replicated, may hold values from 0 to 7, as said below
- target_corr: float32 [36, 5, 4], replicated, may hold values from -3 to 3
- pair_weight: float32 [36, 5, 4], replicated, may hold values from 0.3 to 3
Outputs:
- corr_table: float32 [36, 5, 4], replicated
- map_gradient: float32 [8, 32, 8192], P('bin', 'sky')
The draws below stay inside these ranges and needn't reach their ends.
Inputs may be any that keep to these rules, and one draw needn't show every extreme that they name: `bin_pairs`: every unordered pair of the 8 bins, a bin with itself included, is listed exactly once; the order of the list and of the two bins in a row vary.
All inputs are finite; a program needn't handle non-finite values. No bound on the sum of `survey_mask` on one device may be relied on, other than what follows from the above.
Results may differ from the reference program's by a relative error of at most 0.0015.
Values may be sent and summed in bfloat16 or wider, within the bound.
A program may use at most 64 MiB of HBM per device.

```python
import math
import jax
import jax.numpy as jnp
import numpy as np
from jax import lax

BINS = 8
PAIRS = 36
SCALES = 5
HALF = 8
LAGS = 4
NY = 8192
NX = 32


def draw_lensing_maps(key, part):
    amplitude = jax.random.uniform(jax.random.fold_in(key, 3), (BINS, 1, 1), jnp.float32, 0.5, 0.95)
    shared = jax.random.normal(jax.random.fold_in(key, 1), (NX, NY), jnp.float32)
    single = jax.random.normal(jax.random.fold_in(key, 2), (BINS, NX, NY), jnp.float32)
    mixed = amplitude * shared[None] + jnp.sqrt(1.0 - amplitude * amplitude) * single
    return mixed.astype(jnp.bfloat16)


def draw_bin_pairs(key, part):
    upper_row, upper_col = np.triu_indices(BINS)
    ordering = jax.random.permutation(jax.random.fold_in(key, 11), PAIRS)
    flipped = jax.random.randint(jax.random.fold_in(key, 12), (PAIRS,), 0, 2)
    left_bin = jnp.asarray(upper_row, jnp.int32)[ordering]
    right_bin = jnp.asarray(upper_col, jnp.int32)[ordering]
    first_bin = jnp.where(flipped == 1, right_bin, left_bin)
    second_bin = jnp.where(flipped == 1, left_bin, right_bin)
    return jnp.stack([first_bin, second_bin], axis=1).astype(jnp.int32)


def with_ends(entries, own_key, least, largest):
    longest = entries.shape.index(max(entries.shape))
    spots = []
    for shift in (0, 1):
        where = [jax.random.randint(jax.random.fold_in(own_key, axis), (), 0, length) for axis, length in enumerate(entries.shape)]
        where[longest] = (where[longest] + shift) % entries.shape[longest]
        spots.append(tuple(where))
    return entries.at[spots[0]].set(least).at[spots[1]].set(largest)


def gaussian(own_key, extent, deviation, limit, held_as=jnp.bfloat16):
    entries = deviation * jax.random.normal(own_key, extent, jnp.float32)
    return jnp.clip(entries, min=-limit, max=limit).astype(held_as)


def setup_inputs(seed: int = 0) -> dict:
    arg_keys = jax.random.split(jax.random.key(seed), 7)
    return {
        "lensing_maps": draw_lensing_maps(jax.random.fold_in(arg_keys[6], 71), 0),
        "filter_taps": gaussian(arg_keys[1], (SCALES, 2 * HALF + 1), (2 * HALF + 1) ** -0.5, 1.5, jnp.float32),
        "survey_mask": with_ends((jax.random.randint(arg_keys[2], (NX // 8, NY // 128), 0, 4) < 3).astype(jnp.int32), jax.random.fold_in(arg_keys[2], 1), 0, 1),
        "bin_pairs": draw_bin_pairs(jax.random.fold_in(arg_keys[6], 71), 0),
        "target_corr": gaussian(arg_keys[4], (PAIRS, SCALES, LAGS), 0.5, 3.0, jnp.float32),
        "pair_weight": jnp.clip(jnp.exp(jax.random.uniform(arg_keys[5], (PAIRS, SCALES, LAGS), jnp.float32, math.log(0.3), math.log(3.0))), 0.3, 3.0),
    }


HIGH = lax.Precision.HIGHEST


def expand_mask(survey_mask):
    values = survey_mask.astype(jnp.float32)
    tiles_x, tiles_y = values.shape
    return jnp.broadcast_to(values[:, None, :, None], (tiles_x, 8, tiles_y, 128)).reshape(tiles_x * 8, tiles_y * 128)


def smooth(haloed, filter_taps, row_count):
    tap_count = filter_taps.shape[1]
    half_width = (tap_count - 1) // 2
    widened = haloed.astype(jnp.float32)
    across = filter_taps[:, 0, None, None] * widened[None, 0:row_count]
    for a in range(1, tap_count):
        across = across + filter_taps[:, a, None, None] * widened[None, a:a + row_count]
    padded = jnp.pad(across, ((0, 0), (0, 0), (half_width, half_width)))
    col_count = widened.shape[1]
    result = filter_taps[:, 0, None, None] * padded[:, :, 0:col_count]
    for c in range(1, tap_count):
        result = result + filter_taps[:, c, None, None] * padded[:, :, c:c + col_count]
    return result.astype(jnp.bfloat16)


def lagged(left_maps, right_maps, pixmask, lag_count):
    col_count = left_maps.shape[2]
    columns = []
    for offset in range(lag_count):
        joint_mask = pixmask[:, :col_count - offset] * pixmask[:, offset:]
        product = left_maps[:, :, :col_count - offset].astype(jnp.float32) * right_maps[:, :, offset:].astype(jnp.float32) * joint_mask[None]
        columns.append(jnp.sum(product, axis=(1, 2)))
    return jnp.stack(columns, axis=1)


def adjoint_lags(partner, ahead_w, behind_w, pixmask):
    col_count = partner.shape[2]
    widened = partner.astype(jnp.float32)
    totals = jnp.zeros(partner.shape, jnp.float32)
    for offset in range(ahead_w.shape[1]):
        joint_mask = pixmask[:, :col_count - offset] * pixmask[:, offset:]
        front = jnp.pad(joint_mask[None] * widened[:, :, offset:], ((0, 0), (0, 0), (0, offset)))
        back = jnp.pad(joint_mask[None] * widened[:, :, :col_count - offset], ((0, 0), (0, 0), (offset, 0)))
        totals = totals + ahead_w[:, offset, None, None] * front + behind_w[:, offset, None, None] * back
    return totals


def adjoint_cols(grads, filter_taps):
    tap_count = filter_taps.shape[1]
    half_width = (tap_count - 1) // 2
    col_count = grads.shape[2]
    padded = jnp.pad(grads, ((0, 0), (0, 0), (half_width, half_width)))
    result = filter_taps[:, tap_count - 1, None, None] * padded[:, :, 0:col_count]
    for c in range(1, tap_count):
        result = result + filter_taps[:, tap_count - 1 - c, None, None] * padded[:, :, c:c + col_count]
    return result


def adjoint_rows(widened, filter_taps, row_count):
    tap_count = filter_taps.shape[1]
    result = filter_taps[:, tap_count - 1, None, None] * widened[:, 0:row_count]
    for a in range(1, tap_count):
        result = result + filter_taps[:, tap_count - 1 - a, None, None] * widened[:, a:a + row_count]
    return jnp.sum(result, axis=0)


def reference(lensing_maps, filter_taps, survey_mask, bin_pairs, target_corr, pair_weight):
    half_width = (filter_taps.shape[1] - 1) // 2
    pixmask = expand_mask(survey_mask)
    lag_count = pair_weight.shape[2]
    inverse_area = 1.0 / (NX * NY)

    def filter_one(one_map):
        return smooth(jnp.pad(one_map, ((half_width, half_width), (0, 0))), filter_taps, NX)

    filtered = lax.map(filter_one, lensing_maps)

    def row_of(left_maps):
        def with_partner(partner):
            return lagged(left_maps, partner, pixmask, lag_count) * inverse_area
        return lax.map(with_partner, filtered)

    pair_table = lax.map(row_of, filtered)
    indices = jnp.arange(BINS, dtype=jnp.int32)
    left_hot = (bin_pairs[:, 0:1] == indices[None, :]).astype(jnp.float32)
    right_hot = (bin_pairs[:, 1:2] == indices[None, :]).astype(jnp.float32)
    corr_table = jnp.einsum('pi,pj,ijsl->psl', left_hot, right_hot, pair_table, precision=HIGH)
    pair_grad = pair_weight * (corr_table - target_corr)
    table_grad = jnp.einsum('pi,pj,psl->ijsl', left_hot, right_hot, pair_grad, precision=HIGH)

    def grad_one(inputs):
        row_grad, col_grad = inputs

        def gather_term(totals, terms):
            partner, ahead_w, behind_w = terms
            return totals + adjoint_lags(partner, ahead_w, behind_w, pixmask), None

        totals, _ = lax.scan(gather_term, jnp.zeros((SCALES, NX, NY), jnp.float32), (filtered, row_grad, col_grad))
        col_pass = adjoint_cols(totals, filter_taps)
        widened = jnp.pad(col_pass, ((0, 0), (half_width, half_width), (0, 0)))
        return adjoint_rows(widened, filter_taps, NX)

    map_gradient = lax.map(grad_one, (table_grad, jnp.transpose(table_grad, (1, 0, 2, 3))))
    return (corr_table, map_gradient)
```

```python
import functools

import jax
import jax.numpy as jnp
from jax import lax
from jax.experimental import pallas as pl
from jax.experimental.pallas import tpu as pltpu
from jax.sharding import PartitionSpec as P

F32 = jnp.float32
BF16 = jnp.bfloat16
XB = 32
MESH = pl.DeviceIdType.MESH
VMEM_LIMIT = 60 * 1024 * 1024


def round_up(n, m):
    return -(-n // m) * m


def halves(value):
    hi = value.astype(BF16)
    lo = (value - hi.astype(F32)).astype(BF16)
    return hi, lo


def mm(a, b):
    return jnp.dot(a, b, preferred_element_type=F32)


def mm3(a, b):
    return mm(a[0], b[0]) + mm(a[0], b[1]) + mm(a[1], b[0])


def place(bins, sky):
    return lax.axis_index("bin") * sky + lax.axis_index("sky")


def greet(me, bins, sky):
    count = bins * sky
    barrier = pltpu.get_barrier_semaphore()

    def hello(k, carry):
        other = lax.rem(me + k, count)
        pl.semaphore_signal(
            barrier, inc=1, device_id=(other // sky, lax.rem(other, sky)), device_id_type=MESH
        )
        return carry

    lax.fori_loop(1, count, hello, 0)
    pl.semaphore_wait(barrier, count - 1)


def band(row, height, width, shift, out_width):
    full = pltpu.roll(
        jnp.broadcast_to(row, (height, width)), width - shift, 1, stride=1, stride_axis=0
    )
    return full[:, :out_width]


def same_row(count):
    left = lax.rem(lax.broadcasted_iota(jnp.int32, (count, count), 0), XB)
    right = lax.rem(lax.broadcasted_iota(jnp.int32, (count, count), 1), XB)
    return (left == right).astype(F32)


def step_kernel(
    bins, sky, scales, lags, groups, chunk, halo, tiles, half, area, src_of, dst_of,
    x_ref, mark_ref, tap_ref, pair_ref, fit_ref,
    result_ref, corr_ref,
    y_ref, marks_ref, hi_ref, lo_ref, g_ref, sums_ref, grad_ref,
    col_ref, adj_ref, part_ref, sky_ref, bin_in_ref, bin_ref,
    send_x, recv_x, send_m, recv_m, send_s, recv_s, send_b, recv_b, send_g, recv_g, own_sem, coef_ref,
):
    count = bins * sky
    strip_rows, width = y_ref.shape[1], y_ref.shape[2]
    pieces, part_width = grad_ref.shape[0], grad_ref.shape[3]
    span = adj_ref.shape[2]
    size = bins * XB
    rows = groups * XB
    my_bin, my_sky = lax.axis_index("bin"), lax.axis_index("sky")
    me = place(bins, sky)
    greet(me, bins, sky)

    def window_copy(other, slot):
        return pltpu.make_async_remote_copy(
            src_ref=src_of(x_ref, other),
            dst_ref=y_ref.at[slot],
            send_sem=send_x.at[other],
            recv_sem=recv_x.at[slot],
            device_id=(other // sky, lax.rem(other, sky)),
            device_id_type=MESH,
        )

    def along(axis, src, dst, send, recv, other, slot):
        return pltpu.make_async_remote_copy(
            src_ref=src,
            dst_ref=dst.at[slot],
            send_sem=send.at[other],
            recv_sem=recv.at[slot],
            device_id=(my_bin, other) if axis == "sky" else (other, my_sky),
            device_id_type=MESH,
        )

    def each(n, mine, act):
        def body(k, carry):
            act(lax.rem(mine + k, n))
            return carry

        lax.fori_loop(1, n, body, 0)

    each(sky, my_sky, lambda o: along("sky", mark_ref, marks_ref, send_m, recv_m, o, my_sky).start())
    each(count, me, lambda o: window_copy(o, me).start())
    own_mark = pltpu.make_async_copy(mark_ref, marks_ref.at[my_sky], own_sem.at[0])
    own_mark.start()
    own = pltpu.make_async_copy(src_of(x_ref, me), y_ref.at[me], own_sem.at[1])
    own.start()

    tall = tap_ref.shape[3]
    row_hi, row_lo, back_hi, back_lo = [], [], [], []
    narrow = round_up(rows + 2 * half + 1, 128)
    for s in range(scales):
        taps, turned = tap_ref[0, s], tap_ref[1, s]
        for at, part in enumerate(halves(band(turned[:, :width], width, width, half, width))):
            col_ref[at, s] = part
        for at, part in enumerate(
            halves(band(taps[:, :span], span, span, half + halo, part_width))
        ):
            adj_ref[at, s] = part
        a, b = halves(band(taps[:, :narrow], rows, narrow, half, rows))
        row_hi.append(a)
        row_lo.append(b)
        back = band(turned[:, :narrow], rows, narrow, half, rows)
        back_hi.append(back)
    row_hi = jnp.concatenate(row_hi, axis=0)
    row_lo = jnp.concatenate(row_lo, axis=0)
    back = halves(jnp.concatenate(back_hi, axis=1))
    diag = same_row(size)
    lanes = lax.broadcasted_iota(jnp.int32, (size, width), 1)
    owned = (lanes >= halo) & (lanes < halo + chunk)
    spot = lax.rem(lax.broadcasted_iota(jnp.int32, (bins, size), 1), XB)
    bin_row = lax.broadcasted_iota(jnp.int32, (bins, size), 0)

    pairs = fit_ref.shape[1]
    first = jnp.broadcast_to(pair_ref[:, 0:1], (pairs, size))
    second = jnp.broadcast_to(pair_ref[:, 1:2], (pairs, size))
    right_hot = lax.broadcasted_iota(jnp.int32, (pairs, size), 1) // XB == second
    weight = jnp.zeros((bins, size), F32)
    target = jnp.zeros((bins, size), F32)
    for i in range(bins):
        hot = right_hot & (first == i)
        weight_row = jnp.sum(jnp.where(hot, fit_ref[0], 0.0), axis=0, keepdims=True)
        target_row = jnp.sum(jnp.where(hot, fit_ref[1], 0.0), axis=0, keepdims=True)
        weight = jnp.where(bin_row == i, weight_row, weight)
        target = jnp.where(bin_row == i, target_row, target)
    sums_ref[...] = jnp.zeros_like(sums_ref)

    each(sky, my_sky, lambda o: along("sky", mark_ref, marks_ref, send_m, recv_m, o, o).wait())
    own_mark.wait()
    each(count, me, lambda o: window_copy(o, o).wait())
    own.wait()

    mark_width = mark_ref.shape[1]
    start = me * chunk - halo + 128
    marks = marks_ref[...].reshape(rows, mark_width)
    marks = pltpu.roll(marks, lax.rem(mark_width - start // 128, mark_width), 1)
    which = (lax.broadcasted_iota(jnp.int32, (rows, width), 1) + start) // 128 - start // 128
    mask = jnp.zeros((rows, width), F32)
    for t in range(tiles):
        mask = jnp.where(which == t, jnp.broadcast_to(marks[:, t : t + 1], (rows, width)), mask)
    masks = [
        jnp.concatenate([mask[g * XB : (g + 1) * XB]] * bins, axis=0) > 0 for g in range(groups)
    ]

    for b in range(bins):
        y = jnp.concatenate([y_ref[b * sky + k].astype(F32) for k in range(sky)], axis=0)
        y = y.astype(BF16)
        hi, lo = halves(mm(row_hi, y) + mm(row_lo, y))
        for s in range(scales):
            for g in range(groups):
                part = slice(s * rows + g * XB, s * rows + (g + 1) * XB)
                hi_ref[g, s, b * XB : (b + 1) * XB, :] = hi[part]
                lo_ref[g, s, b * XB : (b + 1) * XB, :] = lo[part]

    for g in range(groups):

        def forward(s, carry):
            matrix = (col_ref[0, s], col_ref[1, s])
            filtered = mm3((hi_ref[g, s], lo_ref[g, s]), matrix).astype(BF16).astype(F32)
            kept = jnp.where(masks[g], filtered, 0.0)
            g_ref[g, s] = kept.astype(BF16)
            left = jnp.where(owned, kept, 0.0).astype(BF16)
            for l in range(lags):
                right = kept if l == 0 else pltpu.roll(kept, width - l, 1)
                gram = lax.dot_general(
                    left, right.astype(BF16), (((1,), (1,)), ((), ())), preferred_element_type=F32
                )
                gram = jnp.sum((gram * diag).reshape(bins, XB, size), axis=1)
                sums_ref[s * lags + l] = sums_ref[s * lags + l] + gram
            return carry

        lax.fori_loop(0, scales, forward, 0)

    table = jnp.zeros((bins, size), F32)
    for at in range(scales * lags):
        value = sums_ref[at]
        for step in (16, 8, 4, 2, 1):
            value = value + pltpu.roll(value, size - step, 1)
        if at:
            value = pltpu.roll(value, at, 1)
        table = jnp.where(spot == at, value, table)

    part_ref[...] = table
    each(sky, my_sky, lambda o: along("sky", part_ref, sky_ref, send_s, recv_s, o, my_sky).start())
    sky_ref[pl.ds(my_sky, 1)] = table[None]
    each(sky, my_sky, lambda o: along("sky", part_ref, sky_ref, send_s, recv_s, o, o).wait())
    table = sky_ref[0]
    for k in range(1, sky):
        table = table + sky_ref[k]
    bin_in_ref[...] = table
    each(bins, my_bin, lambda o: along("bin", bin_in_ref, bin_ref, send_b, recv_b, o, my_bin).start())
    bin_ref[pl.ds(my_bin, 1)] = table[None]
    each(bins, my_bin, lambda o: along("bin", bin_in_ref, bin_ref, send_b, recv_b, o, o).wait())
    table = bin_ref[0]
    for k in range(1, bins):
        table = table + bin_ref[k]
    table = table * area

    picked = jnp.zeros((pairs, size), F32)
    for i in range(bins):
        picked = jnp.where(first == i, jnp.broadcast_to(table[i : i + 1], (pairs, size)), picked)
    picked = jnp.where(right_hot, picked, 0.0)
    step = size // 2
    while step >= XB:
        picked = picked + pltpu.roll(picked, step, 1)
        step //= 2
    corr_ref[...] = picked

    ahead = jnp.where(spot < scales * lags, weight * (table - target), 0.0)
    spread = jnp.broadcast_to(ahead[:, None, :], (bins, XB, size)).reshape(size, size)
    behind = jnp.sum(jnp.transpose(spread * diag).reshape(bins, XB, size), axis=1)

    def coefficient(values, at):
        value = jnp.where(spot == at, values, 0.0)
        value = pltpu.roll(value, lax.rem(size - at, size), 1)
        for step in (1, 2, 4, 8, 16):
            value = value + pltpu.roll(value, step, 1)
        return value

    def grad_copy(piece, other, slot):
        return pltpu.make_async_remote_copy(
            src_ref=grad_ref.at[piece, other],
            dst_ref=dst_of(result_ref, slot, piece),
            send_sem=send_g.at[piece, other],
            recv_sem=recv_g.at[piece, slot],
            device_id=(other // sky, lax.rem(other, sky)),
            device_id_type=MESH,
        )

    own_grads = []
    for piece in range(pieces):
        cut = slice(piece * part_width, piece * part_width + span)
        for g in range(groups):

            def backward(s, carry):
                maps = g_ref[g, s, :, cut].astype(F32)
                total_grad = jnp.zeros((size, span), F32)
                for shift in range(1 - lags, lags):
                    moved = maps if shift == 0 else pltpu.roll(maps, (span - shift) % span, 1)
                    moved = moved.astype(BF16)
                    at = s * (2 * lags - 1) + shift + lags - 1
                    if piece == 0:
                        if shift == 0:
                            coef = coefficient(ahead + behind, s * lags)
                        elif shift > 0:
                            coef = coefficient(ahead, s * lags + shift)
                        else:
                            coef = coefficient(behind, s * lags - shift)
                        if pieces > 1 or groups > 1:
                            coef_ref[at] = coef
                    else:
                        coef = coef_ref[at]
                    full = jnp.broadcast_to(coef[:, None, :], (bins, XB, size))
                    hi, lo = halves(full.reshape(size, size) * diag)
                    total_grad = total_grad + mm(hi, moved) + mm(lo, moved)
                total_grad = jnp.where(masks[g][:, cut], total_grad, 0.0)
                hi, lo = halves(mm3(halves(total_grad), (adj_ref[0, s], adj_ref[1, s])))
                hi_ref[g, s, :, :part_width] = hi
                lo_ref[g, s, :, :part_width] = lo
                return carry

            lax.fori_loop(0, scales, backward, 0)

        for b in range(bins):
            spots = [(g, s) for s in range(scales) for g in range(groups)]
            rows_of = slice(b * XB, (b + 1) * XB)
            hi = jnp.concatenate([hi_ref[g, s, rows_of, :part_width] for g, s in spots], axis=0)
            lo = jnp.concatenate([lo_ref[g, s, rows_of, :part_width] for g, s in spots], axis=0)
            total_rows = mm3(back, (hi, lo))
            for k in range(sky):
                at = b * sky + k
                grad_ref[piece, at] = total_rows[k * strip_rows : (k + 1) * strip_rows]

        each(count, me, lambda o: grad_copy(piece, o, me).start())
        own_grad = pltpu.make_async_copy(
            grad_ref.at[piece, me], dst_of(result_ref, me, piece), own_sem.at[2 + piece]
        )
        own_grad.start()
        own_grads.append(own_grad)
    for piece in range(pieces):
        each(count, me, lambda o: grad_copy(piece, o, o).wait())
        own_grads[piece].wait()


def per_device(lensing_maps, filter_taps, survey_mask, bin_pairs, target_corr, pair_weight):
    scales, tap_count = filter_taps.shape
    half = (tap_count - 1) // 2
    strip = lensing_maps[0]
    strip_rows, cols = strip.shape
    bins, sky = lax.axis_size("bin"), lax.axis_size("sky")
    count = bins * sky
    pairs, lags = pair_weight.shape[0], pair_weight.shape[2]
    row_count = strip_rows * sky
    groups = row_count // XB
    chunk = cols // count
    width = round_up(chunk + 2 * (2 * half + lags - 1), 128)
    halo = (width - chunk) // 2
    out_width = round_up(chunk, 128)
    tiles = width // 128 + 1
    size = bins * XB
    aligned = chunk % 128 == 0
    pieces = out_width // 128
    part_width = out_width // pieces
    span = width - (pieces - 1) * part_width

    windows = jnp.pad(strip, ((0, 0), (halo, halo)))
    if not aligned:
        windows = jnp.stack([windows[:, d * chunk : d * chunk + width] for d in range(count)])
    mark_width = round_up(survey_mask.shape[1] + 1 + tiles, 128)
    marks = jnp.pad(
        survey_mask.astype(F32), ((0, 0), (1, mark_width - survey_mask.shape[1] - 1))
    )
    marks = jnp.broadcast_to(marks, (strip_rows, mark_width))
    tall = max(width, round_up(row_count + 2 * half + 1, 128))
    taps = jnp.stack([filter_taps, filter_taps[:, ::-1]])
    taps = jnp.pad(taps, ((0, 0), (0, 0), (0, tall - tap_count)))[:, :, None, :]
    fit = jnp.stack([pair_weight, target_corr]).reshape(2, pairs, scales * lags)
    fit = jnp.tile(jnp.pad(fit, ((0, 0), (0, 0), (0, XB - scales * lags))), (1, 1, bins))

    if aligned:
        src_of = lambda ref, d: ref.at[:, pl.ds(pl.multiple_of(d * chunk, 128), width)]
        dst_of = lambda ref, d, p: ref.at[
            :, pl.ds(pl.multiple_of(d * chunk + p * part_width, 128), part_width)
        ]
        result_shape = (strip_rows, cols)
    else:
        src_of = lambda ref, d: ref.at[d]
        dst_of = lambda ref, d, p: ref.at[d]
        result_shape = (count, strip_rows, out_width)

    spec = pl.BlockSpec(memory_space=pltpu.VMEM)
    table_shape = (bins, size)
    dma = pltpu.SemaphoreType.DMA
    result, corr = pl.pallas_call(
        functools.partial(
            step_kernel, bins, sky, scales, lags, groups, chunk, halo, tiles, half,
            1.0 / (row_count * cols), src_of, dst_of,
        ),
        out_shape=(
            jax.ShapeDtypeStruct(result_shape, F32),
            jax.ShapeDtypeStruct((pairs, size), F32),
        ),
        in_specs=[spec] * 5,
        out_specs=(spec, spec),
        scratch_shapes=[
            pltpu.VMEM((count, strip_rows, width), BF16),
            pltpu.VMEM((sky, strip_rows, mark_width), F32),
            pltpu.VMEM((groups, scales, size, width), BF16),
            pltpu.VMEM((groups, scales, size, width), BF16),
            pltpu.VMEM((groups, scales, size, width), BF16),
            pltpu.VMEM((scales * lags,) + table_shape, F32),
            pltpu.VMEM((pieces, count, strip_rows, part_width), F32),
            pltpu.VMEM((2, scales, width, width), BF16),
            pltpu.VMEM((2, scales, span, part_width), BF16),
            pltpu.VMEM(table_shape, F32),
            pltpu.VMEM((sky,) + table_shape, F32),
            pltpu.VMEM(table_shape, F32),
            pltpu.VMEM((bins,) + table_shape, F32),
            dma((count,)), dma((count,)), dma((sky,)), dma((sky,)), dma((sky,)), dma((sky,)),
            dma((bins,)), dma((bins,)), dma((pieces, count)), dma((pieces, count)), dma((2 + pieces,)),
            pltpu.VMEM((scales * (2 * lags - 1),) + table_shape, F32),
        ],
        compiler_params=pltpu.CompilerParams(
            collective_id=1, has_side_effects=True, vmem_limit_bytes=VMEM_LIMIT
        ),
    )(windows, marks, taps, bin_pairs, fit)
    if not aligned:
        result = jnp.transpose(result[:, :, :chunk], (1, 0, 2)).reshape(strip_rows, cols)
    corr_table = corr[:, : scales * lags].reshape(pairs, scales, lags)
    return (corr_table, result[None])


def tables(bins, scales, lags):
    lane = lax.broadcasted_iota(jnp.int32, (bins, 128), 1)
    high, low = lane // 64, (lane // 8) % 2
    return lane, high, low, 2 * high + low


def slot_rows(scale, lag):
    scale = scale % 4
    return 64 * (scale // 2) + 16 * lag + 8 * (scale % 2)


def thirds(value):
    hi = value.astype(BF16)
    rest = value - hi.astype(F32)
    mid = rest.astype(BF16)
    lo = (rest - mid.astype(F32)).astype(BF16)
    return hi, mid, lo


def nt(a, b):
    return lax.dot_general(a, b, (((1,), (1,)), ((), ())), preferred_element_type=F32)


def fast_kernel(
    bins, sky, scales, lags, chunk, half, area,
    x_ref, tap_ref, mask_ref, pair_ref, target_ref, weight_ref,
    result_ref, corr_ref,
    pad_ref, y_ref, maps_ref, mark_ref, marks_ref, mask_v_ref, mask_w_ref,
    row_hi_ref, row_lo_ref, back_hi_ref, back_lo_ref, fwd_ref, adj_ref,
    small_ref, fit_ref, pairs_ref, table_ref,
    g_ref, moved_ref, coef_ref, t_ref, cg_hi_ref, cg_lo_ref, grad_ref,
    part_ref, sky_ref, bin_in_ref, bin_ref,
    send_x, recv_x, send_m, recv_m, send_s, recv_s, send_b, recv_b, send_g, recv_g, own_sem,
):
    count = bins * sky
    cols = x_ref.shape[1]
    width = y_ref.shape[2]
    halo = (width - chunk) // 2
    pairs = pair_ref.shape[1]
    taps_n = tap_ref.shape[1]
    size = bins * XB
    groups = size // 32
    vregs = part_ref.shape[0]
    my_bin, my_sky = lax.axis_index("bin"), lax.axis_index("sky")
    me = place(bins, sky)

    barrier = pltpu.get_barrier_semaphore()

    def hello(k, carry):
        other = lax.rem(me + k, count)
        pl.semaphore_signal(
            barrier, inc=1, device_id=(other // sky, lax.rem(other, sky)), device_id_type=MESH
        )
        return carry

    lax.fori_loop(1, count, hello, 0)

    def window_copy(other, slot):
        return pltpu.make_async_remote_copy(
            src_ref=pad_ref.at[:, pl.ds(pl.multiple_of(other * chunk, 128), width)],
            dst_ref=y_ref.at[slot],
            send_sem=send_x.at[other],
            recv_sem=recv_x.at[slot],
            device_id=(other // sky, lax.rem(other, sky)),
            device_id_type=MESH,
        )

    def along(axis, src, dst, send, recv, other, slot):
        return pltpu.make_async_remote_copy(
            src_ref=src,
            dst_ref=dst.at[slot],
            send_sem=send.at[other],
            recv_sem=recv.at[slot],
            device_id=(my_bin, other) if axis == "sky" else (other, my_sky),
            device_id_type=MESH,
        )

    def each(n, mine, act):
        def body(k, carry):
            act(lax.rem(mine + k, n))
            return carry

        lax.fori_loop(1, n, body, 0)

    moved_x = pltpu.roll(x_ref[...].astype(F32), halo, 1)
    edge = lax.broadcasted_iota(jnp.int32, (moved_x.shape[0], 128), 1) < halo
    pad_ref[:, :128] = jnp.where(edge, 0.0, moved_x[:, :128]).astype(BF16)
    pad_ref[:, 128:cols] = moved_x[:, 128:].astype(BF16)
    pad_ref[:, cols:] = jnp.where(edge, moved_x[:, :128], 0.0).astype(BF16)
    mark_ref[...] = jnp.zeros_like(mark_ref)
    mark_ref[:, : mask_ref.shape[1]] = jnp.broadcast_to(
        mask_ref[...].astype(F32), (mark_ref.shape[0], mask_ref.shape[1])
    )

    pl.semaphore_wait(barrier, count - 1)
    each(count, me, lambda o: window_copy(o, me).start())
    each(sky, my_sky, lambda o: along("sky", mark_ref, marks_ref, send_m, recv_m, o, my_sky).start())
    own = pltpu.make_async_copy(
        pad_ref.at[:, pl.ds(pl.multiple_of(me * chunk, 128), width)], y_ref.at[me], own_sem.at[0]
    )
    own.start()
    marks_ref[pl.ds(my_sky, 1)] = mark_ref[...][None]

    small_ref[...] = jnp.zeros_like(small_ref)
    small_ref[:scales, :taps_n] = tap_ref[...]
    tap_hi, tap_lo = halves(small_ref[...])
    tap_row = lax.broadcasted_iota(jnp.int32, (128, 256), 0)
    tap_col = lax.broadcasted_iota(jnp.int32, (128, 256), 1)
    real = tap_row < taps_n

    def spread(hot):
        hot = (hot & real).astype(F32).astype(BF16)
        return mm(tap_hi, hot) + mm(tap_lo, hot)

    straight = spread(tap_col == tap_row)
    turned = spread(tap_col == taps_n - 1 - tap_row)
    spaced = spread(tap_col == bins * (taps_n - 1 - tap_row))
    sub = lax.broadcasted_iota(jnp.int32, (bins, size), 0)
    col = lax.broadcasted_iota(jnp.int32, (bins, size), 1)
    turns = [pltpu.roll(straight, (XB * b - half) % size, 1) for b in range(bins)]
    for s in range(scales):
        reach = halo + half
        for ref, taps in ((fwd_ref, turned), (adj_ref, straight)):
            hi, lo = halves(band(taps[s : s + 1], 256, 256, reach, 128))
            ref[s, :, :128] = hi
            ref[s, :, 128:] = lo
        first = jnp.zeros((bins, size), F32)
        for b in range(bins):
            first = jnp.where(sub == b, jnp.broadcast_to(turns[b][s : s + 1], (bins, size)), first)
        tiles = [
            jnp.where(col // XB == sub, first if x == 0 else pltpu.roll(first, x, 1), 0.0)
            for x in range(XB)
        ]
        hi, lo = halves(jnp.concatenate(tiles, axis=0))
        row_hi_ref[s] = hi
        row_lo_ref[s] = lo
        first = pltpu.roll(
            jnp.broadcast_to(spaced[s : s + 1], (8, size)), 0, 1, stride=bins, stride_axis=0
        )
        tiles = []
        for b in range(bins):
            for k in range(XB // 8):
                shift = (bins * 8 * k - bins * half + b) % size
                apart = col // bins - sub - 8 * k
                near = (apart <= half) & (apart >= -half)
                tiles.append(jnp.where(near, first if shift == 0 else pltpu.roll(first, shift, 1), 0.0))
        hi, lo = halves(jnp.concatenate(tiles, axis=0))
        back_hi_ref[:, s * size : (s + 1) * size] = hi
        back_lo_ref[:, s * size : (s + 1) * size] = lo

    lane, high, low, slot = tables(bins, scales, lags)
    pairs_ref[...] = jnp.full_like(pairs_ref, -1)
    pairs_ref[:2, :pairs] = pair_ref[...]
    fit_ref[...] = jnp.zeros_like(fit_ref)
    for s in range(scales):
        fit_ref[0, s, :lags, :pairs] = weight_ref[s]
        fit_ref[1, s, :lags, :pairs] = target_ref[s]
    bin_of = lax.broadcasted_iota(jnp.int32, (bins, 128), 0)
    first_hot = (pairs_ref[0:1, :] == bin_of).astype(F32)
    second_hot = pairs_ref[1:2, :] == bin_of
    first_hot16 = first_hot.astype(BF16)
    for at in range(2):
        for v in range(vregs):
            tiles = []
            for tile in range(16):
                s, l = 4 * v + 2 * (tile // 8) + tile % 2, (tile // 2) % 4
                if s < scales:
                    row = jnp.broadcast_to(fit_ref[at, s, l : l + 1, :], (bins, 128))
                    tiles.append(jnp.where(second_hot, row, 0.0))
                else:
                    tiles.append(jnp.zeros((bins, 128), F32))
            parts = thirds(jnp.concatenate(tiles, axis=0))
            table_ref[at, v] = nt(first_hot16, parts[0]) + nt(first_hot16, parts[1]) + nt(first_hot16, parts[2])

    each(sky, my_sky, lambda o: along("sky", mark_ref, marks_ref, send_m, recv_m, o, o).wait())
    for k in range(sky):
        marks = pltpu.roll(marks_ref[k], 1, 1)
        marks = pltpu.roll(marks, lax.rem(128 - 2 * me, 128), 1)
        left, one, two, right = [jnp.broadcast_to(marks[:, t : t + 1], (8, 128)) for t in range(4)]
        lanes = lax.broadcasted_iota(jnp.int32, (8, 128), 1)
        mask_v_ref[k, :, :128] = one
        mask_v_ref[k, :, 128:256] = two
        mask_v_ref[k, :, 256:] = jnp.where(lanes < 64, right, left)
        mask_w_ref[k, :, :128] = jnp.where(lanes < 64, left, one)
        mask_w_ref[k, :, 128:256] = jnp.where(lanes < 64, one, two)
        mask_w_ref[k, :, 256:] = jnp.where(lanes < 64, two, right)

    def masked(value, ref):
        tall = size // sky
        return jnp.concatenate(
            [value[k * tall : (k + 1) * tall] * jnp.broadcast_to(ref[k, 0:1, :], (tall, width)) for k in range(sky)],
            axis=0,
        )

    each(count, me, lambda o: window_copy(o, o).wait())
    own.wait()
    for b in range(bins):
        y = jnp.concatenate([y_ref[b * sky + k].astype(F32) for k in range(sky)], axis=0)
        maps_ref[b * XB : (b + 1) * XB, :] = y.astype(BF16)

    def stacked(v):
        return jnp.concatenate(
            [v[:, :256], v[:, 128:], jnp.concatenate([v[:, 256:], v[:, :128]], axis=1)], axis=0
        )

    def forward(s, carry):
        table, last = carry
        y = maps_ref[...]
        hi, lo = halves(mm(row_hi_ref[s], y) + mm(row_lo_ref[s], y))
        p = mm(stacked(hi), fwd_ref[s])
        q = mm(stacked(lo), fwd_ref[s, :, :128])
        f = p[:, :128] + p[:, 128:] + q
        f = jnp.concatenate([f[:size], f[size : 2 * size], f[2 * size :]], axis=1)
        kept16 = masked(f, mask_v_ref).astype(BF16)
        g_ref[s] = kept16
        kept = kept16.astype(F32)
        shifted = [kept16[:, :chunk]] + [
            pltpu.roll(kept, width - l, 1)[:, :chunk].astype(BF16) for l in range(1, lags)
        ]
        total = jnp.zeros((32, 128), F32)
        for g in range(groups):
            right = jnp.concatenate(
                [shifted[l][g * 32 + 16 * h : g * 32 + 16 * h + 16] for h in range(2) for l in range(lags)],
                axis=0,
            )
            total = total + nt(kept16[g * 32 : (g + 1) * 32, :chunk], right)
        z = jnp.zeros((bins, 128), F32)
        for x in range(4):
            z = jnp.where(slot == x, total[bins * x : bins * (x + 1)], z)
        z = z + pltpu.roll(z, 64, 1)
        z = z + jnp.where(low == 0, pltpu.roll(z, 120, 1), pltpu.roll(z, 8, 1))
        return jnp.where(slot == s, z, table), z

    zero = jnp.zeros((bins, 128), F32)
    table, last = lax.fori_loop(0, scales, forward, (zero, zero))
    part_ref[0] = table
    part_ref[1] = last
    each(sky, my_sky, lambda o: along("sky", part_ref, sky_ref, send_s, recv_s, o, my_sky).start())
    sky_ref[pl.ds(my_sky, 1)] = part_ref[...][None]

    def lagging(s, carry):
        kept = g_ref[s].astype(F32)
        for at in range(2 * lags - 1):
            turn = pltpu.roll(kept, halo - (at - lags + 1), 1).astype(BF16)
            for g in range(groups):
                moved_ref[s, g, at * 32 : (at + 1) * 32, :] = turn[g * 32 : (g + 1) * 32]
        return carry

    lax.fori_loop(0, scales, lagging, 0)

    each(sky, my_sky, lambda o: along("sky", part_ref, sky_ref, send_s, recv_s, o, o).wait())
    total = sky_ref[0]
    for k in range(1, sky):
        total = total + sky_ref[k]
    bin_in_ref[...] = total
    each(bins, my_bin, lambda o: along("bin", bin_in_ref, bin_ref, send_b, recv_b, o, my_bin).start())
    bin_ref[pl.ds(my_bin, 1)] = total[None]
    each(bins, my_bin, lambda o: along("bin", bin_in_ref, bin_ref, send_b, recv_b, o, o).wait())
    total = bin_ref[0]
    for k in range(1, bins):
        total = total + bin_ref[k]
    total = total * area

    ahead = [table_ref[0, v] * (total[v] - table_ref[1, v]) for v in range(vregs)]
    over = [jnp.transpose(jnp.concatenate([a] * 16, axis=0)) for a in ahead]
    rows = []
    for s in range(scales):
        back = (128 - slot_rows(s, 0)) % 128
        value = ahead[s // 4] if back == 0 else pltpu.roll(ahead[s // 4], back, 1)
        hi = value.astype(BF16).astype(F32)
        rows += [hi, value - hi]
    e_row = lax.broadcasted_iota(jnp.int32, (128, 256), 0)
    e_col = lax.broadcasted_iota(jnp.int32, (128, 256), 1)
    place_hot = (e_row % 16 < 8) & (e_row // 16 == e_col // 32 - (lags - 1)) & (e_row % 8 == e_col % 8)
    place_hot = place_hot & (e_row < 16 * lags)
    ahead_rows = mm(jnp.concatenate(rows, axis=0).astype(BF16), place_hot.astype(F32).astype(BF16))
    for s in range(scales):
        behind = jnp.zeros((bins, 128), F32)
        for l in range(lags):
            at = slot_rows(s, l)
            behind = jnp.where(lane // 32 == lags - 1 - l, over[s // 4][at : at + 8], behind)
        hi = behind.astype(BF16).astype(F32)
        tiles = []
        for at, value in ((0, hi), (1, behind - hi)):
            z = ahead_rows[(2 * s + at) * 8 : (2 * s + at + 1) * 8]
            value = value.astype(BF16).astype(F32)
            for x in range(4):
                near = (lane // 8) % 4 == x
                tiles.append(
                    jnp.concatenate(
                        [jnp.where(near, z[:, :128] + value, 0.0), jnp.where(near, z[:, 128:], 0.0)], axis=1
                    )
                )
        coef_ref[s] = jnp.concatenate(tiles, axis=0).astype(BF16)

    def backward(s, carry):
        coef = coef_ref[s][:, : 32 * (2 * lags - 1)]
        for g in range(groups):
            t = mm(coef, moved_ref[s, g])
            t_ref[g * 32 : (g + 1) * 32, :] = t[:32] + t[32:]
        hi, lo = halves(masked(t_ref[...], mask_w_ref))
        p = mm(jnp.concatenate([hi[:, :256], hi[:, 128:]], axis=0), adj_ref[s])
        q = mm(jnp.concatenate([lo[:, :256], lo[:, 128:]], axis=0), adj_ref[s, :, :128])
        c = p[:, :128] + p[:, 128:] + q
        hi, lo = halves(jnp.concatenate([c[:size], c[size:]], axis=1))
        cg_hi_ref[s] = hi
        cg_lo_ref[s] = lo
        return carry

    lax.fori_loop(0, scales, backward, 0)
    deep = scales * size
    cg_hi, cg_lo = cg_hi_ref[...].reshape(deep, chunk), cg_lo_ref[...].reshape(deep, chunk)
    out = mm3((back_hi_ref[...], back_lo_ref[...]), (cg_hi, cg_lo))
    grad_ref[...] = out.reshape(count, 8, chunk)

    def grad_copy(other, slot):
        return pltpu.make_async_remote_copy(
            src_ref=grad_ref.at[other],
            dst_ref=result_ref.at[:, pl.ds(pl.multiple_of(slot * chunk, 128), chunk)],
            send_sem=send_g.at[other],
            recv_sem=recv_g.at[slot],
            device_id=(other // sky, lax.rem(other, sky)),
            device_id_type=MESH,
        )

    each(count, me, lambda o: grad_copy(o, me).start())
    own = pltpu.make_async_copy(
        grad_ref.at[me], result_ref.at[:, pl.ds(pl.multiple_of(me * chunk, 128), chunk)], own_sem.at[1]
    )
    own.start()

    hot = jnp.concatenate([first_hot16, jnp.zeros((128 - bins, 128), BF16)], axis=0)
    for v in range(vregs):
        parts = thirds(jnp.transpose(jnp.concatenate([total[v]] * 16, axis=0)))
        picked = mm(parts[0], hot) + mm(parts[1], hot) + mm(parts[2], hot)
        for s in range(4 * v, min(scales, 4 * v + 4)):
            for l in range(lags):
                at = slot_rows(s, l)
                value = jnp.sum(jnp.where(second_hot, picked[at : at + 8], 0.0), axis=0, keepdims=True)
                corr_ref[s, l : l + 1, :] = value[:, :pairs]

    each(count, me, lambda o: grad_copy(o, o).wait())
    own.wait()


def fast_device(lensing_maps, filter_taps, survey_mask, bin_pairs, target_corr, pair_weight):
    scales, tap_count = filter_taps.shape
    half = (tap_count - 1) // 2
    strip = lensing_maps[0]
    strip_rows, cols = strip.shape
    bins, sky = lax.axis_size("bin"), lax.axis_size("sky")
    count = bins * sky
    pairs, lags = pair_weight.shape[0], pair_weight.shape[2]
    chunk = cols // count
    width = chunk + 128
    size = bins * XB
    groups = size // 32
    vregs = 2
    spec = pl.BlockSpec(memory_space=pltpu.VMEM)
    dma = pltpu.SemaphoreType.DMA
    table = (vregs, bins, 128)
    result, corr = pl.pallas_call(
        functools.partial(fast_kernel, bins, sky, scales, lags, chunk, half, 1.0 / (strip_rows * sky * cols)),
        out_shape=(
            jax.ShapeDtypeStruct((strip_rows, cols), F32),
            jax.ShapeDtypeStruct((scales, lags, pairs), F32),
        ),
        in_specs=[spec] * 6,
        out_specs=(spec, spec),
        scratch_shapes=[
            pltpu.VMEM((strip_rows, cols + 128), BF16),
            pltpu.VMEM((count, strip_rows, width), BF16),
            pltpu.VMEM((size, width), BF16),
            pltpu.VMEM((8, 128), F32),
            pltpu.VMEM((sky, 8, 128), F32),
            pltpu.VMEM((sky, 8, width), F32),
            pltpu.VMEM((sky, 8, width), F32),
            pltpu.VMEM((scales, size, size), BF16),
            pltpu.VMEM((scales, size, size), BF16),
            pltpu.VMEM((size, scales * size), BF16),
            pltpu.VMEM((size, scales * size), BF16),
            pltpu.VMEM((scales, 256, 256), BF16),
            pltpu.VMEM((scales, 256, 256), BF16),
            pltpu.VMEM((8, 128), F32),
            pltpu.VMEM((2, scales, 8, 128), F32),
            pltpu.VMEM((8, 128), jnp.int32),
            pltpu.VMEM((2,) + table, F32),
            pltpu.VMEM((scales, size, width), BF16),
            pltpu.VMEM((scales, groups, 32 * (2 * lags - 1), width), BF16),
            pltpu.VMEM((scales, 64, 256), BF16),
            pltpu.VMEM((size, width), F32),
            pltpu.VMEM((scales, size, chunk), BF16),
            pltpu.VMEM((scales, size, chunk), BF16),
            pltpu.VMEM((count, strip_rows, chunk), F32),
            pltpu.VMEM(table, F32),
            pltpu.VMEM((sky,) + table, F32),
            pltpu.VMEM(table, F32),
            pltpu.VMEM((bins,) + table, F32),
            dma((count,)), dma((count,)), dma((sky,)), dma((sky,)), dma((sky,)), dma((sky,)),
            dma((bins,)), dma((bins,)), dma((count,)), dma((count,)), dma((2,)),
        ],
        compiler_params=pltpu.CompilerParams(
            collective_id=1, has_side_effects=True, vmem_limit_bytes=VMEM_LIMIT
        ),
    )(
        strip,
        filter_taps,
        survey_mask,
        bin_pairs.T,
        jnp.transpose(target_corr, (1, 2, 0)),
        jnp.transpose(pair_weight, (1, 2, 0)),
    )
    return (jnp.transpose(corr, (2, 0, 1)), result[None])


def fits(mesh, maps, taps, survey_mask, weight):
    bins, sky = mesh.shape["bin"], mesh.shape["sky"]
    rows, cols = maps.shape[1:]
    return (
        maps.shape[0] == bins == 8
        and rows == XB == 8 * sky
        and cols == 256 * bins * sky
        and survey_mask.shape == (sky, cols // 128)
        and taps.shape[0] <= 8
        and taps.shape[1] == 17
        and weight.shape[0] <= 128
        and weight.shape[2] == 4
    )


def solution(mesh):
    placed = (P("bin", "sky", None), P(), P("sky", None), P(), P(), P())

    def step(lensing_maps, filter_taps, survey_mask, bin_pairs, target_corr, pair_weight):
        fast = fits(mesh, lensing_maps, filter_taps, survey_mask, pair_weight)
        return jax.shard_map(
            fast_device if fast else per_device,
            mesh=mesh,
            in_specs=placed,
            out_specs=(P(), P("bin", "sky", None)),
            check_vma=False,
        )(lensing_maps, filter_taps, survey_mask, bin_pairs, target_corr, pair_weight)

    return step
```

```python
import functools

import jax
import jax.numpy as jnp
from jax import lax
from jax.experimental import pallas as pl
from jax.experimental.pallas import tpu as pltpu
from jax.sharding import PartitionSpec as P

F32 = jnp.float32
BF16 = jnp.bfloat16
XB = 32
MESH = pl.DeviceIdType.MESH
VMEM_LIMIT = 60 * 1024 * 1024


def round_up(n, m):
    return -(-n // m) * m


def halves(value):
    hi = value.astype(BF16)
    lo = (value - hi.astype(F32)).astype(BF16)
    return hi, lo


def mm(a, b):
    return jnp.dot(a, b, preferred_element_type=F32)


def mm3(a, b):
    return mm(a[0], b[0]) + mm(a[0], b[1]) + mm(a[1], b[0])


def place(bins, sky):
    return lax.axis_index("bin") * sky + lax.axis_index("sky")


def greet(me, bins, sky):
    count = bins * sky
    barrier = pltpu.get_barrier_semaphore()

    def hello(k, carry):
        other = lax.rem(me + k, count)
        pl.semaphore_signal(
            barrier, inc=1, device_id=(other // sky, lax.rem(other, sky)), device_id_type=MESH
        )
        return carry

    lax.fori_loop(1, count, hello, 0)
    pl.semaphore_wait(barrier, count - 1)


def band(row, height, width, shift, out_width):
    full = pltpu.roll(
        jnp.broadcast_to(row, (height, width)), width - shift, 1, stride=1, stride_axis=0
    )
    return full[:, :out_width]


def same_row(count):
    left = lax.rem(lax.broadcasted_iota(jnp.int32, (count, count), 0), XB)
    right = lax.rem(lax.broadcasted_iota(jnp.int32, (count, count), 1), XB)
    return (left == right).astype(F32)


def step_kernel(
    bins, sky, scales, lags, groups, chunk, halo, tiles, half, area, src_of, dst_of,
    x_ref, mark_ref, tap_ref, pair_ref, fit_ref,
    result_ref, corr_ref,
    y_ref, marks_ref, hi_ref, lo_ref, g_ref, sums_ref, grad_ref,
    col_ref, adj_ref, part_ref, sky_ref, bin_in_ref, bin_ref,
    send_x, recv_x, send_m, recv_m, send_s, recv_s, send_b, recv_b, send_g, recv_g, own_sem, coef_ref,
):
    count = bins * sky
    strip_rows, width = y_ref.shape[1], y_ref.shape[2]
    pieces, part_width = grad_ref.shape[0], grad_ref.shape[3]
    span = adj_ref.shape[2]
    size = bins * XB
    rows = groups * XB
    my_bin, my_sky = lax.axis_index("bin"), lax.axis_index("sky")
    me = place(bins, sky)
    greet(me, bins, sky)

    def window_copy(other, slot):
        return pltpu.make_async_remote_copy(
            src_ref=src_of(x_ref, other),
            dst_ref=y_ref.at[slot],
            send_sem=send_x.at[other],
            recv_sem=recv_x.at[slot],
            device_id=(other // sky, lax.rem(other, sky)),
            device_id_type=MESH,
        )

    def along(axis, src, dst, send, recv, other, slot):
        return pltpu.make_async_remote_copy(
            src_ref=src,
            dst_ref=dst.at[slot],
            send_sem=send.at[other],
            recv_sem=recv.at[slot],
            device_id=(my_bin, other) if axis == "sky" else (other, my_sky),
            device_id_type=MESH,
        )

    def each(n, mine, act):
        def body(k, carry):
            act(lax.rem(mine + k, n))
            return carry

        lax.fori_loop(1, n, body, 0)

    each(sky, my_sky, lambda o: along("sky", mark_ref, marks_ref, send_m, recv_m, o, my_sky).start())
    each(count, me, lambda o: window_copy(o, me).start())
    own_mark = pltpu.make_async_copy(mark_ref, marks_ref.at[my_sky], own_sem.at[0])
    own_mark.start()
    own = pltpu.make_async_copy(src_of(x_ref, me), y_ref.at[me], own_sem.at[1])
    own.start()

    tall = tap_ref.shape[3]
    row_hi, row_lo, back_hi, back_lo = [], [], [], []
    narrow = round_up(rows + 2 * half + 1, 128)
    for s in range(scales):
        taps, turned = tap_ref[0, s], tap_ref[1, s]
        for at, part in enumerate(halves(band(turned[:, :width], width, width, half, width))):
            col_ref[at, s] = part
        for at, part in enumerate(
            halves(band(taps[:, :span], span, span, half + halo, part_width))
        ):
            adj_ref[at, s] = part
        a, b = halves(band(taps[:, :narrow], rows, narrow, half, rows))
        row_hi.append(a)
        row_lo.append(b)
        back = band(turned[:, :narrow], rows, narrow, half, rows)
        back_hi.append(back)
    row_hi = jnp.concatenate(row_hi, axis=0)
    row_lo = jnp.concatenate(row_lo, axis=0)
    back = halves(jnp.concatenate(back_hi, axis=1))
    diag = same_row(size)
    lanes = lax.broadcasted_iota(jnp.int32, (size, width), 1)
    owned = (lanes >= halo) & (lanes < halo + chunk)
    spot = lax.rem(lax.broadcasted_iota(jnp.int32, (bins, size), 1), XB)
    bin_row = lax.broadcasted_iota(jnp.int32, (bins, size), 0)

    pairs = fit_ref.shape[1]
    first = jnp.broadcast_to(pair_ref[:, 0:1], (pairs, size))
    second = jnp.broadcast_to(pair_ref[:, 1:2], (pairs, size))
    right_hot = lax.broadcasted_iota(jnp.int32, (pairs, size), 1) // XB == second
    weight = jnp.zeros((bins, size), F32)
    target = jnp.zeros((bins, size), F32)
    for i in range(bins):
        hot = right_hot & (first == i)
        weight_row = jnp.sum(jnp.where(hot, fit_ref[0], 0.0), axis=0, keepdims=True)
        target_row = jnp.sum(jnp.where(hot, fit_ref[1], 0.0), axis=0, keepdims=True)
        weight = jnp.where(bin_row == i, weight_row, weight)
        target = jnp.where(bin_row == i, target_row, target)
    sums_ref[...] = jnp.zeros_like(sums_ref)

    each(sky, my_sky, lambda o: along("sky", mark_ref, marks_ref, send_m, recv_m, o, o).wait())
    own_mark.wait()
    each(count, me, lambda o: window_copy(o, o).wait())
    own.wait()

    mark_width = mark_ref.shape[1]
    start = me * chunk - halo + 128
    marks = marks_ref[...].reshape(rows, mark_width)
    marks = pltpu.roll(marks, lax.rem(mark_width - start // 128, mark_width), 1)
    which = (lax.broadcasted_iota(jnp.int32, (rows, width), 1) + start) // 128 - start // 128
    mask = jnp.zeros((rows, width), F32)
    for t in range(tiles):
        mask = jnp.where(which == t, jnp.broadcast_to(marks[:, t : t + 1], (rows, width)), mask)
    masks = [
        jnp.concatenate([mask[g * XB : (g + 1) * XB]] * bins, axis=0) > 0 for g in range(groups)
    ]

    for b in range(bins):
        y = jnp.concatenate([y_ref[b * sky + k].astype(F32) for k in range(sky)], axis=0)
        y = y.astype(BF16)
        hi, lo = halves(mm(row_hi, y) + mm(row_lo, y))
        for s in range(scales):
            for g in range(groups):
                part = slice(s * rows + g * XB, s * rows + (g + 1) * XB)
                hi_ref[g, s, b * XB : (b + 1) * XB, :] = hi[part]
                lo_ref[g, s, b * XB : (b + 1) * XB, :] = lo[part]

    for g in range(groups):

        def forward(s, carry):
            matrix = (col_ref[0, s], col_ref[1, s])
            filtered = mm3((hi_ref[g, s], lo_ref[g, s]), matrix).astype(BF16).astype(F32)
            kept = jnp.where(masks[g], filtered, 0.0)
            g_ref[g, s] = kept.astype(BF16)
            left = jnp.where(owned, kept, 0.0).astype(BF16)
            for l in range(lags):
                right = kept if l == 0 else pltpu.roll(kept, width - l, 1)
                gram = lax.dot_general(
                    left, right.astype(BF16), (((1,), (1,)), ((), ())), preferred_element_type=F32
                )
                gram = jnp.sum((gram * diag).reshape(bins, XB, size), axis=1)
                sums_ref[s * lags + l] = sums_ref[s * lags + l] + gram
            return carry

        lax.fori_loop(0, scales, forward, 0)

    table = jnp.zeros((bins, size), F32)
    for at in range(scales * lags):
        value = sums_ref[at]
        for step in (16, 8, 4, 2, 1):
            value = value + pltpu.roll(value, size - step, 1)
        if at:
            value = pltpu.roll(value, at, 1)
        table = jnp.where(spot == at, value, table)

    part_ref[...] = table
    each(sky, my_sky, lambda o: along("sky", part_ref, sky_ref, send_s, recv_s, o, my_sky).start())
    sky_ref[pl.ds(my_sky, 1)] = table[None]
    each(sky, my_sky, lambda o: along("sky", part_ref, sky_ref, send_s, recv_s, o, o).wait())
    table = sky_ref[0]
    for k in range(1, sky):
        table = table + sky_ref[k]
    bin_in_ref[...] = table
    each(bins, my_bin, lambda o: along("bin", bin_in_ref, bin_ref, send_b, recv_b, o, my_bin).start())
    bin_ref[pl.ds(my_bin, 1)] = table[None]
    each(bins, my_bin, lambda o: along("bin", bin_in_ref, bin_ref, send_b, recv_b, o, o).wait())
    table = bin_ref[0]
    for k in range(1, bins):
        table = table + bin_ref[k]
    table = table * area

    picked = jnp.zeros((pairs, size), F32)
    for i in range(bins):
        picked = jnp.where(first == i, jnp.broadcast_to(table[i : i + 1], (pairs, size)), picked)
    picked = jnp.where(right_hot, picked, 0.0)
    step = size // 2
    while step >= XB:
        picked = picked + pltpu.roll(picked, step, 1)
        step //= 2
    corr_ref[...] = picked

    ahead = jnp.where(spot < scales * lags, weight * (table - target), 0.0)
    spread = jnp.broadcast_to(ahead[:, None, :], (bins, XB, size)).reshape(size, size)
    behind = jnp.sum(jnp.transpose(spread * diag).reshape(bins, XB, size), axis=1)

    def coefficient(values, at):
        value = jnp.where(spot == at, values, 0.0)
        value = pltpu.roll(value, lax.rem(size - at, size), 1)
        for step in (1, 2, 4, 8, 16):
            value = value + pltpu.roll(value, step, 1)
        return value

    def grad_copy(piece, other, slot):
        return pltpu.make_async_remote_copy(
            src_ref=grad_ref.at[piece, other],
            dst_ref=dst_of(result_ref, slot, piece),
            send_sem=send_g.at[piece, other],
            recv_sem=recv_g.at[piece, slot],
            device_id=(other // sky, lax.rem(other, sky)),
            device_id_type=MESH,
        )

    own_grads = []
    for piece in range(pieces):
        cut = slice(piece * part_width, piece * part_width + span)
        for g in range(groups):

            def backward(s, carry):
                maps = g_ref[g, s, :, cut].astype(F32)
                total_grad = jnp.zeros((size, span), F32)
                for shift in range(1 - lags, lags):
                    moved = maps if shift == 0 else pltpu.roll(maps, (span - shift) % span, 1)
                    moved = moved.astype(BF16)
                    at = s * (2 * lags - 1) + shift + lags - 1
                    if piece == 0:
                        if shift == 0:
                            coef = coefficient(ahead + behind, s * lags)
                        elif shift > 0:
                            coef = coefficient(ahead, s * lags + shift)
                        else:
                            coef = coefficient(behind, s * lags - shift)
                        if pieces > 1 or groups > 1:
                            coef_ref[at] = coef
                    else:
                        coef = coef_ref[at]
                    full = jnp.broadcast_to(coef[:, None, :], (bins, XB, size))
                    hi, lo = halves(full.reshape(size, size) * diag)
                    total_grad = total_grad + mm(hi, moved) + mm(lo, moved)
                total_grad = jnp.where(masks[g][:, cut], total_grad, 0.0)
                hi, lo = halves(mm3(halves(total_grad), (adj_ref[0, s], adj_ref[1, s])))
                hi_ref[g, s, :, :part_width] = hi
                lo_ref[g, s, :, :part_width] = lo
                return carry

            lax.fori_loop(0, scales, backward, 0)

        for b in range(bins):
            spots = [(g, s) for s in range(scales) for g in range(groups)]
            rows_of = slice(b * XB, (b + 1) * XB)
            hi = jnp.concatenate([hi_ref[g, s, rows_of, :part_width] for g, s in spots], axis=0)
            lo = jnp.concatenate([lo_ref[g, s, rows_of, :part_width] for g, s in spots], axis=0)
            total_rows = mm3(back, (hi, lo))
            for k in range(sky):
                at = b * sky + k
                grad_ref[piece, at] = total_rows[k * strip_rows : (k + 1) * strip_rows]

        each(count, me, lambda o: grad_copy(piece, o, me).start())
        own_grad = pltpu.make_async_copy(
            grad_ref.at[piece, me], dst_of(result_ref, me, piece), own_sem.at[2 + piece]
        )
        own_grad.start()
        own_grads.append(own_grad)
    for piece in range(pieces):
        each(count, me, lambda o: grad_copy(piece, o, o).wait())
        own_grads[piece].wait()


def per_device(lensing_maps, filter_taps, survey_mask, bin_pairs, target_corr, pair_weight):
    scales, tap_count = filter_taps.shape
    half = (tap_count - 1) // 2
    strip = lensing_maps[0]
    strip_rows, cols = strip.shape
    bins, sky = lax.axis_size("bin"), lax.axis_size("sky")
    count = bins * sky
    pairs, lags = pair_weight.shape[0], pair_weight.shape[2]
    row_count = strip_rows * sky
    groups = row_count // XB
    chunk = cols // count
    width = round_up(chunk + 2 * (2 * half + lags - 1), 128)
    halo = (width - chunk) // 2
    out_width = round_up(chunk, 128)
    tiles = width // 128 + 1
    size = bins * XB
    aligned = chunk % 128 == 0
    pieces = out_width // 128
    part_width = out_width // pieces
    span = width - (pieces - 1) * part_width

    windows = jnp.pad(strip, ((0, 0), (halo, halo)))
    if not aligned:
        windows = jnp.stack([windows[:, d * chunk : d * chunk + width] for d in range(count)])
    mark_width = round_up(survey_mask.shape[1] + 1 + tiles, 128)
    marks = jnp.pad(
        survey_mask.astype(F32), ((0, 0), (1, mark_width - survey_mask.shape[1] - 1))
    )
    marks = jnp.broadcast_to(marks, (strip_rows, mark_width))
    tall = max(width, round_up(row_count + 2 * half + 1, 128))
    taps = jnp.stack([filter_taps, filter_taps[:, ::-1]])
    taps = jnp.pad(taps, ((0, 0), (0, 0), (0, tall - tap_count)))[:, :, None, :]
    fit = jnp.stack([pair_weight, target_corr]).reshape(2, pairs, scales * lags)
    fit = jnp.tile(jnp.pad(fit, ((0, 0), (0, 0), (0, XB - scales * lags))), (1, 1, bins))

    if aligned:
        src_of = lambda ref, d: ref.at[:, pl.ds(pl.multiple_of(d * chunk, 128), width)]
        dst_of = lambda ref, d, p: ref.at[
            :, pl.ds(pl.multiple_of(d * chunk + p * part_width, 128), part_width)
        ]
        result_shape = (strip_rows, cols)
    else:
        src_of = lambda ref, d: ref.at[d]
        dst_of = lambda ref, d, p: ref.at[d]
        result_shape = (count, strip_rows, out_width)

    spec = pl.BlockSpec(memory_space=pltpu.VMEM)
    table_shape = (bins, size)
    dma = pltpu.SemaphoreType.DMA
    result, corr = pl.pallas_call(
        functools.partial(
            step_kernel, bins, sky, scales, lags, groups, chunk, halo, tiles, half,
            1.0 / (row_count * cols), src_of, dst_of,
        ),
        out_shape=(
            jax.ShapeDtypeStruct(result_shape, F32),
            jax.ShapeDtypeStruct((pairs, size), F32),
        ),
        in_specs=[spec] * 5,
        out_specs=(spec, spec),
        scratch_shapes=[
            pltpu.VMEM((count, strip_rows, width), BF16),
            pltpu.VMEM((sky, strip_rows, mark_width), F32),
            pltpu.VMEM((groups, scales, size, width), BF16),
            pltpu.VMEM((groups, scales, size, width), BF16),
            pltpu.VMEM((groups, scales, size, width), BF16),
            pltpu.VMEM((scales * lags,) + table_shape, F32),
            pltpu.VMEM((pieces, count, strip_rows, part_width), F32),
            pltpu.VMEM((2, scales, width, width), BF16),
            pltpu.VMEM((2, scales, span, part_width), BF16),
            pltpu.VMEM(table_shape, F32),
            pltpu.VMEM((sky,) + table_shape, F32),
            pltpu.VMEM(table_shape, F32),
            pltpu.VMEM((bins,) + table_shape, F32),
            dma((count,)), dma((count,)), dma((sky,)), dma((sky,)), dma((sky,)), dma((sky,)),
            dma((bins,)), dma((bins,)), dma((pieces, count)), dma((pieces, count)), dma((2 + pieces,)),
            pltpu.VMEM((scales * (2 * lags - 1),) + table_shape, F32),
        ],
        compiler_params=pltpu.CompilerParams(
            collective_id=1, has_side_effects=True, vmem_limit_bytes=VMEM_LIMIT
        ),
    )(windows, marks, taps, bin_pairs, fit)
    if not aligned:
        result = jnp.transpose(result[:, :, :chunk], (1, 0, 2)).reshape(strip_rows, cols)
    corr_table = corr[:, : scales * lags].reshape(pairs, scales, lags)
    return (corr_table, result[None])


def tables(bins, scales, lags):
    lane = lax.broadcasted_iota(jnp.int32, (bins, 128), 1)
    high, low = lane // 64, (lane // 8) % 2
    return lane, high, low, 2 * high + low


EARLY = 3


def spot_of(scale):
    return (0, scale) if scale < EARLY else (1, scale - EARLY)


def slot_rows(scale, lag):
    slot = spot_of(scale)[1]
    return 64 * (slot // 2) + 16 * lag + 8 * (slot % 2)


def thirds(value):
    hi = value.astype(BF16)
    rest = value - hi.astype(F32)
    mid = rest.astype(BF16)
    lo = (rest - mid.astype(F32)).astype(BF16)
    return hi, mid, lo


def nt(a, b):
    return lax.dot_general(a, b, (((1,), (1,)), ((), ())), preferred_element_type=F32)


def steps(begin, end, body, carry):
    for s in range(begin, end):
        carry = body(s, carry)
    return carry


def fast_kernel(
    bins, sky, scales, lags, chunk, half, area,
    x_hbm, tap_hbm, mask_hbm, pair_hbm, target_hbm, weight_hbm,
    result_ref, corr_ref,
    x_ref, tap_ref, mask_ref, pair_ref, target_ref, weight_ref,
    pad_ref, y_ref, maps_ref, mark_ref, marks_ref, mask_v_ref, mask_w_ref,
    row_hi_ref, row_lo_ref, back_hi_ref, back_lo_ref, fwd_ref, adj_ref,
    small_ref, fit_ref, pairs_ref, table_ref,
    g_ref, moved_ref, coef_ref, t_ref, cg_hi_ref, cg_lo_ref, grad_ref, land_ref,
    part_ref, twin_ref, chip_ref, parts_ref,
    send_x, recv_x, send_m, recv_m, send_c, recv_c, send_t, recv_t, send_g, recv_g, own_sem, in_sem,
):
    count = bins * sky
    cols = x_ref.shape[1]
    width = y_ref.shape[2]
    halo = (width - chunk) // 2
    pairs = pair_ref.shape[1]
    taps_n = tap_ref.shape[1]
    size = bins * XB
    groups = size // 32
    vregs = part_ref.shape[0]
    my_bin, my_sky = lax.axis_index("bin"), lax.axis_index("sky")
    me = place(bins, sky)

    barrier = pltpu.get_barrier_semaphore()

    bits = count.bit_length() - 1
    flips = [(1 - 2 * lax.rem(me // 2**i, 2)) * 2**i for i in range(bits)]

    def across(act):
        def body(k, carry):
            mask = count - 2 - 2 * k
            other = me
            for i in range(1, bits):
                other = other + lax.rem(mask // 2**i, 2) * flips[i]
            act(other)
            return carry

        lax.fori_loop(0, count // 2 - 1, body, 0)

    def each(n, mine, act):
        def body(k, carry):
            act(lax.rem(mine + k, n))
            return carry

        lax.fori_loop(1, n, body, 0)

    def hello(other):
        pl.semaphore_signal(
            barrier, inc=1, device_id=(other // sky, lax.rem(other, sky)), device_id_type=MESH
        )

    each(count, me, hello)
    loads = [
        pltpu.make_async_copy(src, dst, in_sem.at[i])
        for i, (src, dst) in enumerate(
            (
                (x_hbm, x_ref), (mask_hbm, mask_ref), (tap_hbm, tap_ref),
                (pair_hbm, pair_ref), (target_hbm, target_ref), (weight_hbm, weight_ref),
            )
        )
    ]
    for load in loads:
        load.start()

    def window_copy(other, slot):
        return pltpu.make_async_remote_copy(
            src_ref=pad_ref.at[:, pl.ds(pl.multiple_of(other * chunk, 128), width)],
            dst_ref=y_ref.at[slot],
            send_sem=send_x.at[other],
            recv_sem=recv_x.at[slot],
            device_id=(other // sky, lax.rem(other, sky)),
            device_id_type=MESH,
        )

    def along(axis, src, dst, send, recv, other, slot):
        return pltpu.make_async_remote_copy(
            src_ref=src,
            dst_ref=dst.at[slot],
            send_sem=send.at[other],
            recv_sem=recv.at[slot],
            device_id=(my_bin, other) if axis == "sky" else (other, my_sky),
            device_id_type=MESH,
        )

    loads[0].wait()
    loads[1].wait()
    moved_x = pltpu.roll(x_ref[...].astype(F32), halo, 1)
    edge = lax.broadcasted_iota(jnp.int32, (moved_x.shape[0], 128), 1) < halo
    pad_ref[:, :128] = jnp.where(edge, 0.0, moved_x[:, :128]).astype(BF16)
    pad_ref[:, 128:cols] = moved_x[:, 128:].astype(BF16)
    pad_ref[:, cols:] = jnp.where(edge, moved_x[:, :128], 0.0).astype(BF16)
    mark_ref[...] = jnp.zeros_like(mark_ref)
    mark_ref[:, : mask_ref.shape[1]] = jnp.broadcast_to(
        mask_ref[...].astype(F32), (mark_ref.shape[0], mask_ref.shape[1])
    )

    pl.semaphore_wait(barrier, count - 1)
    each(count, me, lambda o: window_copy(o, me).start())
    each(sky, my_sky, lambda o: along("sky", mark_ref, marks_ref, send_m, recv_m, o, my_sky).start())
    own = pltpu.make_async_copy(
        pad_ref.at[:, pl.ds(pl.multiple_of(me * chunk, 128), width)], y_ref.at[me], own_sem.at[0]
    )
    own.start()
    marks_ref[pl.ds(my_sky, 1)] = mark_ref[...][None]

    for load in loads[2:]:
        load.wait()
    small_ref[...] = jnp.zeros_like(small_ref)
    small_ref[:scales, :taps_n] = tap_ref[...]
    tap_hi, tap_lo = halves(small_ref[...])
    tap_row = lax.broadcasted_iota(jnp.int32, (128, 256), 0)
    tap_col = lax.broadcasted_iota(jnp.int32, (128, 256), 1)
    real = tap_row < taps_n

    def spread(hot):
        hot = (hot & real).astype(F32).astype(BF16)
        return mm(tap_hi, hot) + mm(tap_lo, hot)

    straight = spread(tap_col == tap_row)
    turned = spread(tap_col == taps_n - 1 - tap_row)
    spaced = spread(tap_col == bins * (taps_n - 1 - tap_row))
    sub = lax.broadcasted_iota(jnp.int32, (bins, size), 0)
    col = lax.broadcasted_iota(jnp.int32, (bins, size), 1)
    turns = [pltpu.roll(straight, (XB * b - half) % size, 1) for b in range(bins)]
    for s in range(scales):
        reach = halo + half
        for ref, taps in ((fwd_ref, turned), (adj_ref, straight)):
            hi, lo = halves(band(taps[s : s + 1], 256, 256, reach, 128))
            ref[s, :, :128] = hi
            ref[s, :, 128:] = lo
        first = jnp.zeros((bins, size), F32)
        for b in range(bins):
            first = jnp.where(sub == b, jnp.broadcast_to(turns[b][s : s + 1], (bins, size)), first)
        tiles = [
            jnp.where(col // XB == sub, first if x == 0 else pltpu.roll(first, x, 1), 0.0)
            for x in range(XB)
        ]
        hi, lo = halves(jnp.concatenate(tiles, axis=0))
        row_hi_ref[s] = hi
        row_lo_ref[s] = lo
        first = pltpu.roll(
            jnp.broadcast_to(spaced[s : s + 1], (8, size)), 0, 1, stride=bins, stride_axis=0
        )
        tiles = []
        for b in range(bins):
            for k in range(XB // 8):
                shift = (bins * 8 * k - bins * half + b) % size
                apart = col // bins - sub - 8 * k
                near = (apart <= half) & (apart >= -half)
                tiles.append(jnp.where(near, first if shift == 0 else pltpu.roll(first, shift, 1), 0.0))
        hi, lo = halves(jnp.concatenate(tiles, axis=0))
        back_hi_ref[:, s * size : (s + 1) * size] = hi
        back_lo_ref[:, s * size : (s + 1) * size] = lo

    lane, high, low, slot = tables(bins, scales, lags)
    pairs_ref[...] = jnp.full_like(pairs_ref, -1)
    pairs_ref[:2, :pairs] = pair_ref[...]
    fit_ref[...] = jnp.zeros_like(fit_ref)
    for s in range(scales):
        fit_ref[0, s, :lags, :pairs] = weight_ref[s]
        fit_ref[1, s, :lags, :pairs] = target_ref[s]
    bin_of = lax.broadcasted_iota(jnp.int32, (bins, 128), 0)
    first_hot = (pairs_ref[0:1, :] == bin_of).astype(F32)
    second_hot = pairs_ref[1:2, :] == bin_of
    first_hot16 = first_hot.astype(BF16)
    for at in range(2):
        for v in range(vregs):
            tiles = []
            for tile in range(16):
                at_slot, l = 2 * (tile // 8) + tile % 2, (tile // 2) % 4
                s = at_slot + v * EARLY
                if s < scales and spot_of(s) == (v, at_slot):
                    row = jnp.broadcast_to(fit_ref[at, s, l : l + 1, :], (bins, 128))
                    tiles.append(jnp.where(second_hot, row, 0.0))
                else:
                    tiles.append(jnp.zeros((bins, 128), F32))
            parts = thirds(jnp.concatenate(tiles, axis=0))
            table_ref[at, v] = nt(first_hot16, parts[0]) + nt(first_hot16, parts[1]) + nt(first_hot16, parts[2])

    each(sky, my_sky, lambda o: along("sky", mark_ref, marks_ref, send_m, recv_m, o, o).wait())
    for k in range(sky):
        marks = pltpu.roll(marks_ref[k], 1, 1)
        marks = pltpu.roll(marks, lax.rem(128 - 2 * me, 128), 1)
        left, one, two, right = [jnp.broadcast_to(marks[:, t : t + 1], (8, 128)) for t in range(4)]
        lanes = lax.broadcasted_iota(jnp.int32, (8, 128), 1)
        mask_v_ref[k, :, :128] = one
        mask_v_ref[k, :, 128:256] = two
        mask_v_ref[k, :, 256:] = jnp.where(lanes < 64, right, left)
        mask_w_ref[k, :, :128] = jnp.where(lanes < 64, left, one)
        mask_w_ref[k, :, 128:256] = jnp.where(lanes < 64, one, two)
        mask_w_ref[k, :, 256:] = jnp.where(lanes < 64, two, right)

    def masked(value, ref):
        tall = size // sky
        return jnp.concatenate(
            [value[k * tall : (k + 1) * tall] * jnp.broadcast_to(ref[k, 0:1, :], (tall, width)) for k in range(sky)],
            axis=0,
        )

    each(count, me, lambda o: window_copy(o, o).wait())
    own.wait()
    for b in range(bins):
        y = jnp.concatenate([y_ref[b * sky + k].astype(F32) for k in range(sky)], axis=0)
        maps_ref[b * XB : (b + 1) * XB, :] = y.astype(BF16)

    def stacked(v):
        return jnp.concatenate(
            [v[:, :256], v[:, 128:], jnp.concatenate([v[:, 256:], v[:, :128]], axis=1)], axis=0
        )

    def forward(s, carry):
        y = maps_ref[...]
        hi, lo = halves(mm(row_hi_ref[s], y) + mm(row_lo_ref[s], y))
        p = mm(stacked(hi), fwd_ref[s])
        q = mm(stacked(lo), fwd_ref[s, :, :128])
        f = p[:, :128] + p[:, 128:] + q
        f = jnp.concatenate([f[:size], f[size : 2 * size], f[2 * size :]], axis=1)
        kept16 = masked(f, mask_v_ref).astype(BF16)
        g_ref[s] = kept16
        kept = kept16.astype(F32)
        shifted = [kept16[:, :chunk]] + [
            pltpu.roll(kept, width - l, 1)[:, :chunk].astype(BF16) for l in range(1, lags)
        ]
        total = jnp.zeros((32, 128), F32)
        for g in range(groups):
            right = jnp.concatenate(
                [shifted[l][g * 32 + 16 * h : g * 32 + 16 * h + 16] for h in range(2) for l in range(lags)],
                axis=0,
            )
            total = total + nt(kept16[g * 32 : (g + 1) * 32, :chunk], right)
        z = jnp.zeros((bins, 128), F32)
        for x in range(4):
            z = jnp.where(slot == x, total[bins * x : bins * (x + 1)], z)
        z = z + pltpu.roll(z, 64, 1)
        z = z + jnp.where(low == 0, pltpu.roll(z, 120, 1), pltpu.roll(z, 8, 1))
        into = s % EARLY
        return jnp.where(slot == into, z, carry)

    def core_copy(v):
        return pltpu.make_async_remote_copy(
            src_ref=part_ref.at[v],
            dst_ref=twin_ref.at[v],
            send_sem=send_c.at[v],
            recv_sem=recv_c.at[v],
            device_id=((me + flips[0]) // sky, lax.rem(me + flips[0], sky)),
            device_id_type=MESH,
        )

    def table_copy(v, other, to):
        return pltpu.make_async_remote_copy(
            src_ref=chip_ref.at[v],
            dst_ref=parts_ref.at[v, to // 2],
            send_sem=send_t.at[v, other // 2],
            recv_sem=recv_t.at[v, to // 2],
            device_id=(other // sky, lax.rem(other, sky)),
            device_id_type=MESH,
        )

    def send_tables(v):
        core_copy(v).wait()
        chip = part_ref[v] + twin_ref[v]
        chip_ref[v] = chip
        across(lambda o: table_copy(v, o, me).start())
        parts_ref[v, pl.ds(me // 2, 1)] = chip[None]

    zero = jnp.zeros((bins, 128), F32)
    part_ref[0] = steps(0, EARLY, forward, zero)
    core_copy(0).start()
    late = steps(EARLY, EARLY + 1, forward, zero)
    send_tables(0)
    part_ref[1] = steps(EARLY + 1, scales, forward, late)
    core_copy(1).start()

    def lagging(s, carry):
        kept = g_ref[s].astype(F32)
        for at in range(2 * lags - 1):
            turn = pltpu.roll(kept, halo - (at - lags + 1), 1).astype(BF16)
            for g in range(groups):
                moved_ref[s, g, at * 32 : (at + 1) * 32, :] = turn[g * 32 : (g + 1) * 32]
        return carry

    steps(0, 1, lagging, 0)
    send_tables(1)
    steps(1, scales, lagging, 0)

    e_row = lax.broadcasted_iota(jnp.int32, (128, 256), 0)
    e_col = lax.broadcasted_iota(jnp.int32, (128, 256), 1)
    place_hot = (e_row % 16 < 8) & (e_row // 16 == e_col // 32 - (lags - 1)) & (e_row % 8 == e_col % 8)
    place_hot = (place_hot & (e_row < 16 * lags)).astype(F32).astype(BF16)

    def coefficients(v, begin, end):
        across(lambda o: table_copy(v, o, o).wait())
        tables = [parts_ref[v, k] for k in range(count // 2)]
        while len(tables) > 1:
            tables = [tables[k] + tables[k + 1] for k in range(0, len(tables), 2)]
        total = tables[0] * area
        ahead = table_ref[0, v] * (total - table_ref[1, v])
        over = jnp.transpose(jnp.concatenate([ahead] * 16, axis=0))
        rows = []
        for s in range(begin, end):
            back = (128 - slot_rows(s, 0)) % 128
            value = ahead if back == 0 else pltpu.roll(ahead, back, 1)
            hi = value.astype(BF16).astype(F32)
            rows += [hi, value - hi]
        ahead_rows = mm(jnp.concatenate(rows, axis=0).astype(BF16), place_hot)
        for s in range(begin, end):
            behind = jnp.zeros((bins, 128), F32)
            for l in range(lags):
                at = slot_rows(s, l)
                behind = jnp.where(lane // 32 == lags - 1 - l, over[at : at + 8], behind)
            hi = behind.astype(BF16).astype(F32)
            tiles = []
            for at, value in ((0, hi), (1, behind - hi)):
                row = (2 * (s - begin) + at) * 8
                z = ahead_rows[row : row + 8]
                value = value.astype(BF16).astype(F32)
                for x in range(4):
                    near = (lane // 8) % 4 == x
                    tiles.append(
                        jnp.concatenate(
                            [jnp.where(near, z[:, :128] + value, 0.0), jnp.where(near, z[:, 128:], 0.0)], axis=1
                        )
                    )
            coef_ref[s] = jnp.concatenate(tiles, axis=0).astype(BF16)
        return total

    def backward(s, carry):
        coef = coef_ref[s][:, : 32 * (2 * lags - 1)]
        for g in range(groups):
            t = mm(coef, moved_ref[s, g])
            t_ref[g * 32 : (g + 1) * 32, :] = t[:32] + t[32:]
        hi, lo = halves(masked(t_ref[...], mask_w_ref))
        p = mm(jnp.concatenate([hi[:, :256], hi[:, 128:]], axis=0), adj_ref[s])
        q = mm(jnp.concatenate([lo[:, :256], lo[:, 128:]], axis=0), adj_ref[s, :, :128])
        c = p[:, :128] + p[:, 128:] + q
        hi, lo = halves(jnp.concatenate([c[:size], c[size:]], axis=1))
        cg_hi_ref[s] = hi
        cg_lo_ref[s] = lo
        return carry

    totals = []
    for v, (begin, end) in enumerate(((0, EARLY), (EARLY, scales))):
        totals.append(coefficients(v, begin, end))
        steps(begin, end, backward, 0)
    deep = scales * size
    cg_hi, cg_lo = cg_hi_ref[...].reshape(deep, chunk), cg_lo_ref[...].reshape(deep, chunk)
    out = mm3((back_hi_ref[...], back_lo_ref[...]), (cg_hi, cg_lo))

    for k in range(count):
        block = out[8 * k : 8 * k + 8]
        largest = jnp.max(jnp.abs(block), axis=0, keepdims=True)
        largest = jnp.broadcast_to(jnp.max(largest, axis=1, keepdims=True), (8, 128))
        power = jnp.maximum(jnp.ceil(jnp.log2(jnp.maximum(largest, 1e-30)) + 0.001), -90.0)
        scale = jnp.exp2(15.0 - power) * (32766.0 / 32768.0)
        left = jnp.round(block[:, :128] * scale).astype(jnp.int32)
        right = jnp.round(block[:, 128:] * scale).astype(jnp.int32)
        grad_ref[k, :8] = left * 65536 + (right + 32768)
        grad_ref[k, 8:] = power[:1].astype(jnp.int32)

    def grad_copy(other, slot):
        return pltpu.make_async_remote_copy(
            src_ref=grad_ref.at[other],
            dst_ref=land_ref.at[slot],
            send_sem=send_g.at[other],
            recv_sem=recv_g.at[slot],
            device_id=(other // sky, lax.rem(other, sky)),
            device_id_type=MESH,
        )

    each(count, me, lambda o: grad_copy(o, me).start())
    own = pltpu.make_async_copy(grad_ref.at[me], land_ref.at[me], own_sem.at[1])
    own.start()

    hot = jnp.concatenate([first_hot16, jnp.zeros((128 - bins, 128), BF16)], axis=0)
    for v in range(vregs):
        parts = thirds(jnp.transpose(jnp.concatenate([totals[v]] * 16, axis=0)))
        picked = mm(parts[0], hot) + mm(parts[1], hot) + mm(parts[2], hot)
        for s in [s for s in range(scales) if spot_of(s)[0] == v]:
            for l in range(lags):
                at = slot_rows(s, l)
                value = jnp.sum(jnp.where(second_hot, picked[at : at + 8], 0.0), axis=0, keepdims=True)
                corr_ref[s, l : l + 1, :] = value[:, :pairs]

    def unpack(slot):
        word = land_ref[pl.ds(slot, 1), :8][0]
        power = jnp.broadcast_to(land_ref[pl.ds(slot, 1), 8:][0], (8, 128)).astype(F32)
        scale = jnp.exp2(power - 15.0) * (32768.0 / 32766.0)
        at = pl.multiple_of(slot * chunk, 128)
        result_ref[:, pl.ds(at, 128)] = (word >> 16).astype(F32) * scale
        result_ref[:, pl.ds(at + 128, 128)] = ((word & 65535) - 32768).astype(F32) * scale

    own.wait()
    unpack(me)

    def receive(k, carry):
        slot = lax.rem(me + count - k, count)
        grad_copy(slot, slot).wait_recv()
        unpack(slot)
        return carry

    lax.fori_loop(1, count, receive, 0)
    each(count, me, lambda o: grad_copy(o, o).wait_send())


def fast_device(lensing_maps, filter_taps, survey_mask, bin_pairs, target_corr, pair_weight):
    scales, tap_count = filter_taps.shape
    half = (tap_count - 1) // 2
    strip = lensing_maps[0]
    strip_rows, cols = strip.shape
    bins, sky = lax.axis_size("bin"), lax.axis_size("sky")
    count = bins * sky
    pairs, lags = pair_weight.shape[0], pair_weight.shape[2]
    chunk = cols // count
    width = chunk + 128
    size = bins * XB
    groups = size // 32
    vregs = 2
    spec = pl.BlockSpec(memory_space=pltpu.VMEM)
    dma = pltpu.SemaphoreType.DMA
    table = (vregs, bins, 128)
    result, corr = pl.pallas_call(
        functools.partial(fast_kernel, bins, sky, scales, lags, chunk, half, 1.0 / (strip_rows * sky * cols)),
        out_shape=(
            pltpu.VMEM((strip_rows, cols), F32),
            pltpu.VMEM((scales, lags, pairs), F32),
        ),
        in_specs=[pl.BlockSpec(memory_space=pl.ANY)] * 6,
        out_specs=(spec, spec),
        scratch_shapes=[
            pltpu.VMEM((strip_rows, cols), BF16),
            pltpu.VMEM(filter_taps.shape, F32),
            pltpu.VMEM(survey_mask.shape, jnp.int32),
            pltpu.VMEM((2, pairs), jnp.int32),
            pltpu.VMEM((scales, lags, pairs), F32),
            pltpu.VMEM((scales, lags, pairs), F32),
            pltpu.VMEM((strip_rows, cols + 128), BF16),
            pltpu.VMEM((count, strip_rows, width), BF16),
            pltpu.VMEM((size, width), BF16),
            pltpu.VMEM((8, 128), F32),
            pltpu.VMEM((sky, 8, 128), F32),
            pltpu.VMEM((sky, 8, width), F32),
            pltpu.VMEM((sky, 8, width), F32),
            pltpu.VMEM((scales, size, size), BF16),
            pltpu.VMEM((scales, size, size), BF16),
            pltpu.VMEM((size, scales * size), BF16),
            pltpu.VMEM((size, scales * size), BF16),
            pltpu.VMEM((scales, 256, 256), BF16),
            pltpu.VMEM((scales, 256, 256), BF16),
            pltpu.VMEM((8, 128), F32),
            pltpu.VMEM((2, scales, 8, 128), F32),
            pltpu.VMEM((8, 128), jnp.int32),
            pltpu.VMEM((2,) + table, F32),
            pltpu.VMEM((scales, size, width), BF16),
            pltpu.VMEM((scales, groups, 32 * (2 * lags - 1), width), BF16),
            pltpu.VMEM((scales, 64, 256), BF16),
            pltpu.VMEM((size, width), F32),
            pltpu.VMEM((scales, size, chunk), BF16),
            pltpu.VMEM((scales, size, chunk), BF16),
            pltpu.VMEM((count, strip_rows + 1, 128), jnp.int32),
            pltpu.VMEM((count, strip_rows + 1, 128), jnp.int32),
            pltpu.VMEM(table, F32),
            pltpu.VMEM(table, F32),
            pltpu.VMEM(table, F32),
            pltpu.VMEM((vregs, count // 2, bins, 128), F32),
            dma((count,)), dma((count,)), dma((sky,)), dma((sky,)), dma((vregs,)), dma((vregs,)),
            dma((vregs, count // 2)), dma((vregs, count // 2)),
            dma((count,)), dma((count,)), dma((2,)), dma((6,)),
        ],
        compiler_params=pltpu.CompilerParams(
            collective_id=1, has_side_effects=True, vmem_limit_bytes=VMEM_LIMIT
        ),
    )(
        strip,
        filter_taps,
        survey_mask,
        bin_pairs.T,
        jnp.transpose(target_corr, (1, 2, 0)),
        jnp.transpose(pair_weight, (1, 2, 0)),
    )
    return (jnp.transpose(corr, (2, 0, 1)), result[None])


def fits(mesh, maps, taps, survey_mask, weight):
    bins, sky = mesh.shape["bin"], mesh.shape["sky"]
    rows, cols = maps.shape[1:]
    return (
        maps.shape[0] == bins == 8
        and rows == XB == 8 * sky
        and cols == 256 * bins * sky
        and survey_mask.shape == (sky, cols // 128)
        and EARLY < taps.shape[0] <= 2 * EARLY
        and taps.shape[1] == 17
        and weight.shape[0] <= 128
        and weight.shape[2] == 4
    )


def solution(mesh):
    placed = (P("bin", "sky", None), P(), P("sky", None), P(), P(), P())

    def step(lensing_maps, filter_taps, survey_mask, bin_pairs, target_corr, pair_weight):
        fast = fits(mesh, lensing_maps, filter_taps, survey_mask, pair_weight)
        return jax.shard_map(
            fast_device if fast else per_device,
            mesh=mesh,
            in_specs=placed,
            out_specs=(P(), P("bin", "sky", None)),
            check_vma=False,
        )(lensing_maps, filter_taps, survey_mask, bin_pairs, target_corr, pair_weight)

    return step
```

```python
import functools

import jax
import jax.numpy as jnp
from jax import lax
from jax.experimental import pallas as pl
from jax.experimental.pallas import tpu as pltpu
from jax.sharding import PartitionSpec as P

F32 = jnp.float32
BF16 = jnp.bfloat16
XB = 32
MESH = pl.DeviceIdType.MESH
VMEM_LIMIT = 60 * 1024 * 1024


def round_up(n, m):
    return -(-n // m) * m


def halves(value):
    hi = value.astype(BF16)
    lo = (value - hi.astype(F32)).astype(BF16)
    return hi, lo


def mm(a, b):
    return jnp.dot(a, b, preferred_element_type=F32)


def mm3(a, b):
    return mm(a[0], b[0]) + mm(a[0], b[1]) + mm(a[1], b[0])


def place(bins, sky):
    return lax.axis_index("bin") * sky + lax.axis_index("sky")


def greet(me, bins, sky):
    count = bins * sky
    barrier = pltpu.get_barrier_semaphore()

    def hello(k, carry):
        other = lax.rem(me + k, count)
        pl.semaphore_signal(
            barrier, inc=1, device_id=(other // sky, lax.rem(other, sky)), device_id_type=MESH
        )
        return carry

    lax.fori_loop(1, count, hello, 0)
    pl.semaphore_wait(barrier, count - 1)


def band(row, height, width, shift, out_width):
    full = pltpu.roll(
        jnp.broadcast_to(row, (height, width)), width - shift, 1, stride=1, stride_axis=0
    )
    return full[:, :out_width]


def same_row(count):
    left = lax.rem(lax.broadcasted_iota(jnp.int32, (count, count), 0), XB)
    right = lax.rem(lax.broadcasted_iota(jnp.int32, (count, count), 1), XB)
    return (left == right).astype(F32)


def step_kernel(
    bins, sky, scales, lags, groups, chunk, halo, tiles, half, area, src_of, dst_of,
    x_ref, mark_ref, tap_ref, pair_ref, fit_ref,
    result_ref, corr_ref,
    y_ref, marks_ref, hi_ref, lo_ref, g_ref, sums_ref, grad_ref,
    col_ref, adj_ref, part_ref, sky_ref, bin_in_ref, bin_ref,
    send_x, recv_x, send_m, recv_m, send_s, recv_s, send_b, recv_b, send_g, recv_g, own_sem, coef_ref,
):
    count = bins * sky
    strip_rows, width = y_ref.shape[1], y_ref.shape[2]
    pieces, part_width = grad_ref.shape[0], grad_ref.shape[3]
    span = adj_ref.shape[2]
    size = bins * XB
    rows = groups * XB
    my_bin, my_sky = lax.axis_index("bin"), lax.axis_index("sky")
    me = place(bins, sky)
    greet(me, bins, sky)

    def window_copy(other, slot):
        return pltpu.make_async_remote_copy(
            src_ref=src_of(x_ref, other),
            dst_ref=y_ref.at[slot],
            send_sem=send_x.at[other],
            recv_sem=recv_x.at[slot],
            device_id=(other // sky, lax.rem(other, sky)),
            device_id_type=MESH,
        )

    def along(axis, src, dst, send, recv, other, slot):
        return pltpu.make_async_remote_copy(
            src_ref=src,
            dst_ref=dst.at[slot],
            send_sem=send.at[other],
            recv_sem=recv.at[slot],
            device_id=(my_bin, other) if axis == "sky" else (other, my_sky),
            device_id_type=MESH,
        )

    def each(n, mine, act):
        def body(k, carry):
            act(lax.rem(mine + k, n))
            return carry

        lax.fori_loop(1, n, body, 0)

    each(sky, my_sky, lambda o: along("sky", mark_ref, marks_ref, send_m, recv_m, o, my_sky).start())
    each(count, me, lambda o: window_copy(o, me).start())
    own_mark = pltpu.make_async_copy(mark_ref, marks_ref.at[my_sky], own_sem.at[0])
    own_mark.start()
    own = pltpu.make_async_copy(src_of(x_ref, me), y_ref.at[me], own_sem.at[1])
    own.start()

    tall = tap_ref.shape[3]
    row_hi, row_lo, back_hi, back_lo = [], [], [], []
    narrow = round_up(rows + 2 * half + 1, 128)
    for s in range(scales):
        taps, turned = tap_ref[0, s], tap_ref[1, s]
        for at, part in enumerate(halves(band(turned[:, :width], width, width, half, width))):
            col_ref[at, s] = part
        for at, part in enumerate(
            halves(band(taps[:, :span], span, span, half + halo, part_width))
        ):
            adj_ref[at, s] = part
        a, b = halves(band(taps[:, :narrow], rows, narrow, half, rows))
        row_hi.append(a)
        row_lo.append(b)
        back = band(turned[:, :narrow], rows, narrow, half, rows)
        back_hi.append(back)
    row_hi = jnp.concatenate(row_hi, axis=0)
    row_lo = jnp.concatenate(row_lo, axis=0)
    back = halves(jnp.concatenate(back_hi, axis=1))
    diag = same_row(size)
    lanes = lax.broadcasted_iota(jnp.int32, (size, width), 1)
    owned = (lanes >= halo) & (lanes < halo + chunk)
    spot = lax.rem(lax.broadcasted_iota(jnp.int32, (bins, size), 1), XB)
    bin_row = lax.broadcasted_iota(jnp.int32, (bins, size), 0)

    pairs = fit_ref.shape[1]
    first = jnp.broadcast_to(pair_ref[:, 0:1], (pairs, size))
    second = jnp.broadcast_to(pair_ref[:, 1:2], (pairs, size))
    right_hot = lax.broadcasted_iota(jnp.int32, (pairs, size), 1) // XB == second
    weight = jnp.zeros((bins, size), F32)
    target = jnp.zeros((bins, size), F32)
    for i in range(bins):
        hot = right_hot & (first == i)
        weight_row = jnp.sum(jnp.where(hot, fit_ref[0], 0.0), axis=0, keepdims=True)
        target_row = jnp.sum(jnp.where(hot, fit_ref[1], 0.0), axis=0, keepdims=True)
        weight = jnp.where(bin_row == i, weight_row, weight)
        target = jnp.where(bin_row == i, target_row, target)
    sums_ref[...] = jnp.zeros_like(sums_ref)

    each(sky, my_sky, lambda o: along("sky", mark_ref, marks_ref, send_m, recv_m, o, o).wait())
    own_mark.wait()
    each(count, me, lambda o: window_copy(o, o).wait())
    own.wait()

    mark_width = mark_ref.shape[1]
    start = me * chunk - halo + 128
    marks = marks_ref[...].reshape(rows, mark_width)
    marks = pltpu.roll(marks, lax.rem(mark_width - start // 128, mark_width), 1)
    which = (lax.broadcasted_iota(jnp.int32, (rows, width), 1) + start) // 128 - start // 128
    mask = jnp.zeros((rows, width), F32)
    for t in range(tiles):
        mask = jnp.where(which == t, jnp.broadcast_to(marks[:, t : t + 1], (rows, width)), mask)
    masks = [
        jnp.concatenate([mask[g * XB : (g + 1) * XB]] * bins, axis=0) > 0 for g in range(groups)
    ]

    for b in range(bins):
        y = jnp.concatenate([y_ref[b * sky + k].astype(F32) for k in range(sky)], axis=0)
        y = y.astype(BF16)
        hi, lo = halves(mm(row_hi, y) + mm(row_lo, y))
        for s in range(scales):
            for g in range(groups):
                part = slice(s * rows + g * XB, s * rows + (g + 1) * XB)
                hi_ref[g, s, b * XB : (b + 1) * XB, :] = hi[part]
                lo_ref[g, s, b * XB : (b + 1) * XB, :] = lo[part]

    for g in range(groups):

        def forward(s, carry):
            matrix = (col_ref[0, s], col_ref[1, s])
            filtered = mm3((hi_ref[g, s], lo_ref[g, s]), matrix).astype(BF16).astype(F32)
            kept = jnp.where(masks[g], filtered, 0.0)
            g_ref[g, s] = kept.astype(BF16)
            left = jnp.where(owned, kept, 0.0).astype(BF16)
            for l in range(lags):
                right = kept if l == 0 else pltpu.roll(kept, width - l, 1)
                gram = lax.dot_general(
                    left, right.astype(BF16), (((1,), (1,)), ((), ())), preferred_element_type=F32
                )
                gram = jnp.sum((gram * diag).reshape(bins, XB, size), axis=1)
                sums_ref[s * lags + l] = sums_ref[s * lags + l] + gram
            return carry

        lax.fori_loop(0, scales, forward, 0)

    table = jnp.zeros((bins, size), F32)
    for at in range(scales * lags):
        value = sums_ref[at]
        for step in (16, 8, 4, 2, 1):
            value = value + pltpu.roll(value, size - step, 1)
        if at:
            value = pltpu.roll(value, at, 1)
        table = jnp.where(spot == at, value, table)

    part_ref[...] = table
    each(sky, my_sky, lambda o: along("sky", part_ref, sky_ref, send_s, recv_s, o, my_sky).start())
    sky_ref[pl.ds(my_sky, 1)] = table[None]
    each(sky, my_sky, lambda o: along("sky", part_ref, sky_ref, send_s, recv_s, o, o).wait())
    table = sky_ref[0]
    for k in range(1, sky):
        table = table + sky_ref[k]
    bin_in_ref[...] = table
    each(bins, my_bin, lambda o: along("bin", bin_in_ref, bin_ref, send_b, recv_b, o, my_bin).start())
    bin_ref[pl.ds(my_bin, 1)] = table[None]
    each(bins, my_bin, lambda o: along("bin", bin_in_ref, bin_ref, send_b, recv_b, o, o).wait())
    table = bin_ref[0]
    for k in range(1, bins):
        table = table + bin_ref[k]
    table = table * area

    picked = jnp.zeros((pairs, size), F32)
    for i in range(bins):
        picked = jnp.where(first == i, jnp.broadcast_to(table[i : i + 1], (pairs, size)), picked)
    picked = jnp.where(right_hot, picked, 0.0)
    step = size // 2
    while step >= XB:
        picked = picked + pltpu.roll(picked, step, 1)
        step //= 2
    corr_ref[...] = picked

    ahead = jnp.where(spot < scales * lags, weight * (table - target), 0.0)
    spread = jnp.broadcast_to(ahead[:, None, :], (bins, XB, size)).reshape(size, size)
    behind = jnp.sum(jnp.transpose(spread * diag).reshape(bins, XB, size), axis=1)

    def coefficient(values, at):
        value = jnp.where(spot == at, values, 0.0)
        value = pltpu.roll(value, lax.rem(size - at, size), 1)
        for step in (1, 2, 4, 8, 16):
            value = value + pltpu.roll(value, step, 1)
        return value

    def grad_copy(piece, other, slot):
        return pltpu.make_async_remote_copy(
            src_ref=grad_ref.at[piece, other],
            dst_ref=dst_of(result_ref, slot, piece),
            send_sem=send_g.at[piece, other],
            recv_sem=recv_g.at[piece, slot],
            device_id=(other // sky, lax.rem(other, sky)),
            device_id_type=MESH,
        )

    own_grads = []
    for piece in range(pieces):
        cut = slice(piece * part_width, piece * part_width + span)
        for g in range(groups):

            def backward(s, carry):
                maps = g_ref[g, s, :, cut].astype(F32)
                total_grad = jnp.zeros((size, span), F32)
                for shift in range(1 - lags, lags):
                    moved = maps if shift == 0 else pltpu.roll(maps, (span - shift) % span, 1)
                    moved = moved.astype(BF16)
                    at = s * (2 * lags - 1) + shift + lags - 1
                    if piece == 0:
                        if shift == 0:
                            coef = coefficient(ahead + behind, s * lags)
                        elif shift > 0:
                            coef = coefficient(ahead, s * lags + shift)
                        else:
                            coef = coefficient(behind, s * lags - shift)
                        if pieces > 1 or groups > 1:
                            coef_ref[at] = coef
                    else:
                        coef = coef_ref[at]
                    full = jnp.broadcast_to(coef[:, None, :], (bins, XB, size))
                    hi, lo = halves(full.reshape(size, size) * diag)
                    total_grad = total_grad + mm(hi, moved) + mm(lo, moved)
                total_grad = jnp.where(masks[g][:, cut], total_grad, 0.0)
                hi, lo = halves(mm3(halves(total_grad), (adj_ref[0, s], adj_ref[1, s])))
                hi_ref[g, s, :, :part_width] = hi
                lo_ref[g, s, :, :part_width] = lo
                return carry

            lax.fori_loop(0, scales, backward, 0)

        for b in range(bins):
            spots = [(g, s) for s in range(scales) for g in range(groups)]
            rows_of = slice(b * XB, (b + 1) * XB)
            hi = jnp.concatenate([hi_ref[g, s, rows_of, :part_width] for g, s in spots], axis=0)
            lo = jnp.concatenate([lo_ref[g, s, rows_of, :part_width] for g, s in spots], axis=0)
            total_rows = mm3(back, (hi, lo))
            for k in range(sky):
                at = b * sky + k
                grad_ref[piece, at] = total_rows[k * strip_rows : (k + 1) * strip_rows]

        each(count, me, lambda o: grad_copy(piece, o, me).start())
        own_grad = pltpu.make_async_copy(
            grad_ref.at[piece, me], dst_of(result_ref, me, piece), own_sem.at[2 + piece]
        )
        own_grad.start()
        own_grads.append(own_grad)
    for piece in range(pieces):
        each(count, me, lambda o: grad_copy(piece, o, o).wait())
        own_grads[piece].wait()


def per_device(lensing_maps, filter_taps, survey_mask, bin_pairs, target_corr, pair_weight):
    scales, tap_count = filter_taps.shape
    half = (tap_count - 1) // 2
    strip = lensing_maps[0]
    strip_rows, cols = strip.shape
    bins, sky = lax.axis_size("bin"), lax.axis_size("sky")
    count = bins * sky
    pairs, lags = pair_weight.shape[0], pair_weight.shape[2]
    row_count = strip_rows * sky
    groups = row_count // XB
    chunk = cols // count
    width = round_up(chunk + 2 * (2 * half + lags - 1), 128)
    halo = (width - chunk) // 2
    out_width = round_up(chunk, 128)
    tiles = width // 128 + 1
    size = bins * XB
    aligned = chunk % 128 == 0
    pieces = out_width // 128
    part_width = out_width // pieces
    span = width - (pieces - 1) * part_width

    windows = jnp.pad(strip, ((0, 0), (halo, halo)))
    if not aligned:
        windows = jnp.stack([windows[:, d * chunk : d * chunk + width] for d in range(count)])
    mark_width = round_up(survey_mask.shape[1] + 1 + tiles, 128)
    marks = jnp.pad(
        survey_mask.astype(F32), ((0, 0), (1, mark_width - survey_mask.shape[1] - 1))
    )
    marks = jnp.broadcast_to(marks, (strip_rows, mark_width))
    tall = max(width, round_up(row_count + 2 * half + 1, 128))
    taps = jnp.stack([filter_taps, filter_taps[:, ::-1]])
    taps = jnp.pad(taps, ((0, 0), (0, 0), (0, tall - tap_count)))[:, :, None, :]
    fit = jnp.stack([pair_weight, target_corr]).reshape(2, pairs, scales * lags)
    fit = jnp.tile(jnp.pad(fit, ((0, 0), (0, 0), (0, XB - scales * lags))), (1, 1, bins))

    if aligned:
        src_of = lambda ref, d: ref.at[:, pl.ds(pl.multiple_of(d * chunk, 128), width)]
        dst_of = lambda ref, d, p: ref.at[
            :, pl.ds(pl.multiple_of(d * chunk + p * part_width, 128), part_width)
        ]
        result_shape = (strip_rows, cols)
    else:
        src_of = lambda ref, d: ref.at[d]
        dst_of = lambda ref, d, p: ref.at[d]
        result_shape = (count, strip_rows, out_width)

    spec = pl.BlockSpec(memory_space=pltpu.VMEM)
    table_shape = (bins, size)
    dma = pltpu.SemaphoreType.DMA
    result, corr = pl.pallas_call(
        functools.partial(
            step_kernel, bins, sky, scales, lags, groups, chunk, halo, tiles, half,
            1.0 / (row_count * cols), src_of, dst_of,
        ),
        out_shape=(
            jax.ShapeDtypeStruct(result_shape, F32),
            jax.ShapeDtypeStruct((pairs, size), F32),
        ),
        in_specs=[spec] * 5,
        out_specs=(spec, spec),
        scratch_shapes=[
            pltpu.VMEM((count, strip_rows, width), BF16),
            pltpu.VMEM((sky, strip_rows, mark_width), F32),
            pltpu.VMEM((groups, scales, size, width), BF16),
            pltpu.VMEM((groups, scales, size, width), BF16),
            pltpu.VMEM((groups, scales, size, width), BF16),
            pltpu.VMEM((scales * lags,) + table_shape, F32),
            pltpu.VMEM((pieces, count, strip_rows, part_width), F32),
            pltpu.VMEM((2, scales, width, width), BF16),
            pltpu.VMEM((2, scales, span, part_width), BF16),
            pltpu.VMEM(table_shape, F32),
            pltpu.VMEM((sky,) + table_shape, F32),
            pltpu.VMEM(table_shape, F32),
            pltpu.VMEM((bins,) + table_shape, F32),
            dma((count,)), dma((count,)), dma((sky,)), dma((sky,)), dma((sky,)), dma((sky,)),
            dma((bins,)), dma((bins,)), dma((pieces, count)), dma((pieces, count)), dma((2 + pieces,)),
            pltpu.VMEM((scales * (2 * lags - 1),) + table_shape, F32),
        ],
        compiler_params=pltpu.CompilerParams(
            collective_id=1, has_side_effects=True, vmem_limit_bytes=VMEM_LIMIT
        ),
    )(windows, marks, taps, bin_pairs, fit)
    if not aligned:
        result = jnp.transpose(result[:, :, :chunk], (1, 0, 2)).reshape(strip_rows, cols)
    corr_table = corr[:, : scales * lags].reshape(pairs, scales, lags)
    return (corr_table, result[None])


def tables(bins, scales, lags):
    lane = lax.broadcasted_iota(jnp.int32, (bins, 128), 1)
    high, low = lane // 64, (lane // 8) % 2
    return lane, high, low, 2 * high + low


EARLY = 3


def spot_of(scale):
    return (0, scale) if scale < EARLY else (1, scale - EARLY)


def slot_rows(scale, lag):
    slot = spot_of(scale)[1]
    return 64 * (slot // 2) + 16 * lag + 8 * (slot % 2)


def thirds(value):
    hi = value.astype(BF16)
    rest = value - hi.astype(F32)
    mid = rest.astype(BF16)
    lo = (rest - mid.astype(F32)).astype(BF16)
    return hi, mid, lo


def nt(a, b):
    return lax.dot_general(a, b, (((1,), (1,)), ((), ())), preferred_element_type=F32)


def steps(begin, end, body, carry):
    for s in range(begin, end):
        carry = body(s, carry)
    return carry


def fast_kernel(
    bins, sky, scales, lags, chunk, half, area,
    x_hbm, tap_hbm, mask_hbm, pair_hbm, target_hbm, weight_hbm,
    result_ref, corr_ref,
    x_ref, tap_ref, mask_ref, pair_ref, target_ref, weight_ref,
    pad_ref, wide_ref, y_ref, maps_ref, mark_ref, marks_ref, mask_v_ref, mask_w_ref,
    row_hi_ref, row_lo_ref, back_hi_ref, back_lo_ref, fwd_ref, adj_ref,
    small_ref, fit_ref, pairs_ref, table_ref,
    g_ref, moved_ref, coef_ref, t_ref, cg_hi_ref, cg_lo_ref, out_ref, grad_ref, land_ref,
    part_ref, twin_ref, chip_ref, parts_ref,
    send_x, recv_x, send_y, recv_y, send_m, recv_m, send_c, recv_c, send_t, recv_t, send_g, recv_g, own_sem, in_sem,
):
    count = bins * sky
    cols = x_ref.shape[1]
    width = y_ref.shape[2]
    halo = (width - chunk) // 2
    pairs = pair_ref.shape[1]
    taps_n = tap_ref.shape[1]
    size = bins * XB
    groups = size // 32
    vregs = part_ref.shape[0]
    my_bin, my_sky = lax.axis_index("bin"), lax.axis_index("sky")
    me = place(bins, sky)

    barrier = pltpu.get_barrier_semaphore()

    bits = count.bit_length() - 1
    flips = [(1 - 2 * lax.rem(me // 2**i, 2)) * 2**i for i in range(bits)]

    def across(act):
        def body(k, carry):
            mask = count - 2 - 2 * k
            other = me
            for i in range(1, bits):
                other = other + lax.rem(mask // 2**i, 2) * flips[i]
            act(other)
            return carry

        lax.fori_loop(0, count // 2 - 1, body, 0)

    def each(n, mine, act):
        def body(k, carry):
            act(lax.rem(mine + k, n))
            return carry

        lax.fori_loop(1, n, body, 0)

    def hello(other):
        pl.semaphore_signal(
            barrier, inc=1, device_id=(other // sky, lax.rem(other, sky)), device_id_type=MESH
        )

    hello(me + flips[0])
    across(hello)
    loads = [
        pltpu.make_async_copy(src, dst, in_sem.at[i])
        for i, (src, dst) in enumerate(
            (
                (x_hbm, x_ref), (mask_hbm, mask_ref), (tap_hbm, tap_ref),
                (pair_hbm, pair_ref), (target_hbm, target_ref), (weight_hbm, weight_ref),
            )
        )
    ]
    for load in loads:
        load.start()

    chip, core = me // 2, lax.rem(me, 2)
    twin = me + flips[0]
    wide = 2 * chunk + 2 * halo

    def remote(src, dst, send, recv, other):
        return pltpu.make_async_remote_copy(
            src_ref=src,
            dst_ref=dst,
            send_sem=send,
            recv_sem=recv,
            device_id=(other // sky, lax.rem(other, sky)),
            device_id_type=MESH,
        )

    def window_copy(other, slot):
        to, at = other // 2, slot // 2
        src = pad_ref.at[:, pl.ds(pl.multiple_of(to * 2 * chunk, 128), wide)]
        return remote(src, wide_ref.at[at], send_x.at[to], recv_x.at[at], other)

    def twin_copy(at):
        src = wide_ref.at[at, :, pl.ds(pl.multiple_of((1 - core) * chunk, 128), width)]
        return remote(src, y_ref.at[at], send_y.at[at], recv_y.at[at], twin)

    beside = me + flips[1]

    def mark_copy(n, slot, to):
        src = mark_ref if n < 2 else marks_ref.at[slot]
        return remote(src, marks_ref.at[slot], send_m.at[n], recv_m.at[n], to)

    loads[0].wait()
    loads[1].wait()
    moved_x = pltpu.roll(x_ref[...].astype(F32), halo, 1)
    edge = lax.broadcasted_iota(jnp.int32, (moved_x.shape[0], 128), 1) < halo
    pad_ref[:, :128] = jnp.where(edge, 0.0, moved_x[:, :128]).astype(BF16)
    pad_ref[:, 128:cols] = moved_x[:, 128:].astype(BF16)
    pad_ref[:, cols:] = jnp.where(edge, moved_x[:, :128], 0.0).astype(BF16)
    mark_ref[...] = jnp.zeros_like(mark_ref)
    mark_ref[:, : mask_ref.shape[1]] = jnp.broadcast_to(
        mask_ref[...].astype(F32), (mark_ref.shape[0], mask_ref.shape[1])
    )

    pl.semaphore_wait(barrier, count // 2)
    across(lambda o: window_copy(o, me).start())
    mark_copy(0, my_sky, twin).start()
    mark_copy(1, my_sky, beside).start()
    at = pl.multiple_of(chip * 2 * chunk, 128)
    wide_ref[pl.ds(chip, 1)] = pad_ref[:, pl.ds(at, wide)][None]
    twin_copy(chip).start()
    marks_ref[pl.ds(my_sky, 1)] = mark_ref[...][None]

    for load in loads[2:]:
        load.wait()
    small_ref[...] = jnp.zeros_like(small_ref)
    small_ref[:scales, :taps_n] = tap_ref[...]
    tap_hi, tap_lo = halves(small_ref[...])
    tap_row = lax.broadcasted_iota(jnp.int32, (128, 256), 0)
    tap_col = lax.broadcasted_iota(jnp.int32, (128, 256), 1)
    real = tap_row < taps_n

    def spread(hot):
        hot = (hot & real).astype(F32).astype(BF16)
        return mm(tap_hi, hot) + mm(tap_lo, hot)

    straight = spread(tap_col == tap_row)
    turned = spread(tap_col == taps_n - 1 - tap_row)
    spaced = spread(tap_col == bins * (taps_n - 1 - tap_row))
    sub = lax.broadcasted_iota(jnp.int32, (bins, size), 0)
    col = lax.broadcasted_iota(jnp.int32, (bins, size), 1)
    turns = [pltpu.roll(straight, (XB * b - half) % size, 1) for b in range(bins)]
    for s in range(scales):
        reach = halo + half
        for ref, taps in ((fwd_ref, turned), (adj_ref, straight)):
            hi, lo = halves(band(taps[s : s + 1], 256, 256, reach, 128))
            ref[s, :, :128] = hi
            ref[s, :, 128:] = lo
        first = jnp.zeros((bins, size), F32)
        for b in range(bins):
            first = jnp.where(sub == b, jnp.broadcast_to(turns[b][s : s + 1], (bins, size)), first)
        tiles = [
            jnp.where(col // XB == sub, first if x == 0 else pltpu.roll(first, x, 1), 0.0)
            for x in range(XB)
        ]
        hi, lo = halves(jnp.concatenate(tiles, axis=0))
        row_hi_ref[s] = hi
        row_lo_ref[s] = lo
        first = pltpu.roll(
            jnp.broadcast_to(spaced[s : s + 1], (8, size)), 0, 1, stride=bins, stride_axis=0
        )
        tiles = []
        for b in range(bins):
            for k in range(XB // 8):
                shift = (bins * 8 * k - bins * half + b) % size
                apart = col // bins - sub - 8 * k
                near = (apart <= half) & (apart >= -half)
                tiles.append(jnp.where(near, first if shift == 0 else pltpu.roll(first, shift, 1), 0.0))
        hi, lo = halves(jnp.concatenate(tiles, axis=0))
        back_hi_ref[:, s * size : (s + 1) * size] = hi
        back_lo_ref[:, s * size : (s + 1) * size] = lo

    lane, high, low, slot = tables(bins, scales, lags)
    pairs_ref[...] = jnp.full_like(pairs_ref, -1)
    pairs_ref[:2, :pairs] = pair_ref[...]
    fit_ref[...] = jnp.zeros_like(fit_ref)
    for s in range(scales):
        fit_ref[0, s, :lags, :pairs] = weight_ref[s]
        fit_ref[1, s, :lags, :pairs] = target_ref[s]
    bin_of = lax.broadcasted_iota(jnp.int32, (bins, 128), 0)
    first_hot = (pairs_ref[0:1, :] == bin_of).astype(F32)
    second_hot = pairs_ref[1:2, :] == bin_of
    first_hot16 = first_hot.astype(BF16)
    for at in range(2):
        for v in range(vregs):
            tiles = []
            for tile in range(16):
                at_slot, l = 2 * (tile // 8) + tile % 2, (tile // 2) % 4
                s = at_slot + v * EARLY
                if s < scales and spot_of(s) == (v, at_slot):
                    row = jnp.broadcast_to(fit_ref[at, s, l : l + 1, :], (bins, 128))
                    tiles.append(jnp.where(second_hot, row, 0.0))
                else:
                    tiles.append(jnp.zeros((bins, 128), F32))
            parts = thirds(jnp.concatenate(tiles, axis=0))
            table_ref[at, v] = nt(first_hot16, parts[0]) + nt(first_hot16, parts[1]) + nt(first_hot16, parts[2])

    far = lax.rem(beside, sky)
    mark_copy(1, far, beside).wait()
    mark_copy(2, far, twin).start()
    mark_copy(0, lax.rem(twin, sky), twin).wait()
    mark_copy(2, lax.rem(beside + flips[0], sky), twin).wait()
    for k in range(sky):
        marks = pltpu.roll(marks_ref[k], 1, 1)
        marks = pltpu.roll(marks, lax.rem(128 - 2 * me, 128), 1)
        left, one, two, right = [jnp.broadcast_to(marks[:, t : t + 1], (8, 128)) for t in range(4)]
        lanes = lax.broadcasted_iota(jnp.int32, (8, 128), 1)
        mask_v_ref[k, :, :128] = one
        mask_v_ref[k, :, 128:256] = two
        mask_v_ref[k, :, 256:] = jnp.where(lanes < 64, right, left)
        mask_w_ref[k, :, :128] = jnp.where(lanes < 64, left, one)
        mask_w_ref[k, :, 128:256] = jnp.where(lanes < 64, one, two)
        mask_w_ref[k, :, 256:] = jnp.where(lanes < 64, two, right)

    def masked(value, ref):
        tall = size // sky
        return jnp.concatenate(
            [value[k * tall : (k + 1) * tall] * jnp.broadcast_to(ref[k, 0:1, :], (tall, width)) for k in range(sky)],
            axis=0,
        )

    def pass_on(k, carry):
        mask = 2 * k
        other = me
        for i in range(1, bits):
            other = other + lax.rem(mask // 2**i, 2) * flips[i]
        window_copy(other, other).wait()
        twin_copy(other // 2).start()
        return carry

    lax.fori_loop(1, count // 2, pass_on, 0)
    lax.fori_loop(0, count // 2, lambda k, carry: (twin_copy(k).wait(), carry)[1], 0)
    mine = pl.multiple_of(core * chunk, 128)
    for b in range(bins):
        rows = []
        for k in range(sky):
            direct = wide_ref[(b * sky + k) // 2, :, pl.ds(mine, width)].astype(F32)
            passed = y_ref[(b * sky + k) // 2].astype(F32)
            rows.append(jnp.where(core == k % 2, direct, passed))
        maps_ref[b * XB : (b + 1) * XB, :] = jnp.concatenate(rows, axis=0).astype(BF16)

    def stacked(v):
        return jnp.concatenate(
            [v[:, :256], v[:, 128:], jnp.concatenate([v[:, 256:], v[:, :128]], axis=1)], axis=0
        )

    def forward(s, carry):
        y = maps_ref[...]
        hi, lo = halves(mm(row_hi_ref[s], y) + mm(row_lo_ref[s], y))
        p = mm(stacked(hi), fwd_ref[s])
        q = mm(stacked(lo), fwd_ref[s, :, :128])
        f = p[:, :128] + p[:, 128:] + q
        f = jnp.concatenate([f[:size], f[size : 2 * size], f[2 * size :]], axis=1)
        kept16 = masked(f, mask_v_ref).astype(BF16)
        g_ref[s] = kept16
        shifted = [kept16[:, l : l + chunk] for l in range(lags)]
        total = jnp.zeros((32, 128), F32)
        for g in range(groups):
            right = jnp.concatenate(
                [shifted[l][g * 32 + 16 * h : g * 32 + 16 * h + 16] for h in range(2) for l in range(lags)],
                axis=0,
            )
            total = total + nt(kept16[g * 32 : (g + 1) * 32, :chunk], right)
        z = jnp.zeros((bins, 128), F32)
        for x in range(4):
            z = jnp.where(slot == x, total[bins * x : bins * (x + 1)], z)
        z = z + pltpu.roll(z, 64, 1)
        z = z + jnp.where(low == 0, pltpu.roll(z, 120, 1), pltpu.roll(z, 8, 1))
        into = s % EARLY
        return jnp.where(slot == into, z, carry)

    def core_copy(v):
        return pltpu.make_async_remote_copy(
            src_ref=part_ref.at[v],
            dst_ref=twin_ref.at[v],
            send_sem=send_c.at[v],
            recv_sem=recv_c.at[v],
            device_id=((me + flips[0]) // sky, lax.rem(me + flips[0], sky)),
            device_id_type=MESH,
        )

    def table_copy(v, other, to):
        return pltpu.make_async_remote_copy(
            src_ref=chip_ref.at[v],
            dst_ref=parts_ref.at[v, to // 2],
            send_sem=send_t.at[v, other // 2],
            recv_sem=recv_t.at[v, to // 2],
            device_id=(other // sky, lax.rem(other, sky)),
            device_id_type=MESH,
        )

    def send_tables(v):
        core_copy(v).wait()
        chip = part_ref[v] + twin_ref[v]
        chip_ref[v] = chip
        across(lambda o: table_copy(v, o, me).start())
        parts_ref[v, pl.ds(me // 2, 1)] = chip[None]

    zero = jnp.zeros((bins, 128), F32)
    part_ref[0] = steps(0, EARLY, forward, zero)
    core_copy(0).start()
    late = steps(EARLY, EARLY + 1, forward, zero)
    send_tables(0)
    part_ref[1] = steps(EARLY + 1, scales, forward, late)
    core_copy(1).start()

    def lagging(s, carry):
        kept = g_ref[s]
        for at in range(2 * lags - 1):
            cut = width - halo + (at - lags + 1)
            turn = jnp.concatenate([kept[:, cut:], kept[:, :cut]], axis=1)
            for g in range(groups):
                side = (g % 2) * width
                moved_ref[s, g // 2, at * 32 : (at + 1) * 32, side : side + width] = turn[g * 32 : (g + 1) * 32]
        return carry

    steps(0, 1, lagging, 0)
    send_tables(1)
    steps(1, scales, lagging, 0)

    e_row = lax.broadcasted_iota(jnp.int32, (128, 256), 0)
    e_col = lax.broadcasted_iota(jnp.int32, (128, 256), 1)
    place_hot = (e_row % 16 < 8) & (e_row // 16 == e_col // 32 - (lags - 1)) & (e_row % 8 == e_col % 8)
    place_hot = (place_hot & (e_row < 16 * lags)).astype(F32).astype(BF16)

    def coefficients(v, begin, end):
        across(lambda o: table_copy(v, o, o).wait())
        tables = [parts_ref[v, k] for k in range(count // 2)]
        while len(tables) > 1:
            tables = [tables[k] + tables[k + 1] for k in range(0, len(tables), 2)]
        total = tables[0] * area
        ahead = table_ref[0, v] * (total - table_ref[1, v])
        over = jnp.transpose(jnp.concatenate([ahead] * 16, axis=0))
        rows = []
        for s in range(begin, end):
            back = (128 - slot_rows(s, 0)) % 128
            value = ahead if back == 0 else pltpu.roll(ahead, back, 1)
            hi = value.astype(BF16).astype(F32)
            rows += [hi, value - hi]
        ahead_rows = mm(jnp.concatenate(rows, axis=0).astype(BF16), place_hot)
        for s in range(begin, end):
            behind = jnp.zeros((bins, 128), F32)
            for l in range(lags):
                at = slot_rows(s, l)
                behind = jnp.where(lane // 32 == lags - 1 - l, over[at : at + 8], behind)
            hi = behind.astype(BF16).astype(F32)
            tiles = []
            for at, value in ((0, hi), (1, behind - hi)):
                row = (2 * (s - begin) + at) * 8
                z = ahead_rows[row : row + 8]
                value = value.astype(BF16).astype(F32)
                for x in range(4):
                    near = (lane // 8) % 4 == x
                    tiles.append(
                        jnp.concatenate(
                            [jnp.where(near, z[:, :128] + value, 0.0), jnp.where(near, z[:, 128:], 0.0)], axis=1
                        )
                    )
            coef_ref[s] = jnp.concatenate(tiles, axis=0).astype(BF16)
        return total

    def backward(s, carry):
        coef = coef_ref[s][:, : 32 * (2 * lags - 1)]
        for g in range(0, groups, 2):
            t = mm(coef, moved_ref[s, g // 2])
            t = t[:32] + t[32:]
            t_ref[g * 32 : (g + 1) * 32, :] = t[:, :width]
            t_ref[(g + 1) * 32 : (g + 2) * 32, :] = t[:, width:]
        hi, lo = halves(masked(t_ref[...], mask_w_ref))
        p = mm(jnp.concatenate([hi[:, :256], hi[:, 128:]], axis=0), adj_ref[s])
        q = mm(jnp.concatenate([lo[:, :256], lo[:, 128:]], axis=0), adj_ref[s, :, :128])
        c = p[:, :128] + p[:, 128:] + q
        hi, lo = halves(jnp.concatenate([c[:size], c[size:]], axis=1))
        cg_hi_ref[s] = hi
        cg_lo_ref[s] = lo
        return carry

    totals = []
    for v, (begin, end) in enumerate(((0, EARLY), (EARLY, scales))):
        totals.append(coefficients(v, begin, end))
        steps(begin, end, backward, 0)
        deep = (end - begin) * size
        cg_hi = cg_hi_ref[begin:end].reshape(deep, chunk)
        cg_lo = cg_lo_ref[begin:end].reshape(deep, chunk)
        part = slice(begin * size, end * size)
        out = mm3((back_hi_ref[:, part], back_lo_ref[:, part]), (cg_hi, cg_lo))
        if v == 0:
            out_ref[...] = out
    out = out_ref[...] + out

    for k in range(count):
        block = out[8 * k : 8 * k + 8]
        largest = jnp.max(jnp.abs(block), axis=0, keepdims=True)
        largest = jnp.broadcast_to(jnp.max(largest, axis=1, keepdims=True), (8, 128))
        power = jnp.maximum(jnp.ceil(jnp.log2(jnp.maximum(largest, 1e-30)) + 0.001), -90.0)
        scale = jnp.exp2(15.0 - power) * (32766.0 / 32768.0)
        left = jnp.round(block[:, :128] * scale).astype(jnp.int32)
        right = jnp.round(block[:, 128:] * scale).astype(jnp.int32)
        grad_ref[k, :8] = left * 65536 + (right + 32768)
        grad_ref[k, 8:] = power[:1].astype(jnp.int32)

    def grad_copy(other, slot):
        return pltpu.make_async_remote_copy(
            src_ref=grad_ref.at[other],
            dst_ref=land_ref.at[slot],
            send_sem=send_g.at[other],
            recv_sem=recv_g.at[slot],
            device_id=(other // sky, lax.rem(other, sky)),
            device_id_type=MESH,
        )

    each(count, me, lambda o: grad_copy(o, me).start())
    own = pltpu.make_async_copy(grad_ref.at[me], land_ref.at[me], own_sem.at[1])
    own.start()

    hot = jnp.concatenate([first_hot16, jnp.zeros((128 - bins, 128), BF16)], axis=0)
    for v in range(vregs):
        parts = thirds(jnp.transpose(jnp.concatenate([totals[v]] * 16, axis=0)))
        picked = mm(parts[0], hot) + mm(parts[1], hot) + mm(parts[2], hot)
        for s in [s for s in range(scales) if spot_of(s)[0] == v]:
            for l in range(lags):
                at = slot_rows(s, l)
                value = jnp.sum(jnp.where(second_hot, picked[at : at + 8], 0.0), axis=0, keepdims=True)
                corr_ref[s, l : l + 1, :] = value[:, :pairs]

    def unpack(slot):
        word = land_ref[pl.ds(slot, 1), :8][0]
        power = jnp.broadcast_to(land_ref[pl.ds(slot, 1), 8:][0], (8, 128)).astype(F32)
        scale = jnp.exp2(power - 15.0) * (32768.0 / 32766.0)
        at = pl.multiple_of(slot * chunk, 128)
        result_ref[:, pl.ds(at, 128)] = (word >> 16).astype(F32) * scale
        result_ref[:, pl.ds(at + 128, 128)] = ((word & 65535) - 32768).astype(F32) * scale

    own.wait()
    unpack(me)

    def receive(k, carry):
        slot = lax.rem(me + count - k, count)
        grad_copy(slot, slot).wait_recv()
        unpack(slot)
        return carry

    lax.fori_loop(1, count, receive, 0)
    each(count, me, lambda o: grad_copy(o, o).wait_send())


def fast_device(lensing_maps, filter_taps, survey_mask, bin_pairs, target_corr, pair_weight):
    scales, tap_count = filter_taps.shape
    half = (tap_count - 1) // 2
    strip = lensing_maps[0]
    strip_rows, cols = strip.shape
    bins, sky = lax.axis_size("bin"), lax.axis_size("sky")
    count = bins * sky
    pairs, lags = pair_weight.shape[0], pair_weight.shape[2]
    chunk = cols // count
    width = chunk + 128
    size = bins * XB
    groups = size // 32
    vregs = 2
    spec = pl.BlockSpec(memory_space=pltpu.VMEM)
    dma = pltpu.SemaphoreType.DMA
    table = (vregs, bins, 128)
    result, corr = pl.pallas_call(
        functools.partial(fast_kernel, bins, sky, scales, lags, chunk, half, 1.0 / (strip_rows * sky * cols)),
        out_shape=(
            pltpu.VMEM((strip_rows, cols), F32),
            pltpu.VMEM((scales, lags, pairs), F32),
        ),
        in_specs=[pl.BlockSpec(memory_space=pl.ANY)] * 6,
        out_specs=(spec, spec),
        scratch_shapes=[
            pltpu.VMEM((strip_rows, cols), BF16),
            pltpu.VMEM(filter_taps.shape, F32),
            pltpu.VMEM(survey_mask.shape, jnp.int32),
            pltpu.VMEM((2, pairs), jnp.int32),
            pltpu.VMEM((scales, lags, pairs), F32),
            pltpu.VMEM((scales, lags, pairs), F32),
            pltpu.VMEM((strip_rows, cols + 128), BF16),
            pltpu.VMEM((count // 2, strip_rows, 2 * chunk + 128), BF16),
            pltpu.VMEM((count // 2, strip_rows, width), BF16),
            pltpu.VMEM((size, width), BF16),
            pltpu.VMEM((8, 128), F32),
            pltpu.VMEM((sky, 8, 128), F32),
            pltpu.VMEM((sky, 8, width), F32),
            pltpu.VMEM((sky, 8, width), F32),
            pltpu.VMEM((scales, size, size), BF16),
            pltpu.VMEM((scales, size, size), BF16),
            pltpu.VMEM((size, scales * size), BF16),
            pltpu.VMEM((size, scales * size), BF16),
            pltpu.VMEM((scales, 256, 256), BF16),
            pltpu.VMEM((scales, 256, 256), BF16),
            pltpu.VMEM((8, 128), F32),
            pltpu.VMEM((2, scales, 8, 128), F32),
            pltpu.VMEM((8, 128), jnp.int32),
            pltpu.VMEM((2,) + table, F32),
            pltpu.VMEM((scales, size, width), BF16),
            pltpu.VMEM((scales, groups // 2, 32 * (2 * lags - 1), 2 * width), BF16),
            pltpu.VMEM((scales, 64, 256), BF16),
            pltpu.VMEM((size, width), F32),
            pltpu.VMEM((scales, size, chunk), BF16),
            pltpu.VMEM((scales, size, chunk), BF16),
            pltpu.VMEM((size, chunk), F32),
            pltpu.VMEM((count, strip_rows + 1, 128), jnp.int32),
            pltpu.VMEM((count, strip_rows + 1, 128), jnp.int32),
            pltpu.VMEM(table, F32),
            pltpu.VMEM(table, F32),
            pltpu.VMEM(table, F32),
            pltpu.VMEM((vregs, count // 2, bins, 128), F32),
            dma((count // 2,)), dma((count // 2,)), dma((count // 2,)), dma((count // 2,)), dma((3,)), dma((3,)),
            dma((vregs,)), dma((vregs,)),
            dma((vregs, count // 2)), dma((vregs, count // 2)),
            dma((count,)), dma((count,)), dma((2,)), dma((6,)),
        ],
        compiler_params=pltpu.CompilerParams(
            collective_id=1, has_side_effects=True, vmem_limit_bytes=VMEM_LIMIT
        ),
    )(
        strip,
        filter_taps,
        survey_mask,
        bin_pairs.T,
        jnp.transpose(target_corr, (1, 2, 0)),
        jnp.transpose(pair_weight, (1, 2, 0)),
    )
    return (jnp.transpose(corr, (2, 0, 1)), result[None])


def fits(mesh, maps, taps, survey_mask, weight):
    bins, sky = mesh.shape["bin"], mesh.shape["sky"]
    rows, cols = maps.shape[1:]
    return (
        maps.shape[0] == bins == 8
        and rows == XB == 8 * sky
        and cols == 256 * bins * sky
        and survey_mask.shape == (sky, cols // 128)
        and EARLY < taps.shape[0] <= 2 * EARLY
        and taps.shape[1] == 17
        and weight.shape[0] <= 128
        and weight.shape[2] == 4
    )


def solution(mesh):
    placed = (P("bin", "sky", None), P(), P("sky", None), P(), P(), P())

    def step(lensing_maps, filter_taps, survey_mask, bin_pairs, target_corr, pair_weight):
        fast = fits(mesh, lensing_maps, filter_taps, survey_mask, pair_weight)
        return jax.shard_map(
            fast_device if fast else per_device,
            mesh=mesh,
            in_specs=placed,
            out_specs=(P(), P("bin", "sky", None)),
            check_vma=False,
        )(lensing_maps, filter_taps, survey_mask, bin_pairs, target_corr, pair_weight)

    return step
```

```python
import functools

import jax
import jax.numpy as jnp
from jax import lax
from jax.experimental import pallas as pl
from jax.experimental.pallas import tpu as pltpu
from jax.sharding import PartitionSpec as P

F32 = jnp.float32
BF16 = jnp.bfloat16
XB = 32
MESH = pl.DeviceIdType.MESH
VMEM_LIMIT = 60 * 1024 * 1024


def round_up(n, m):
    return -(-n // m) * m


def halves(value):
    hi = value.astype(BF16)
    lo = (value - hi.astype(F32)).astype(BF16)
    return hi, lo


def mm(a, b):
    return jnp.dot(a, b, preferred_element_type=F32)


def mm3(a, b):
    return mm(a[0], b[0]) + mm(a[0], b[1]) + mm(a[1], b[0])


def place(bins, sky):
    return lax.axis_index("bin") * sky + lax.axis_index("sky")


def greet(me, bins, sky):
    count = bins * sky
    barrier = pltpu.get_barrier_semaphore()

    def hello(k, carry):
        other = lax.rem(me + k, count)
        pl.semaphore_signal(
            barrier, inc=1, device_id=(other // sky, lax.rem(other, sky)), device_id_type=MESH
        )
        return carry

    lax.fori_loop(1, count, hello, 0)
    pl.semaphore_wait(barrier, count - 1)


def band(row, height, width, shift, out_width):
    full = pltpu.roll(
        jnp.broadcast_to(row, (height, width)), width - shift, 1, stride=1, stride_axis=0
    )
    return full[:, :out_width]


def same_row(count):
    left = lax.rem(lax.broadcasted_iota(jnp.int32, (count, count), 0), XB)
    right = lax.rem(lax.broadcasted_iota(jnp.int32, (count, count), 1), XB)
    return (left == right).astype(F32)


def step_kernel(
    bins, sky, scales, lags, groups, chunk, halo, tiles, half, area, src_of, dst_of,
    x_ref, mark_ref, tap_ref, pair_ref, fit_ref,
    result_ref, corr_ref,
    y_ref, marks_ref, hi_ref, lo_ref, g_ref, sums_ref, grad_ref,
    col_ref, adj_ref, part_ref, sky_ref, bin_in_ref, bin_ref,
    send_x, recv_x, send_m, recv_m, send_s, recv_s, send_b, recv_b, send_g, recv_g, own_sem, coef_ref,
):
    count = bins * sky
    strip_rows, width = y_ref.shape[1], y_ref.shape[2]
    pieces, part_width = grad_ref.shape[0], grad_ref.shape[3]
    span = adj_ref.shape[2]
    size = bins * XB
    rows = groups * XB
    my_bin, my_sky = lax.axis_index("bin"), lax.axis_index("sky")
    me = place(bins, sky)
    greet(me, bins, sky)

    def window_copy(other, slot):
        return pltpu.make_async_remote_copy(
            src_ref=src_of(x_ref, other),
            dst_ref=y_ref.at[slot],
            send_sem=send_x.at[other],
            recv_sem=recv_x.at[slot],
            device_id=(other // sky, lax.rem(other, sky)),
            device_id_type=MESH,
        )

    def along(axis, src, dst, send, recv, other, slot):
        return pltpu.make_async_remote_copy(
            src_ref=src,
            dst_ref=dst.at[slot],
            send_sem=send.at[other],
            recv_sem=recv.at[slot],
            device_id=(my_bin, other) if axis == "sky" else (other, my_sky),
            device_id_type=MESH,
        )

    def each(n, mine, act):
        def body(k, carry):
            act(lax.rem(mine + k, n))
            return carry

        lax.fori_loop(1, n, body, 0)

    each(sky, my_sky, lambda o: along("sky", mark_ref, marks_ref, send_m, recv_m, o, my_sky).start())
    each(count, me, lambda o: window_copy(o, me).start())
    own_mark = pltpu.make_async_copy(mark_ref, marks_ref.at[my_sky], own_sem.at[0])
    own_mark.start()
    own = pltpu.make_async_copy(src_of(x_ref, me), y_ref.at[me], own_sem.at[1])
    own.start()

    tall = tap_ref.shape[3]
    row_hi, row_lo, back_hi, back_lo = [], [], [], []
    narrow = round_up(rows + 2 * half + 1, 128)
    for s in range(scales):
        taps, turned = tap_ref[0, s], tap_ref[1, s]
        for at, part in enumerate(halves(band(turned[:, :width], width, width, half, width))):
            col_ref[at, s] = part
        for at, part in enumerate(
            halves(band(taps[:, :span], span, span, half + halo, part_width))
        ):
            adj_ref[at, s] = part
        a, b = halves(band(taps[:, :narrow], rows, narrow, half, rows))
        row_hi.append(a)
        row_lo.append(b)
        back = band(turned[:, :narrow], rows, narrow, half, rows)
        back_hi.append(back)
    row_hi = jnp.concatenate(row_hi, axis=0)
    row_lo = jnp.concatenate(row_lo, axis=0)
    back = halves(jnp.concatenate(back_hi, axis=1))
    diag = same_row(size)
    lanes = lax.broadcasted_iota(jnp.int32, (size, width), 1)
    owned = (lanes >= halo) & (lanes < halo + chunk)
    spot = lax.rem(lax.broadcasted_iota(jnp.int32, (bins, size), 1), XB)
    bin_row = lax.broadcasted_iota(jnp.int32, (bins, size), 0)

    pairs = fit_ref.shape[1]
    first = jnp.broadcast_to(pair_ref[:, 0:1], (pairs, size))
    second = jnp.broadcast_to(pair_ref[:, 1:2], (pairs, size))
    right_hot = lax.broadcasted_iota(jnp.int32, (pairs, size), 1) // XB == second
    weight = jnp.zeros((bins, size), F32)
    target = jnp.zeros((bins, size), F32)
    for i in range(bins):
        hot = right_hot & (first == i)
        weight_row = jnp.sum(jnp.where(hot, fit_ref[0], 0.0), axis=0, keepdims=True)
        target_row = jnp.sum(jnp.where(hot, fit_ref[1], 0.0), axis=0, keepdims=True)
        weight = jnp.where(bin_row == i, weight_row, weight)
        target = jnp.where(bin_row == i, target_row, target)
    sums_ref[...] = jnp.zeros_like(sums_ref)

    each(sky, my_sky, lambda o: along("sky", mark_ref, marks_ref, send_m, recv_m, o, o).wait())
    own_mark.wait()
    each(count, me, lambda o: window_copy(o, o).wait())
    own.wait()

    mark_width = mark_ref.shape[1]
    start = me * chunk - halo + 128
    marks = marks_ref[...].reshape(rows, mark_width)
    marks = pltpu.roll(marks, lax.rem(mark_width - start // 128, mark_width), 1)
    which = (lax.broadcasted_iota(jnp.int32, (rows, width), 1) + start) // 128 - start // 128
    mask = jnp.zeros((rows, width), F32)
    for t in range(tiles):
        mask = jnp.where(which == t, jnp.broadcast_to(marks[:, t : t + 1], (rows, width)), mask)
    masks = [
        jnp.concatenate([mask[g * XB : (g + 1) * XB]] * bins, axis=0) > 0 for g in range(groups)
    ]

    for b in range(bins):
        y = jnp.concatenate([y_ref[b * sky + k].astype(F32) for k in range(sky)], axis=0)
        y = y.astype(BF16)
        hi, lo = halves(mm(row_hi, y) + mm(row_lo, y))
        for s in range(scales):
            for g in range(groups):
                part = slice(s * rows + g * XB, s * rows + (g + 1) * XB)
                hi_ref[g, s, b * XB : (b + 1) * XB, :] = hi[part]
                lo_ref[g, s, b * XB : (b + 1) * XB, :] = lo[part]

    for g in range(groups):

        def forward(s, carry):
            matrix = (col_ref[0, s], col_ref[1, s])
            filtered = mm3((hi_ref[g, s], lo_ref[g, s]), matrix).astype(BF16).astype(F32)
            kept = jnp.where(masks[g], filtered, 0.0)
            g_ref[g, s] = kept.astype(BF16)
            left = jnp.where(owned, kept, 0.0).astype(BF16)
            for l in range(lags):
                right = kept if l == 0 else pltpu.roll(kept, width - l, 1)
                gram = lax.dot_general(
                    left, right.astype(BF16), (((1,), (1,)), ((), ())), preferred_element_type=F32
                )
                gram = jnp.sum((gram * diag).reshape(bins, XB, size), axis=1)
                sums_ref[s * lags + l] = sums_ref[s * lags + l] + gram
            return carry

        lax.fori_loop(0, scales, forward, 0)

    table = jnp.zeros((bins, size), F32)
    for at in range(scales * lags):
        value = sums_ref[at]
        for step in (16, 8, 4, 2, 1):
            value = value + pltpu.roll(value, size - step, 1)
        if at:
            value = pltpu.roll(value, at, 1)
        table = jnp.where(spot == at, value, table)

    part_ref[...] = table
    each(sky, my_sky, lambda o: along("sky", part_ref, sky_ref, send_s, recv_s, o, my_sky).start())
    sky_ref[pl.ds(my_sky, 1)] = table[None]
    each(sky, my_sky, lambda o: along("sky", part_ref, sky_ref, send_s, recv_s, o, o).wait())
    table = sky_ref[0]
    for k in range(1, sky):
        table = table + sky_ref[k]
    bin_in_ref[...] = table
    each(bins, my_bin, lambda o: along("bin", bin_in_ref, bin_ref, send_b, recv_b, o, my_bin).start())
    bin_ref[pl.ds(my_bin, 1)] = table[None]
    each(bins, my_bin, lambda o: along("bin", bin_in_ref, bin_ref, send_b, recv_b, o, o).wait())
    table = bin_ref[0]
    for k in range(1, bins):
        table = table + bin_ref[k]
    table = table * area

    picked = jnp.zeros((pairs, size), F32)
    for i in range(bins):
        picked = jnp.where(first == i, jnp.broadcast_to(table[i : i + 1], (pairs, size)), picked)
    picked = jnp.where(right_hot, picked, 0.0)
    step = size // 2
    while step >= XB:
        picked = picked + pltpu.roll(picked, step, 1)
        step //= 2
    corr_ref[...] = picked

    ahead = jnp.where(spot < scales * lags, weight * (table - target), 0.0)
    spread = jnp.broadcast_to(ahead[:, None, :], (bins, XB, size)).reshape(size, size)
    behind = jnp.sum(jnp.transpose(spread * diag).reshape(bins, XB, size), axis=1)

    def coefficient(values, at):
        value = jnp.where(spot == at, values, 0.0)
        value = pltpu.roll(value, lax.rem(size - at, size), 1)
        for step in (1, 2, 4, 8, 16):
            value = value + pltpu.roll(value, step, 1)
        return value

    def grad_copy(piece, other, slot):
        return pltpu.make_async_remote_copy(
            src_ref=grad_ref.at[piece, other],
            dst_ref=dst_of(result_ref, slot, piece),
            send_sem=send_g.at[piece, other],
            recv_sem=recv_g.at[piece, slot],
            device_id=(other // sky, lax.rem(other, sky)),
            device_id_type=MESH,
        )

    own_grads = []
    for piece in range(pieces):
        cut = slice(piece * part_width, piece * part_width + span)
        for g in range(groups):

            def backward(s, carry):
                maps = g_ref[g, s, :, cut].astype(F32)
                total_grad = jnp.zeros((size, span), F32)
                for shift in range(1 - lags, lags):
                    moved = maps if shift == 0 else pltpu.roll(maps, (span - shift) % span, 1)
                    moved = moved.astype(BF16)
                    at = s * (2 * lags - 1) + shift + lags - 1
                    if piece == 0:
                        if shift == 0:
                            coef = coefficient(ahead + behind, s * lags)
                        elif shift > 0:
                            coef = coefficient(ahead, s * lags + shift)
                        else:
                            coef = coefficient(behind, s * lags - shift)
                        if pieces > 1 or groups > 1:
                            coef_ref[at] = coef
                    else:
                        coef = coef_ref[at]
                    full = jnp.broadcast_to(coef[:, None, :], (bins, XB, size))
                    hi, lo = halves(full.reshape(size, size) * diag)
                    total_grad = total_grad + mm(hi, moved) + mm(lo, moved)
                total_grad = jnp.where(masks[g][:, cut], total_grad, 0.0)
                hi, lo = halves(mm3(halves(total_grad), (adj_ref[0, s], adj_ref[1, s])))
                hi_ref[g, s, :, :part_width] = hi
                lo_ref[g, s, :, :part_width] = lo
                return carry

            lax.fori_loop(0, scales, backward, 0)

        for b in range(bins):
            spots = [(g, s) for s in range(scales) for g in range(groups)]
            rows_of = slice(b * XB, (b + 1) * XB)
            hi = jnp.concatenate([hi_ref[g, s, rows_of, :part_width] for g, s in spots], axis=0)
            lo = jnp.concatenate([lo_ref[g, s, rows_of, :part_width] for g, s in spots], axis=0)
            total_rows = mm3(back, (hi, lo))
            for k in range(sky):
                at = b * sky + k
                grad_ref[piece, at] = total_rows[k * strip_rows : (k + 1) * strip_rows]

        each(count, me, lambda o: grad_copy(piece, o, me).start())
        own_grad = pltpu.make_async_copy(
            grad_ref.at[piece, me], dst_of(result_ref, me, piece), own_sem.at[2 + piece]
        )
        own_grad.start()
        own_grads.append(own_grad)
    for piece in range(pieces):
        each(count, me, lambda o: grad_copy(piece, o, o).wait())
        own_grads[piece].wait()


def per_device(lensing_maps, filter_taps, survey_mask, bin_pairs, target_corr, pair_weight):
    scales, tap_count = filter_taps.shape
    half = (tap_count - 1) // 2
    strip = lensing_maps[0]
    strip_rows, cols = strip.shape
    bins, sky = lax.axis_size("bin"), lax.axis_size("sky")
    count = bins * sky
    pairs, lags = pair_weight.shape[0], pair_weight.shape[2]
    row_count = strip_rows * sky
    groups = row_count // XB
    chunk = cols // count
    width = round_up(chunk + 2 * (2 * half + lags - 1), 128)
    halo = (width - chunk) // 2
    out_width = round_up(chunk, 128)
    tiles = width // 128 + 1
    size = bins * XB
    aligned = chunk % 128 == 0
    pieces = out_width // 128
    part_width = out_width // pieces
    span = width - (pieces - 1) * part_width

    windows = jnp.pad(strip, ((0, 0), (halo, halo)))
    if not aligned:
        windows = jnp.stack([windows[:, d * chunk : d * chunk + width] for d in range(count)])
    mark_width = round_up(survey_mask.shape[1] + 1 + tiles, 128)
    marks = jnp.pad(
        survey_mask.astype(F32), ((0, 0), (1, mark_width - survey_mask.shape[1] - 1))
    )
    marks = jnp.broadcast_to(marks, (strip_rows, mark_width))
    tall = max(width, round_up(row_count + 2 * half + 1, 128))
    taps = jnp.stack([filter_taps, filter_taps[:, ::-1]])
    taps = jnp.pad(taps, ((0, 0), (0, 0), (0, tall - tap_count)))[:, :, None, :]
    fit = jnp.stack([pair_weight, target_corr]).reshape(2, pairs, scales * lags)
    fit = jnp.tile(jnp.pad(fit, ((0, 0), (0, 0), (0, XB - scales * lags))), (1, 1, bins))

    if aligned:
        src_of = lambda ref, d: ref.at[:, pl.ds(pl.multiple_of(d * chunk, 128), width)]
        dst_of = lambda ref, d, p: ref.at[
            :, pl.ds(pl.multiple_of(d * chunk + p * part_width, 128), part_width)
        ]
        result_shape = (strip_rows, cols)
    else:
        src_of = lambda ref, d: ref.at[d]
        dst_of = lambda ref, d, p: ref.at[d]
        result_shape = (count, strip_rows, out_width)

    spec = pl.BlockSpec(memory_space=pltpu.VMEM)
    table_shape = (bins, size)
    dma = pltpu.SemaphoreType.DMA
    result, corr = pl.pallas_call(
        functools.partial(
            step_kernel, bins, sky, scales, lags, groups, chunk, halo, tiles, half,
            1.0 / (row_count * cols), src_of, dst_of,
        ),
        out_shape=(
            jax.ShapeDtypeStruct(result_shape, F32),
            jax.ShapeDtypeStruct((pairs, size), F32),
        ),
        in_specs=[spec] * 5,
        out_specs=(spec, spec),
        scratch_shapes=[
            pltpu.VMEM((count, strip_rows, width), BF16),
            pltpu.VMEM((sky, strip_rows, mark_width), F32),
            pltpu.VMEM((groups, scales, size, width), BF16),
            pltpu.VMEM((groups, scales, size, width), BF16),
            pltpu.VMEM((groups, scales, size, width), BF16),
            pltpu.VMEM((scales * lags,) + table_shape, F32),
            pltpu.VMEM((pieces, count, strip_rows, part_width), F32),
            pltpu.VMEM((2, scales, width, width), BF16),
            pltpu.VMEM((2, scales, span, part_width), BF16),
            pltpu.VMEM(table_shape, F32),
            pltpu.VMEM((sky,) + table_shape, F32),
            pltpu.VMEM(table_shape, F32),
            pltpu.VMEM((bins,) + table_shape, F32),
            dma((count,)), dma((count,)), dma((sky,)), dma((sky,)), dma((sky,)), dma((sky,)),
            dma((bins,)), dma((bins,)), dma((pieces, count)), dma((pieces, count)), dma((2 + pieces,)),
            pltpu.VMEM((scales * (2 * lags - 1),) + table_shape, F32),
        ],
        compiler_params=pltpu.CompilerParams(
            collective_id=1, has_side_effects=True, vmem_limit_bytes=VMEM_LIMIT
        ),
    )(windows, marks, taps, bin_pairs, fit)
    if not aligned:
        result = jnp.transpose(result[:, :, :chunk], (1, 0, 2)).reshape(strip_rows, cols)
    corr_table = corr[:, : scales * lags].reshape(pairs, scales, lags)
    return (corr_table, result[None])


def tables(bins, scales, lags):
    lane = lax.broadcasted_iota(jnp.int32, (bins, 128), 1)
    high, low = lane // 64, (lane // 8) % 2
    return lane, high, low, 2 * high + low


EARLY = 3


def spot_of(scale):
    return (0, scale) if scale < EARLY else (1, scale - EARLY)


def slot_rows(scale, lag):
    slot = spot_of(scale)[1]
    return 64 * (slot // 2) + 16 * lag + 8 * (slot % 2)


def thirds(value):
    hi = value.astype(BF16)
    rest = value - hi.astype(F32)
    mid = rest.astype(BF16)
    lo = (rest - mid.astype(F32)).astype(BF16)
    return hi, mid, lo


def nt(a, b):
    return lax.dot_general(a, b, (((1,), (1,)), ((), ())), preferred_element_type=F32)


def steps(begin, end, body, carry):
    for s in range(begin, end):
        carry = body(s, carry)
    return carry


def fast_kernel(
    bins, sky, scales, lags, chunk, half, area,
    x_hbm, tap_hbm, mask_hbm, pair_hbm, target_hbm, weight_hbm,
    result_ref, corr_ref,
    x_ref, tap_ref, mask_ref, pair_ref, target_ref, weight_ref,
    pad_ref, wide_ref, y_ref, cols_ref, mark_ref, marks_ref, mask_v_ref, mask_w_ref,
    row_hi_ref, row_lo_ref, back_hi_ref, back_lo_ref, fwd_ref, adj_ref,
    small_ref, fit_ref, pairs_ref, table_ref,
    g_ref, moved_ref, coef_ref, t_ref, cg_hi_ref, cg_lo_ref, out_ref, grad_ref, land_ref,
    part_ref, twin_ref, parts_ref,
    send_x, recv_x, send_y, recv_y, send_m, recv_m, send_c, recv_c, send_t, recv_t, send_g, recv_g, in_sem,
):
    count = bins * sky
    cols = x_ref.shape[1]
    width = y_ref.shape[2]
    halo = (width - chunk) // 2
    pairs = pair_ref.shape[1]
    taps_n = tap_ref.shape[1]
    size = bins * XB
    groups = size // 32
    vregs = part_ref.shape[0]
    my_bin, my_sky = lax.axis_index("bin"), lax.axis_index("sky")
    me = place(bins, sky)

    barrier = pltpu.get_barrier_semaphore()

    bits = count.bit_length() - 1
    flips = [(1 - 2 * lax.rem(me // 2**i, 2)) * 2**i for i in range(bits)]

    def flipped(mask):
        other = me
        for i in range(bits):
            if (mask >> i) & 1:
                other = other + flips[i]
        return other

    def arrived(ref, sem):
        pltpu.make_async_copy(ref, ref, sem).wait()

    chips = count // 2
    far_first = range(chips - 1, 0, -1)

    def hello(other):
        pl.semaphore_signal(
            barrier, inc=1, device_id=(other // sky, lax.rem(other, sky)), device_id_type=MESH
        )

    hello(me + flips[0])
    for k in far_first:
        hello(flipped(2 * k))
    loads = [
        pltpu.make_async_copy(src, dst, in_sem.at[i])
        for i, (src, dst) in enumerate(
            (
                (x_hbm, x_ref), (mask_hbm, mask_ref), (tap_hbm, tap_ref),
                (pair_hbm, pair_ref), (target_hbm, target_ref), (weight_hbm, weight_ref),
            )
        )
    ]
    for load in loads:
        load.start()

    chip, core = me // 2, lax.rem(me, 2)
    twin = me + flips[0]
    wide = 2 * chunk + 2 * halo

    def remote(src, dst, send, recv, other):
        return pltpu.make_async_remote_copy(
            src_ref=src,
            dst_ref=dst,
            send_sem=send,
            recv_sem=recv,
            device_id=(other // sky, lax.rem(other, sky)),
            device_id_type=MESH,
        )

    def window_copy(k):
        other = flipped(2 * k)
        src = pad_ref.at[:, pl.ds(pl.multiple_of((other // 2) * 2 * chunk, 128), wide)]
        return remote(src, wide_ref.at[k], send_x.at[0], recv_x.at[k], other)

    def twin_copy(k):
        src = wide_ref.at[k, :, pl.ds(pl.multiple_of((1 - core) * chunk, 128), width)]
        return remote(src, y_ref.at[k], send_y.at[0], recv_y.at[k // 4], twin)

    beside = me + flips[1]

    def mark_copy(n, slot, to):
        src = mark_ref if n < 2 else marks_ref.at[slot]
        return remote(src, marks_ref.at[slot], send_m.at[n], recv_m.at[n], to)

    loads[0].wait()
    loads[1].wait()
    moved_x = pltpu.roll(x_ref[...].astype(F32), halo, 1)
    edge = lax.broadcasted_iota(jnp.int32, (moved_x.shape[0], 128), 1) < halo
    pad_ref[:, :128] = jnp.where(edge, 0.0, moved_x[:, :128]).astype(BF16)
    pad_ref[:, 128:cols] = moved_x[:, 128:].astype(BF16)
    pad_ref[:, cols:] = jnp.where(edge, moved_x[:, :128], 0.0).astype(BF16)
    mark_ref[...] = jnp.zeros_like(mark_ref)
    mark_ref[:, : mask_ref.shape[1]] = jnp.broadcast_to(
        mask_ref[...].astype(F32), (mark_ref.shape[0], mask_ref.shape[1])
    )

    pl.semaphore_wait(barrier, count // 2)
    for k in far_first:
        window_copy(k).start()
    mark_copy(0, my_sky, twin).start()
    mark_copy(1, my_sky, beside).start()
    at = pl.multiple_of(chip * 2 * chunk, 128)
    wide_ref[0] = pad_ref[:, pl.ds(at, wide)]
    twin_copy(0).start()
    marks_ref[pl.ds(my_sky, 1)] = mark_ref[...][None]

    for load in loads[2:]:
        load.wait()
    small_ref[...] = jnp.zeros_like(small_ref)
    small_ref[:scales, :taps_n] = tap_ref[...]
    tap_hi, tap_lo = halves(small_ref[...])
    tap_row = lax.broadcasted_iota(jnp.int32, (128, 256), 0)
    tap_col = lax.broadcasted_iota(jnp.int32, (128, 256), 1)
    real = tap_row < taps_n

    def spread(hot):
        hot = (hot & real).astype(F32).astype(BF16)
        return mm(tap_hi, hot) + mm(tap_lo, hot)

    straight = spread(tap_col == tap_row)
    turned = spread(tap_col == taps_n - 1 - tap_row)
    spaced = spread(tap_col == bins * (taps_n - 1 - tap_row))
    sub = lax.broadcasted_iota(jnp.int32, (bins, size), 0)
    col = lax.broadcasted_iota(jnp.int32, (bins, size), 1)
    turns = [pltpu.roll(straight, (XB * b - half) % size, 1) for b in range(bins)]
    for s in range(scales):
        reach = halo + half
        for ref, taps in ((fwd_ref, turned), (adj_ref, straight)):
            hi, lo = halves(band(taps[s : s + 1], 256, 256, reach, 128))
            ref[s, :, :128] = hi
            ref[s, :, 128:] = lo
        first = jnp.zeros((bins, size), F32)
        for b in range(bins):
            first = jnp.where(sub == b, jnp.broadcast_to(turns[b][s : s + 1], (bins, size)), first)
        tiles = [
            jnp.where(col // XB == sub, first if x == 0 else pltpu.roll(first, x, 1), 0.0)
            for x in range(XB)
        ]
        hi, lo = halves(jnp.concatenate(tiles, axis=0))
        row_hi_ref[s] = hi
        row_lo_ref[s] = lo
        first = pltpu.roll(
            jnp.broadcast_to(spaced[s : s + 1], (8, size)), 0, 1, stride=bins, stride_axis=0
        )
        tiles = []
        for b in range(bins):
            for k in range(XB // 8):
                shift = (bins * 8 * k - bins * half + b) % size
                apart = col // bins - sub - 8 * k
                near = (apart <= half) & (apart >= -half)
                tiles.append(jnp.where(near, first if shift == 0 else pltpu.roll(first, shift, 1), 0.0))
        hi, lo = halves(jnp.concatenate(tiles, axis=0))
        back_hi_ref[:, s * size : (s + 1) * size] = hi
        back_lo_ref[:, s * size : (s + 1) * size] = lo

    lane, high, low, slot = tables(bins, scales, lags)
    pairs_ref[...] = jnp.full_like(pairs_ref, -1)
    pairs_ref[:2, :pairs] = pair_ref[...]
    fit_ref[...] = jnp.zeros_like(fit_ref)
    for s in range(scales):
        fit_ref[0, s, :lags, :pairs] = weight_ref[s]
        fit_ref[1, s, :lags, :pairs] = target_ref[s]
    bin_of = lax.broadcasted_iota(jnp.int32, (bins, 128), 0)
    first_hot = (pairs_ref[0:1, :] == bin_of).astype(F32)
    second_hot = pairs_ref[1:2, :] == bin_of
    first_hot16 = first_hot.astype(BF16)
    for at in range(2):
        for v in range(vregs):
            tiles = []
            for tile in range(16):
                at_slot, l = 2 * (tile // 8) + tile % 2, (tile // 2) % 4
                s = at_slot + v * EARLY
                if s < scales and spot_of(s) == (v, at_slot):
                    row = jnp.broadcast_to(fit_ref[at, s, l : l + 1, :], (bins, 128))
                    tiles.append(jnp.where(second_hot, row, 0.0))
                else:
                    tiles.append(jnp.zeros((bins, 128), F32))
            parts = thirds(jnp.concatenate(tiles, axis=0))
            table_ref[at, v] = nt(first_hot16, parts[0]) + nt(first_hot16, parts[1]) + nt(first_hot16, parts[2])

    far = lax.rem(beside, sky)
    mark_copy(1, far, beside).wait()
    mark_copy(2, far, twin).start()
    mark_copy(0, lax.rem(twin, sky), twin).wait()
    mark_copy(2, lax.rem(beside + flips[0], sky), twin).wait()
    for k in range(sky):
        marks = pltpu.roll(marks_ref[k], 1, 1)
        marks = pltpu.roll(marks, lax.rem(128 - 2 * me, 128), 1)
        left, one, two, right = [jnp.broadcast_to(marks[:, t : t + 1], (8, 128)) for t in range(4)]
        lanes = lax.broadcasted_iota(jnp.int32, (8, 128), 1)
        mask_v_ref[k, :, :128] = one
        mask_v_ref[k, :, 128:256] = two
        mask_v_ref[k, :, 256:] = jnp.where(lanes < 64, right, left)
        mask_w_ref[k, :, :128] = jnp.where(lanes < 64, left, one)
        mask_w_ref[k, :, 128:256] = jnp.where(lanes < 64, one, two)
        mask_w_ref[k, :, 256:] = jnp.where(lanes < 64, two, right)

    def masked(value, ref):
        tall = size // sky
        return jnp.concatenate(
            [value[k * tall : (k + 1) * tall] * jnp.broadcast_to(ref[k, 0:1, :], (tall, width)) for k in range(sky)],
            axis=0,
        )

    def stacked(v):
        return jnp.concatenate(
            [v[:, :256], v[:, 128:], jnp.concatenate([v[:, 256:], v[:, :128]], axis=1)], axis=0
        )

    mine = pl.multiple_of(core * chunk, 128)

    def pass_on(layer):
        for k in range(4 * layer, 4 * layer + 4):
            if k:
                window_copy(k).wait_recv()
                twin_copy(k).start()

    def columns(layer):
        arrived(y_ref.at[4 * layer : 4 * layer + 4], recv_y.at[layer])
        first = (flipped(8 * layer) // 8) * 4
        rows = []
        for c in range(4):
            slot = 4 * layer + lax.rem(chip + c % 2, 2) + 2 * lax.rem(chip // 2 + c // 2, 2)
            direct = wide_ref[pl.ds(slot, 1), :, pl.ds(mine, width)][0].astype(F32)
            passed = y_ref[pl.ds(slot, 1)][0].astype(F32)
            rows.append(jnp.where(core == 0, direct, passed))
            rows.append(jnp.where(core == 1, direct, passed))
        y = stacked(jnp.concatenate(rows, axis=0).astype(BF16))
        tall = 2 * XB
        at = pl.multiple_of(first * 16, tall)
        for s in range(scales):
            p = mm(y, fwd_ref[s])
            f = p[:, :128] + p[:, 128:]
            hi, lo = halves(jnp.concatenate([f[:tall], f[tall : 2 * tall], f[2 * tall :]], axis=1))
            cols_ref[s, pl.ds(at, tall), :width] = hi
            cols_ref[s, pl.ds(at, tall), width:] = lo

    layers = count // 8
    pass_on(0)
    for layer in range(layers):
        if layer + 1 < layers:
            pass_on(layer + 1)
        columns(layer)

    def forward(s, carry):
        p = mm(row_hi_ref[s], cols_ref[s])
        q = mm(row_lo_ref[s], cols_ref[s, :, :width])
        f = p[:, :width] + p[:, width:] + q
        kept16 = masked(f, mask_v_ref).astype(BF16)
        g_ref[s] = kept16
        shifted = [kept16[:, l : l + chunk] for l in range(lags)]
        total = jnp.zeros((32, 128), F32)
        for g in range(groups):
            right = jnp.concatenate(
                [shifted[l][g * 32 + 16 * h : g * 32 + 16 * h + 16] for h in range(2) for l in range(lags)],
                axis=0,
            )
            total = total + nt(kept16[g * 32 : (g + 1) * 32, :chunk], right)
        z = jnp.zeros((bins, 128), F32)
        for x in range(4):
            z = jnp.where(slot == x, total[bins * x : bins * (x + 1)], z)
        z = z + pltpu.roll(z, 64, 1)
        z = z + jnp.where(low == 0, pltpu.roll(z, 120, 1), pltpu.roll(z, 8, 1))
        into = s % EARLY
        return jnp.where(slot == into, z, carry)

    def core_copy(v):
        return pltpu.make_async_remote_copy(
            src_ref=part_ref.at[v],
            dst_ref=twin_ref.at[v],
            send_sem=send_c.at[v],
            recv_sem=recv_c.at[v],
            device_id=((me + flips[0]) // sky, lax.rem(me + flips[0], sky)),
            device_id_type=MESH,
        )

    def send_tables(v):
        core_copy(v).wait()
        parts_ref[v, 0] = part_ref[v] + twin_ref[v]
        for k in far_first:
            remote(parts_ref.at[v, 0], parts_ref.at[v, k], send_t.at[v], recv_t.at[v], flipped(2 * k)).start()

    zero = jnp.zeros((bins, 128), F32)
    part_ref[0] = steps(0, EARLY, forward, zero)
    core_copy(0).start()
    late = steps(EARLY, EARLY + 1, forward, zero)
    send_tables(0)
    part_ref[1] = steps(EARLY + 1, scales, forward, late)
    core_copy(1).start()

    def lagging(s, carry):
        kept = g_ref[s]
        for at in range(2 * lags - 1):
            cut = width - halo + (at - lags + 1)
            turn = jnp.concatenate([kept[:, cut:], kept[:, :cut]], axis=1)
            for g in range(groups):
                side = (g % 2) * width
                moved_ref[s, g // 2, at * 32 : (at + 1) * 32, side : side + width] = turn[g * 32 : (g + 1) * 32]
        return carry

    steps(0, 1, lagging, 0)
    send_tables(1)
    steps(1, scales, lagging, 0)

    e_row = lax.broadcasted_iota(jnp.int32, (128, 256), 0)
    e_col = lax.broadcasted_iota(jnp.int32, (128, 256), 1)
    place_hot = (e_row % 16 < 8) & (e_row // 16 == e_col // 32 - (lags - 1)) & (e_row % 8 == e_col % 8)
    place_hot = (place_hot & (e_row < 16 * lags)).astype(F32).astype(BF16)

    def coefficients(v, begin, end):
        arrived(parts_ref.at[v, 1:], recv_t.at[v])
        tables = [parts_ref[v, k] for k in range(chips)]
        while len(tables) > 1:
            tables = [tables[k] + tables[k + 1] for k in range(0, len(tables), 2)]
        total = tables[0] * area
        ahead = table_ref[0, v] * (total - table_ref[1, v])
        over = jnp.transpose(jnp.concatenate([ahead] * 16, axis=0))
        rows = []
        for s in range(begin, end):
            back = (128 - slot_rows(s, 0)) % 128
            value = ahead if back == 0 else pltpu.roll(ahead, back, 1)
            hi = value.astype(BF16).astype(F32)
            rows += [hi, value - hi]
        ahead_rows = mm(jnp.concatenate(rows, axis=0).astype(BF16), place_hot)
        for s in range(begin, end):
            behind = jnp.zeros((bins, 128), F32)
            for l in range(lags):
                at = slot_rows(s, l)
                behind = jnp.where(lane // 32 == lags - 1 - l, over[at : at + 8], behind)
            hi = behind.astype(BF16).astype(F32)
            tiles = []
            for at, value in ((0, hi), (1, behind - hi)):
                row = (2 * (s - begin) + at) * 8
                z = ahead_rows[row : row + 8]
                value = value.astype(BF16).astype(F32)
                for x in range(4):
                    near = (lane // 8) % 4 == x
                    tiles.append(
                        jnp.concatenate(
                            [jnp.where(near, z[:, :128] + value, 0.0), jnp.where(near, z[:, 128:], 0.0)], axis=1
                        )
                    )
            coef_ref[s] = jnp.concatenate(tiles, axis=0).astype(BF16)
        return total

    def backward(s, carry):
        coef = coef_ref[s][:, : 32 * (2 * lags - 1)]
        for g in range(0, groups, 2):
            t = mm(coef, moved_ref[s, g // 2])
            t = t[:32] + t[32:]
            t_ref[g * 32 : (g + 1) * 32, :] = t[:, :width]
            t_ref[(g + 1) * 32 : (g + 2) * 32, :] = t[:, width:]
        hi, lo = halves(masked(t_ref[...], mask_w_ref))
        p = mm(jnp.concatenate([hi[:, :256], hi[:, 128:]], axis=0), adj_ref[s])
        q = mm(jnp.concatenate([lo[:, :256], lo[:, 128:]], axis=0), adj_ref[s, :, :128])
        c = p[:, :128] + p[:, 128:] + q
        hi, lo = halves(jnp.concatenate([c[:size], c[size:]], axis=1))
        cg_hi_ref[s] = hi
        cg_lo_ref[s] = lo
        return carry

    totals = []
    for v, (begin, end) in enumerate(((0, EARLY), (EARLY, scales))):
        totals.append(coefficients(v, begin, end))
        steps(begin, end, backward, 0)
        deep = (end - begin) * size
        cg_hi = cg_hi_ref[begin:end].reshape(deep, chunk)
        cg_lo = cg_lo_ref[begin:end].reshape(deep, chunk)
        part = slice(begin * size, end * size)
        out = mm3((back_hi_ref[:, part], back_lo_ref[:, part]), (cg_hi, cg_lo))
        if v == 0:
            out_ref[...] = out
    out = out_ref[...] + out

    for k in range(count):
        block = out[8 * k : 8 * k + 8]
        largest = jnp.max(jnp.abs(block), axis=0, keepdims=True)
        largest = jnp.broadcast_to(jnp.max(largest, axis=1, keepdims=True), (8, 128))
        power = jnp.maximum(jnp.ceil(jnp.log2(jnp.maximum(largest, 1e-30)) + 0.001), -90.0)
        scale = jnp.exp2(15.0 - power) * (32766.0 / 32768.0)
        left = jnp.round(block[:, :128] * scale).astype(jnp.int32)
        right = jnp.round(block[:, 128:] * scale).astype(jnp.int32)
        grad_ref[k, :8] = left * 65536 + (right + 32768)
        grad_ref[k, 8:] = power[:1].astype(jnp.int32)

    for k in range(count - 1, 0, -1):
        other = flipped(k)
        remote(grad_ref.at[other], land_ref.at[k], send_g.at[0], recv_g.at[k // 8], other).start()
    land_ref[0] = grad_ref[pl.ds(me, 1)][0]

    hot = jnp.concatenate([first_hot16, jnp.zeros((128 - bins, 128), BF16)], axis=0)
    for v in range(vregs):
        parts = thirds(jnp.transpose(jnp.concatenate([totals[v]] * 16, axis=0)))
        picked = mm(parts[0], hot) + mm(parts[1], hot) + mm(parts[2], hot)
        for s in [s for s in range(scales) if spot_of(s)[0] == v]:
            for l in range(lags):
                at = slot_rows(s, l)
                value = jnp.sum(jnp.where(second_hot, picked[at : at + 8], 0.0), axis=0, keepdims=True)
                corr_ref[s, l : l + 1, :] = value[:, :pairs]

    for layer in range(count // 8):
        arrived(land_ref.at[max(8 * layer, 1) : 8 * layer + 8], recv_g.at[layer])
        for k in range(8 * layer, 8 * layer + 8):
            word = land_ref[k, :8]
            power = jnp.broadcast_to(land_ref[k, 8:], (8, 128)).astype(F32)
            scale = jnp.exp2(power - 15.0) * (32768.0 / 32766.0)
            at = pl.multiple_of(flipped(k) * chunk, 128)
            result_ref[:, pl.ds(at, 128)] = (word >> 16).astype(F32) * scale
            result_ref[:, pl.ds(at + 128, 128)] = ((word & 65535) - 32768).astype(F32) * scale

    arrived(wide_ref.at[1:], send_x.at[0])
    arrived(y_ref, send_y.at[0])
    for v in range(vregs):
        arrived(parts_ref.at[v, 1:], send_t.at[v])
    arrived(land_ref.at[1:], send_g.at[0])


def fast_device(lensing_maps, filter_taps, survey_mask, bin_pairs, target_corr, pair_weight):
    scales, tap_count = filter_taps.shape
    half = (tap_count - 1) // 2
    strip = lensing_maps[0]
    strip_rows, cols = strip.shape
    bins, sky = lax.axis_size("bin"), lax.axis_size("sky")
    count = bins * sky
    pairs, lags = pair_weight.shape[0], pair_weight.shape[2]
    chunk = cols // count
    width = chunk + 128
    size = bins * XB
    groups = size // 32
    vregs = 2
    spec = pl.BlockSpec(memory_space=pltpu.VMEM)
    dma = pltpu.SemaphoreType.DMA
    table = (vregs, bins, 128)
    result, corr = pl.pallas_call(
        functools.partial(fast_kernel, bins, sky, scales, lags, chunk, half, 1.0 / (strip_rows * sky * cols)),
        out_shape=(
            pltpu.VMEM((strip_rows, cols), F32),
            pltpu.VMEM((scales, lags, pairs), F32),
        ),
        in_specs=[pl.BlockSpec(memory_space=pl.ANY)] * 6,
        out_specs=(spec, spec),
        scratch_shapes=[
            pltpu.VMEM((strip_rows, cols), BF16),
            pltpu.VMEM(filter_taps.shape, F32),
            pltpu.VMEM(survey_mask.shape, jnp.int32),
            pltpu.VMEM((2, pairs), jnp.int32),
            pltpu.VMEM((scales, lags, pairs), F32),
            pltpu.VMEM((scales, lags, pairs), F32),
            pltpu.VMEM((strip_rows, cols + 128), BF16),
            pltpu.VMEM((count // 2, strip_rows, 2 * chunk + 128), BF16),
            pltpu.VMEM((count // 2, strip_rows, width), BF16),
            pltpu.VMEM((scales, size, 2 * width), BF16),
            pltpu.VMEM((8, 128), F32),
            pltpu.VMEM((sky, 8, 128), F32),
            pltpu.VMEM((sky, 8, width), F32),
            pltpu.VMEM((sky, 8, width), F32),
            pltpu.VMEM((scales, size, size), BF16),
            pltpu.VMEM((scales, size, size), BF16),
            pltpu.VMEM((size, scales * size), BF16),
            pltpu.VMEM((size, scales * size), BF16),
            pltpu.VMEM((scales, 256, 256), BF16),
            pltpu.VMEM((scales, 256, 256), BF16),
            pltpu.VMEM((8, 128), F32),
            pltpu.VMEM((2, scales, 8, 128), F32),
            pltpu.VMEM((8, 128), jnp.int32),
            pltpu.VMEM((2,) + table, F32),
            pltpu.VMEM((scales, size, width), BF16),
            pltpu.VMEM((scales, groups // 2, 32 * (2 * lags - 1), 2 * width), BF16),
            pltpu.VMEM((scales, 64, 256), BF16),
            pltpu.VMEM((size, width), F32),
            pltpu.VMEM((scales, size, chunk), BF16),
            pltpu.VMEM((scales, size, chunk), BF16),
            pltpu.VMEM((size, chunk), F32),
            pltpu.VMEM((count, strip_rows + 1, 128), jnp.int32),
            pltpu.VMEM((count, strip_rows + 1, 128), jnp.int32),
            pltpu.VMEM(table, F32),
            pltpu.VMEM(table, F32),
            pltpu.VMEM((vregs, count // 2, bins, 128), F32),
            dma((1,)), dma((count // 2,)), dma((1,)), dma((count // 8,)), dma((3,)), dma((3,)),
            dma((vregs,)), dma((vregs,)), dma((vregs,)), dma((vregs,)),
            dma((1,)), dma((count // 8,)), dma((6,)),
        ],
        compiler_params=pltpu.CompilerParams(
            collective_id=1, has_side_effects=True, vmem_limit_bytes=VMEM_LIMIT
        ),
    )(
        strip,
        filter_taps,
        survey_mask,
        bin_pairs.T,
        jnp.transpose(target_corr, (1, 2, 0)),
        jnp.transpose(pair_weight, (1, 2, 0)),
    )
    return (jnp.transpose(corr, (2, 0, 1)), result[None])


def fits(mesh, maps, taps, survey_mask, weight):
    bins, sky = mesh.shape["bin"], mesh.shape["sky"]
    rows, cols = maps.shape[1:]
    return (
        maps.shape[0] == bins == 8
        and rows == XB == 8 * sky
        and cols == 256 * bins * sky
        and survey_mask.shape == (sky, cols // 128)
        and EARLY < taps.shape[0] <= 2 * EARLY
        and taps.shape[1] == 17
        and weight.shape[0] <= 128
        and weight.shape[2] == 4
    )


def solution(mesh):
    placed = (P("bin", "sky", None), P(), P("sky", None), P(), P(), P())

    def step(lensing_maps, filter_taps, survey_mask, bin_pairs, target_corr, pair_weight):
        fast = fits(mesh, lensing_maps, filter_taps, survey_mask, pair_weight)
        return jax.shard_map(
            fast_device if fast else per_device,
            mesh=mesh,
            in_specs=placed,
            out_specs=(P(), P("bin", "sky", None)),
            check_vma=False,
        )(lensing_maps, filter_taps, survey_mask, bin_pairs, target_corr, pair_weight)

    return step
```

```python
import functools

import jax
import jax.numpy as jnp
from jax import lax
from jax.experimental import pallas as pl
from jax.experimental.pallas import tpu as pltpu
from jax.sharding import PartitionSpec as P

F32 = jnp.float32
BF16 = jnp.bfloat16
XB = 32
MESH = pl.DeviceIdType.MESH
VMEM_LIMIT = 60 * 1024 * 1024


def round_up(n, m):
    return -(-n // m) * m


def halves(value):
    hi = value.astype(BF16)
    lo = (value - hi.astype(F32)).astype(BF16)
    return hi, lo


def mm(a, b):
    return jnp.dot(a, b, preferred_element_type=F32)


def mm3(a, b):
    return mm(a[0], b[0]) + mm(a[0], b[1]) + mm(a[1], b[0])


def place(bins, sky):
    return lax.axis_index("bin") * sky + lax.axis_index("sky")


def greet(me, bins, sky):
    count = bins * sky
    barrier = pltpu.get_barrier_semaphore()

    def hello(k, carry):
        other = lax.rem(me + k, count)
        pl.semaphore_signal(
            barrier, inc=1, device_id=(other // sky, lax.rem(other, sky)), device_id_type=MESH
        )
        return carry

    lax.fori_loop(1, count, hello, 0)
    pl.semaphore_wait(barrier, count - 1)


def band(row, height, width, shift, out_width):
    full = pltpu.roll(
        jnp.broadcast_to(row, (height, width)), width - shift, 1, stride=1, stride_axis=0
    )
    return full[:, :out_width]


def same_row(count):
    left = lax.rem(lax.broadcasted_iota(jnp.int32, (count, count), 0), XB)
    right = lax.rem(lax.broadcasted_iota(jnp.int32, (count, count), 1), XB)
    return (left == right).astype(F32)


def step_kernel(
    bins, sky, scales, lags, groups, chunk, halo, tiles, half, area, src_of, dst_of,
    x_ref, mark_ref, tap_ref, pair_ref, fit_ref,
    result_ref, corr_ref,
    y_ref, marks_ref, hi_ref, lo_ref, g_ref, sums_ref, grad_ref,
    col_ref, adj_ref, part_ref, sky_ref, bin_in_ref, bin_ref,
    send_x, recv_x, send_m, recv_m, send_s, recv_s, send_b, recv_b, send_g, recv_g, own_sem, coef_ref,
):
    count = bins * sky
    strip_rows, width = y_ref.shape[1], y_ref.shape[2]
    pieces, part_width = grad_ref.shape[0], grad_ref.shape[3]
    span = adj_ref.shape[2]
    size = bins * XB
    rows = groups * XB
    my_bin, my_sky = lax.axis_index("bin"), lax.axis_index("sky")
    me = place(bins, sky)
    greet(me, bins, sky)

    def window_copy(other, slot):
        return pltpu.make_async_remote_copy(
            src_ref=src_of(x_ref, other),
            dst_ref=y_ref.at[slot],
            send_sem=send_x.at[other],
            recv_sem=recv_x.at[slot],
            device_id=(other // sky, lax.rem(other, sky)),
            device_id_type=MESH,
        )

    def along(axis, src, dst, send, recv, other, slot):
        return pltpu.make_async_remote_copy(
            src_ref=src,
            dst_ref=dst.at[slot],
            send_sem=send.at[other],
            recv_sem=recv.at[slot],
            device_id=(my_bin, other) if axis == "sky" else (other, my_sky),
            device_id_type=MESH,
        )

    def each(n, mine, act):
        def body(k, carry):
            act(lax.rem(mine + k, n))
            return carry

        lax.fori_loop(1, n, body, 0)

    each(sky, my_sky, lambda o: along("sky", mark_ref, marks_ref, send_m, recv_m, o, my_sky).start())
    each(count, me, lambda o: window_copy(o, me).start())
    own_mark = pltpu.make_async_copy(mark_ref, marks_ref.at[my_sky], own_sem.at[0])
    own_mark.start()
    own = pltpu.make_async_copy(src_of(x_ref, me), y_ref.at[me], own_sem.at[1])
    own.start()

    tall = tap_ref.shape[3]
    row_hi, row_lo, back_hi, back_lo = [], [], [], []
    narrow = round_up(rows + 2 * half + 1, 128)
    for s in range(scales):
        taps, turned = tap_ref[0, s], tap_ref[1, s]
        for at, part in enumerate(halves(band(turned[:, :width], width, width, half, width))):
            col_ref[at, s] = part
        for at, part in enumerate(
            halves(band(taps[:, :span], span, span, half + halo, part_width))
        ):
            adj_ref[at, s] = part
        a, b = halves(band(taps[:, :narrow], rows, narrow, half, rows))
        row_hi.append(a)
        row_lo.append(b)
        back = band(turned[:, :narrow], rows, narrow, half, rows)
        back_hi.append(back)
    row_hi = jnp.concatenate(row_hi, axis=0)
    row_lo = jnp.concatenate(row_lo, axis=0)
    back = halves(jnp.concatenate(back_hi, axis=1))
    diag = same_row(size)
    lanes = lax.broadcasted_iota(jnp.int32, (size, width), 1)
    owned = (lanes >= halo) & (lanes < halo + chunk)
    spot = lax.rem(lax.broadcasted_iota(jnp.int32, (bins, size), 1), XB)
    bin_row = lax.broadcasted_iota(jnp.int32, (bins, size), 0)

    pairs = fit_ref.shape[1]
    first = jnp.broadcast_to(pair_ref[:, 0:1], (pairs, size))
    second = jnp.broadcast_to(pair_ref[:, 1:2], (pairs, size))
    right_hot = lax.broadcasted_iota(jnp.int32, (pairs, size), 1) // XB == second
    weight = jnp.zeros((bins, size), F32)
    target = jnp.zeros((bins, size), F32)
    for i in range(bins):
        hot = right_hot & (first == i)
        weight_row = jnp.sum(jnp.where(hot, fit_ref[0], 0.0), axis=0, keepdims=True)
        target_row = jnp.sum(jnp.where(hot, fit_ref[1], 0.0), axis=0, keepdims=True)
        weight = jnp.where(bin_row == i, weight_row, weight)
        target = jnp.where(bin_row == i, target_row, target)
    sums_ref[...] = jnp.zeros_like(sums_ref)

    each(sky, my_sky, lambda o: along("sky", mark_ref, marks_ref, send_m, recv_m, o, o).wait())
    own_mark.wait()
    each(count, me, lambda o: window_copy(o, o).wait())
    own.wait()

    mark_width = mark_ref.shape[1]
    start = me * chunk - halo + 128
    marks = marks_ref[...].reshape(rows, mark_width)
    marks = pltpu.roll(marks, lax.rem(mark_width - start // 128, mark_width), 1)
    which = (lax.broadcasted_iota(jnp.int32, (rows, width), 1) + start) // 128 - start // 128
    mask = jnp.zeros((rows, width), F32)
    for t in range(tiles):
        mask = jnp.where(which == t, jnp.broadcast_to(marks[:, t : t + 1], (rows, width)), mask)
    masks = [
        jnp.concatenate([mask[g * XB : (g + 1) * XB]] * bins, axis=0) > 0 for g in range(groups)
    ]

    for b in range(bins):
        y = jnp.concatenate([y_ref[b * sky + k].astype(F32) for k in range(sky)], axis=0)
        y = y.astype(BF16)
        hi, lo = halves(mm(row_hi, y) + mm(row_lo, y))
        for s in range(scales):
            for g in range(groups):
                part = slice(s * rows + g * XB, s * rows + (g + 1) * XB)
                hi_ref[g, s, b * XB : (b + 1) * XB, :] = hi[part]
                lo_ref[g, s, b * XB : (b + 1) * XB, :] = lo[part]

    for g in range(groups):

        def forward(s, carry):
            matrix = (col_ref[0, s], col_ref[1, s])
            filtered = mm3((hi_ref[g, s], lo_ref[g, s]), matrix).astype(BF16).astype(F32)
            kept = jnp.where(masks[g], filtered, 0.0)
            g_ref[g, s] = kept.astype(BF16)
            left = jnp.where(owned, kept, 0.0).astype(BF16)
            for l in range(lags):
                right = kept if l == 0 else pltpu.roll(kept, width - l, 1)
                gram = lax.dot_general(
                    left, right.astype(BF16), (((1,), (1,)), ((), ())), preferred_element_type=F32
                )
                gram = jnp.sum((gram * diag).reshape(bins, XB, size), axis=1)
                sums_ref[s * lags + l] = sums_ref[s * lags + l] + gram
            return carry

        lax.fori_loop(0, scales, forward, 0)

    table = jnp.zeros((bins, size), F32)
    for at in range(scales * lags):
        value = sums_ref[at]
        for step in (16, 8, 4, 2, 1):
            value = value + pltpu.roll(value, size - step, 1)
        if at:
            value = pltpu.roll(value, at, 1)
        table = jnp.where(spot == at, value, table)

    part_ref[...] = table
    each(sky, my_sky, lambda o: along("sky", part_ref, sky_ref, send_s, recv_s, o, my_sky).start())
    sky_ref[pl.ds(my_sky, 1)] = table[None]
    each(sky, my_sky, lambda o: along("sky", part_ref, sky_ref, send_s, recv_s, o, o).wait())
    table = sky_ref[0]
    for k in range(1, sky):
        table = table + sky_ref[k]
    bin_in_ref[...] = table
    each(bins, my_bin, lambda o: along("bin", bin_in_ref, bin_ref, send_b, recv_b, o, my_bin).start())
    bin_ref[pl.ds(my_bin, 1)] = table[None]
    each(bins, my_bin, lambda o: along("bin", bin_in_ref, bin_ref, send_b, recv_b, o, o).wait())
    table = bin_ref[0]
    for k in range(1, bins):
        table = table + bin_ref[k]
    table = table * area

    picked = jnp.zeros((pairs, size), F32)
    for i in range(bins):
        picked = jnp.where(first == i, jnp.broadcast_to(table[i : i + 1], (pairs, size)), picked)
    picked = jnp.where(right_hot, picked, 0.0)
    step = size // 2
    while step >= XB:
        picked = picked + pltpu.roll(picked, step, 1)
        step //= 2
    corr_ref[...] = picked

    ahead = jnp.where(spot < scales * lags, weight * (table - target), 0.0)
    spread = jnp.broadcast_to(ahead[:, None, :], (bins, XB, size)).reshape(size, size)
    behind = jnp.sum(jnp.transpose(spread * diag).reshape(bins, XB, size), axis=1)

    def coefficient(values, at):
        value = jnp.where(spot == at, values, 0.0)
        value = pltpu.roll(value, lax.rem(size - at, size), 1)
        for step in (1, 2, 4, 8, 16):
            value = value + pltpu.roll(value, step, 1)
        return value

    def grad_copy(piece, other, slot):
        return pltpu.make_async_remote_copy(
            src_ref=grad_ref.at[piece, other],
            dst_ref=dst_of(result_ref, slot, piece),
            send_sem=send_g.at[piece, other],
            recv_sem=recv_g.at[piece, slot],
            device_id=(other // sky, lax.rem(other, sky)),
            device_id_type=MESH,
        )

    own_grads = []
    for piece in range(pieces):
        cut = slice(piece * part_width, piece * part_width + span)
        for g in range(groups):

            def backward(s, carry):
                maps = g_ref[g, s, :, cut].astype(F32)
                total_grad = jnp.zeros((size, span), F32)
                for shift in range(1 - lags, lags):
                    moved = maps if shift == 0 else pltpu.roll(maps, (span - shift) % span, 1)
                    moved = moved.astype(BF16)
                    at = s * (2 * lags - 1) + shift + lags - 1
                    if piece == 0:
                        if shift == 0:
                            coef = coefficient(ahead + behind, s * lags)
                        elif shift > 0:
                            coef = coefficient(ahead, s * lags + shift)
                        else:
                            coef = coefficient(behind, s * lags - shift)
                        if pieces > 1 or groups > 1:
                            coef_ref[at] = coef
                    else:
                        coef = coef_ref[at]
                    full = jnp.broadcast_to(coef[:, None, :], (bins, XB, size))
                    hi, lo = halves(full.reshape(size, size) * diag)
                    total_grad = total_grad + mm(hi, moved) + mm(lo, moved)
                total_grad = jnp.where(masks[g][:, cut], total_grad, 0.0)
                hi, lo = halves(mm3(halves(total_grad), (adj_ref[0, s], adj_ref[1, s])))
                hi_ref[g, s, :, :part_width] = hi
                lo_ref[g, s, :, :part_width] = lo
                return carry

            lax.fori_loop(0, scales, backward, 0)

        for b in range(bins):
            spots = [(g, s) for s in range(scales) for g in range(groups)]
            rows_of = slice(b * XB, (b + 1) * XB)
            hi = jnp.concatenate([hi_ref[g, s, rows_of, :part_width] for g, s in spots], axis=0)
            lo = jnp.concatenate([lo_ref[g, s, rows_of, :part_width] for g, s in spots], axis=0)
            total_rows = mm3(back, (hi, lo))
            for k in range(sky):
                at = b * sky + k
                grad_ref[piece, at] = total_rows[k * strip_rows : (k + 1) * strip_rows]

        each(count, me, lambda o: grad_copy(piece, o, me).start())
        own_grad = pltpu.make_async_copy(
            grad_ref.at[piece, me], dst_of(result_ref, me, piece), own_sem.at[2 + piece]
        )
        own_grad.start()
        own_grads.append(own_grad)
    for piece in range(pieces):
        each(count, me, lambda o: grad_copy(piece, o, o).wait())
        own_grads[piece].wait()


def per_device(lensing_maps, filter_taps, survey_mask, bin_pairs, target_corr, pair_weight):
    scales, tap_count = filter_taps.shape
    half = (tap_count - 1) // 2
    strip = lensing_maps[0]
    strip_rows, cols = strip.shape
    bins, sky = lax.axis_size("bin"), lax.axis_size("sky")
    count = bins * sky
    pairs, lags = pair_weight.shape[0], pair_weight.shape[2]
    row_count = strip_rows * sky
    groups = row_count // XB
    chunk = cols // count
    width = round_up(chunk + 2 * (2 * half + lags - 1), 128)
    halo = (width - chunk) // 2
    out_width = round_up(chunk, 128)
    tiles = width // 128 + 1
    size = bins * XB
    aligned = chunk % 128 == 0
    pieces = out_width // 128
    part_width = out_width // pieces
    span = width - (pieces - 1) * part_width

    windows = jnp.pad(strip, ((0, 0), (halo, halo)))
    if not aligned:
        windows = jnp.stack([windows[:, d * chunk : d * chunk + width] for d in range(count)])
    mark_width = round_up(survey_mask.shape[1] + 1 + tiles, 128)
    marks = jnp.pad(
        survey_mask.astype(F32), ((0, 0), (1, mark_width - survey_mask.shape[1] - 1))
    )
    marks = jnp.broadcast_to(marks, (strip_rows, mark_width))
    tall = max(width, round_up(row_count + 2 * half + 1, 128))
    taps = jnp.stack([filter_taps, filter_taps[:, ::-1]])
    taps = jnp.pad(taps, ((0, 0), (0, 0), (0, tall - tap_count)))[:, :, None, :]
    fit = jnp.stack([pair_weight, target_corr]).reshape(2, pairs, scales * lags)
    fit = jnp.tile(jnp.pad(fit, ((0, 0), (0, 0), (0, XB - scales * lags))), (1, 1, bins))

    if aligned:
        src_of = lambda ref, d: ref.at[:, pl.ds(pl.multiple_of(d * chunk, 128), width)]
        dst_of = lambda ref, d, p: ref.at[
            :, pl.ds(pl.multiple_of(d * chunk + p * part_width, 128), part_width)
        ]
        result_shape = (strip_rows, cols)
    else:
        src_of = lambda ref, d: ref.at[d]
        dst_of = lambda ref, d, p: ref.at[d]
        result_shape = (count, strip_rows, out_width)

    spec = pl.BlockSpec(memory_space=pltpu.VMEM)
    table_shape = (bins, size)
    dma = pltpu.SemaphoreType.DMA
    result, corr = pl.pallas_call(
        functools.partial(
            step_kernel, bins, sky, scales, lags, groups, chunk, halo, tiles, half,
            1.0 / (row_count * cols), src_of, dst_of,
        ),
        out_shape=(
            jax.ShapeDtypeStruct(result_shape, F32),
            jax.ShapeDtypeStruct((pairs, size), F32),
        ),
        in_specs=[spec] * 5,
        out_specs=(spec, spec),
        scratch_shapes=[
            pltpu.VMEM((count, strip_rows, width), BF16),
            pltpu.VMEM((sky, strip_rows, mark_width), F32),
            pltpu.VMEM((groups, scales, size, width), BF16),
            pltpu.VMEM((groups, scales, size, width), BF16),
            pltpu.VMEM((groups, scales, size, width), BF16),
            pltpu.VMEM((scales * lags,) + table_shape, F32),
            pltpu.VMEM((pieces, count, strip_rows, part_width), F32),
            pltpu.VMEM((2, scales, width, width), BF16),
            pltpu.VMEM((2, scales, span, part_width), BF16),
            pltpu.VMEM(table_shape, F32),
            pltpu.VMEM((sky,) + table_shape, F32),
            pltpu.VMEM(table_shape, F32),
            pltpu.VMEM((bins,) + table_shape, F32),
            dma((count,)), dma((count,)), dma((sky,)), dma((sky,)), dma((sky,)), dma((sky,)),
            dma((bins,)), dma((bins,)), dma((pieces, count)), dma((pieces, count)), dma((2 + pieces,)),
            pltpu.VMEM((scales * (2 * lags - 1),) + table_shape, F32),
        ],
        compiler_params=pltpu.CompilerParams(
            collective_id=1, has_side_effects=True, vmem_limit_bytes=VMEM_LIMIT
        ),
    )(windows, marks, taps, bin_pairs, fit)
    if not aligned:
        result = jnp.transpose(result[:, :, :chunk], (1, 0, 2)).reshape(strip_rows, cols)
    corr_table = corr[:, : scales * lags].reshape(pairs, scales, lags)
    return (corr_table, result[None])


def tables(bins, scales, lags):
    lane = lax.broadcasted_iota(jnp.int32, (bins, 128), 1)
    high, low = lane // 64, (lane // 8) % 2
    return lane, high, low, 2 * high + low


EARLY = 2


def spot_of(scale):
    return (0, scale) if scale < EARLY else (1, scale - EARLY)


def slot_rows(scale, lag):
    slot = spot_of(scale)[1]
    return 64 * (slot // 2) + 16 * lag + 8 * (slot % 2)


def thirds(value):
    hi = value.astype(BF16)
    rest = value - hi.astype(F32)
    mid = rest.astype(BF16)
    lo = (rest - mid.astype(F32)).astype(BF16)
    return hi, mid, lo


def nt(a, b):
    return lax.dot_general(a, b, (((1,), (1,)), ((), ())), preferred_element_type=F32)


def steps(begin, end, body, carry):
    for s in range(begin, end):
        carry = body(s, carry)
    return carry


def fast_kernel(
    bins, sky, scales, lags, chunk, half, area,
    x_hbm, tap_hbm, mask_hbm, pair_hbm, target_hbm, weight_hbm,
    result_ref, corr_ref,
    x_ref, tap_ref, mask_ref, pair_ref, target_ref, weight_ref,
    pad_ref, wide_ref, y_ref, cols_ref, mark_ref, marks_ref, mask_v_ref, mask_w_ref,
    row_hi_ref, row_lo_ref, back_hi_ref, back_lo_ref, fwd_ref, adj_ref,
    small_ref, fit_ref, pairs_ref, table_ref,
    g_ref, moved_ref, coef_ref, t_ref, cg_hi_ref, cg_lo_ref, out_ref, grad_ref, land_ref,
    part_ref, twin_ref, parts_ref,
    send_x, recv_x, recv_w, send_y, recv_y, send_m, recv_m, send_c, recv_c, send_t, recv_t, send_g, recv_g, in_sem,
):
    count = bins * sky
    cols = x_ref.shape[1]
    width = y_ref.shape[2]
    halo = (width - chunk) // 2
    pairs = pair_ref.shape[1]
    taps_n = tap_ref.shape[1]
    size = bins * XB
    groups = size // 32
    vregs = part_ref.shape[0]
    my_bin, my_sky = lax.axis_index("bin"), lax.axis_index("sky")
    me = place(bins, sky)

    barrier = pltpu.get_barrier_semaphore()

    bits = count.bit_length() - 1
    flips = [(1 - 2 * lax.rem(me // 2**i, 2)) * 2**i for i in range(bits)]

    def flipped(mask):
        other = me
        for i in range(bits):
            if (mask >> i) & 1:
                other = other + flips[i]
        return other

    def arrived(ref, sem):
        pltpu.make_async_copy(ref, ref, sem).wait()

    chips = count // 2
    far_first = range(chips - 1, 0, -1)

    def hello(other):
        pl.semaphore_signal(
            barrier, inc=1, device_id=(other // sky, lax.rem(other, sky)), device_id_type=MESH
        )

    hello(me + flips[0])
    for k in far_first:
        hello(flipped(2 * k))
    loads = [
        pltpu.make_async_copy(src, dst, in_sem.at[i])
        for i, (src, dst) in enumerate(
            (
                (x_hbm, x_ref), (mask_hbm, mask_ref), (tap_hbm, tap_ref),
                (pair_hbm, pair_ref), (target_hbm, target_ref), (weight_hbm, weight_ref),
            )
        )
    ]
    for load in loads:
        load.start()

    chip, core = me // 2, lax.rem(me, 2)
    twin = me + flips[0]
    wide = 2 * chunk + 2 * halo

    def remote(src, dst, send, recv, other):
        return pltpu.make_async_remote_copy(
            src_ref=src,
            dst_ref=dst,
            send_sem=send,
            recv_sem=recv,
            device_id=(other // sky, lax.rem(other, sky)),
            device_id_type=MESH,
        )

    def window_copy(k):
        other = flipped(2 * k)
        at = (1 - core) * chunk
        src = pad_ref.at[:, pl.ds(pl.multiple_of((other // 2) * 2 * chunk + at, 128), width)]
        dst = wide_ref.at[k, :, pl.ds(pl.multiple_of(at, 128), width)]
        return remote(src, dst, send_x.at[0], recv_x.at[k], other)

    def rest_copy(k):
        other = flipped(2 * k)
        at = core * width
        src = pad_ref.at[:, pl.ds(pl.multiple_of((other // 2) * 2 * chunk + at, 128), wide - width)]
        dst = wide_ref.at[k, :, pl.ds(pl.multiple_of(at, 128), wide - width)]
        return remote(src, dst, send_x.at[0], recv_w.at[k // 4], other)

    def twin_copy(k):
        src = wide_ref.at[k, :, pl.ds(pl.multiple_of((1 - core) * chunk, 128), width)]
        return remote(src, y_ref.at[k], send_y.at[0], recv_y.at[k // 4], twin)

    beside = me + flips[1]

    def mark_copy(n, slot, to):
        src = mark_ref if n < 2 else marks_ref.at[slot]
        return remote(src, marks_ref.at[slot], send_m.at[n], recv_m.at[n], to)

    loads[0].wait()
    loads[1].wait()
    moved_x = pltpu.roll(x_ref[...].astype(F32), halo, 1)
    edge = lax.broadcasted_iota(jnp.int32, (moved_x.shape[0], 128), 1) < halo
    pad_ref[:, :128] = jnp.where(edge, 0.0, moved_x[:, :128]).astype(BF16)
    pad_ref[:, 128:cols] = moved_x[:, 128:].astype(BF16)
    pad_ref[:, cols:] = jnp.where(edge, moved_x[:, :128], 0.0).astype(BF16)
    mark_ref[...] = jnp.zeros_like(mark_ref)
    mark_ref[:, : mask_ref.shape[1]] = jnp.broadcast_to(
        mask_ref[...].astype(F32), (mark_ref.shape[0], mask_ref.shape[1])
    )

    pl.semaphore_wait(barrier, count // 2)
    for k in far_first:
        window_copy(k).start()
    for k in far_first:
        rest_copy(k).start()
    mark_copy(0, my_sky, twin).start()
    mark_copy(1, my_sky, beside).start()
    at = pl.multiple_of(chip * 2 * chunk, 128)
    wide_ref[0] = pad_ref[:, pl.ds(at, wide)]
    twin_copy(0).start()
    marks_ref[pl.ds(my_sky, 1)] = mark_ref[...][None]

    for load in loads[2:]:
        load.wait()
    small_ref[...] = jnp.zeros_like(small_ref)
    small_ref[:scales, :taps_n] = tap_ref[...]
    tap_hi, tap_lo = halves(small_ref[...])
    tap_row = lax.broadcasted_iota(jnp.int32, (128, 256), 0)
    tap_col = lax.broadcasted_iota(jnp.int32, (128, 256), 1)
    real = tap_row < taps_n

    def spread(hot):
        hot = (hot & real).astype(F32).astype(BF16)
        return mm(tap_hi, hot) + mm(tap_lo, hot)

    straight = spread(tap_col == tap_row)
    turned = spread(tap_col == taps_n - 1 - tap_row)
    spaced = spread(tap_col == bins * (taps_n - 1 - tap_row))
    sub = lax.broadcasted_iota(jnp.int32, (bins, size), 0)
    col = lax.broadcasted_iota(jnp.int32, (bins, size), 1)
    turns = [pltpu.roll(straight, (XB * b - half) % size, 1) for b in range(bins)]
    for s in range(scales):
        reach = halo + half
        hi, lo = halves(band(turned[s : s + 1], 256, 256, reach, 128))
        fwd_ref[s, :, :128] = hi
        fwd_ref[s, :, 128:] = lo
        first = jnp.zeros((bins, size), F32)
        for b in range(bins):
            first = jnp.where(sub == b, jnp.broadcast_to(turns[b][s : s + 1], (bins, size)), first)
        tiles = [
            jnp.where(col // XB == sub, first if x == 0 else pltpu.roll(first, x, 1), 0.0)
            for x in range(XB)
        ]
        hi, lo = halves(jnp.concatenate(tiles, axis=0))
        row_hi_ref[s] = hi
        row_lo_ref[s] = lo

    lane, high, low, slot = tables(bins, scales, lags)
    pairs_ref[...] = jnp.full_like(pairs_ref, -1)
    pairs_ref[:2, :pairs] = pair_ref[...]
    fit_ref[...] = jnp.zeros_like(fit_ref)
    for s in range(scales):
        fit_ref[0, s, :lags, :pairs] = weight_ref[s]
        fit_ref[1, s, :lags, :pairs] = target_ref[s]
    bin_of = lax.broadcasted_iota(jnp.int32, (bins, 128), 0)
    first_hot = (pairs_ref[0:1, :] == bin_of).astype(F32)
    second_hot = pairs_ref[1:2, :] == bin_of
    first_hot16 = first_hot.astype(BF16)
    far = lax.rem(beside, sky)
    mark_copy(1, far, beside).wait()
    mark_copy(2, far, twin).start()
    mark_copy(0, lax.rem(twin, sky), twin).wait()
    mark_copy(2, lax.rem(beside + flips[0], sky), twin).wait()
    for k in range(sky):
        marks = pltpu.roll(marks_ref[k], 1, 1)
        marks = pltpu.roll(marks, lax.rem(128 - 2 * me, 128), 1)
        left, one, two, right = [jnp.broadcast_to(marks[:, t : t + 1], (8, 128)) for t in range(4)]
        lanes = lax.broadcasted_iota(jnp.int32, (8, 128), 1)
        mask_v_ref[k, :, :128] = one
        mask_v_ref[k, :, 128:256] = two
        mask_v_ref[k, :, 256:] = jnp.where(lanes < 64, right, left)
        mask_w_ref[k, :, :128] = jnp.where(lanes < 64, left, one)
        mask_w_ref[k, :, 128:256] = jnp.where(lanes < 64, one, two)
        mask_w_ref[k, :, 256:] = jnp.where(lanes < 64, two, right)

    def masked(value, ref):
        tall = size // sky
        return jnp.concatenate(
            [value[k * tall : (k + 1) * tall] * jnp.broadcast_to(ref[k, 0:1, :], (tall, width)) for k in range(sky)],
            axis=0,
        )

    def stacked(v):
        return jnp.concatenate(
            [v[:, :256], v[:, 128:], jnp.concatenate([v[:, 256:], v[:, :128]], axis=1)], axis=0
        )

    mine = pl.multiple_of(core * chunk, 128)

    def pass_on(layer):
        for k in range(4 * layer, 4 * layer + 4):
            if k:
                window_copy(k).wait_recv()
                twin_copy(k).start()

    def columns(layer):
        arrived(wide_ref.at[max(4 * layer, 1) : 4 * layer + 4, :, : wide - width], recv_w.at[layer])
        arrived(y_ref.at[4 * layer : 4 * layer + 4], recv_y.at[layer])
        first = (flipped(8 * layer) // 8) * 4
        rows = []
        for c in range(4):
            slot = 4 * layer + lax.rem(chip + c % 2, 2) + 2 * lax.rem(chip // 2 + c // 2, 2)
            direct = wide_ref[pl.ds(slot, 1), :, pl.ds(mine, width)][0].astype(F32)
            passed = y_ref[pl.ds(slot, 1)][0].astype(F32)
            rows.append(jnp.where(core == 0, direct, passed))
            rows.append(jnp.where(core == 1, direct, passed))
        y = stacked(jnp.concatenate(rows, axis=0).astype(BF16))
        tall = 2 * XB
        at = pl.multiple_of(first * 16, tall)
        for s in range(scales):
            p = mm(y, fwd_ref[s])
            f = p[:, :128] + p[:, 128:]
            hi, lo = halves(jnp.concatenate([f[:tall], f[tall : 2 * tall], f[2 * tall :]], axis=1))
            cols_ref[s, pl.ds(at, tall), :width] = hi
            cols_ref[s, pl.ds(at, tall), width:] = lo

    layers = count // 8
    pass_on(0)
    for layer in range(layers):
        if layer + 1 < layers:
            pass_on(layer + 1)
        columns(layer)

    def forward(s, carry):
        p = mm(row_hi_ref[s], cols_ref[s])
        q = mm(row_lo_ref[s], cols_ref[s, :, :width])
        f = p[:, :width] + p[:, width:] + q
        kept16 = masked(f, mask_v_ref).astype(BF16)
        g_ref[s] = kept16
        shifted = [kept16[:, l : l + chunk] for l in range(lags)]
        total = jnp.zeros((32, 128), F32)
        for g in range(groups):
            right = jnp.concatenate(
                [shifted[l][g * 32 + 16 * h : g * 32 + 16 * h + 16] for h in range(2) for l in range(lags)],
                axis=0,
            )
            total = total + nt(kept16[g * 32 : (g + 1) * 32, :chunk], right)
        z = jnp.zeros((bins, 128), F32)
        for x in range(4):
            z = jnp.where(slot == x, total[bins * x : bins * (x + 1)], z)
        z = z + pltpu.roll(z, 64, 1)
        z = z + jnp.where(low == 0, pltpu.roll(z, 120, 1), pltpu.roll(z, 8, 1))
        into = s if s < EARLY else s - EARLY
        return jnp.where(slot == into, z, carry)

    def core_copy(v):
        return pltpu.make_async_remote_copy(
            src_ref=part_ref.at[v],
            dst_ref=twin_ref.at[v],
            send_sem=send_c.at[v],
            recv_sem=recv_c.at[v],
            device_id=((me + flips[0]) // sky, lax.rem(me + flips[0], sky)),
            device_id_type=MESH,
        )

    def send_tables(v):
        core_copy(v).wait()
        parts_ref[v, 0] = part_ref[v] + twin_ref[v]
        for k in far_first:
            remote(parts_ref.at[v, 0], parts_ref.at[v, k], send_t.at[v], recv_t.at[v], flipped(2 * k)).start()

    zero = jnp.zeros((bins, 128), F32)
    part_ref[0] = steps(0, EARLY, forward, zero)
    core_copy(0).start()
    late = steps(EARLY, EARLY + 1, forward, zero)
    send_tables(0)
    part_ref[1] = steps(EARLY + 1, scales, forward, late)
    core_copy(1).start()

    def lagging(s, carry):
        kept = g_ref[s]
        for at in range(2 * lags - 1):
            cut = width - halo + (at - lags + 1)
            turn = jnp.concatenate([kept[:, cut:], kept[:, :cut]], axis=1)
            for g in range(groups):
                side = (g % 2) * width
                moved_ref[s, g // 2, at * 32 : (at + 1) * 32, side : side + width] = turn[g * 32 : (g + 1) * 32]
        return carry

    steps(0, 1, lagging, 0)
    send_tables(1)
    steps(1, scales, lagging, 0)

    for s in range(scales):
        hi, lo = halves(band(straight[s : s + 1], 256, 256, reach, 128))
        adj_ref[s, :, :128] = hi
        adj_ref[s, :, 128:] = lo
        first = pltpu.roll(
            jnp.broadcast_to(spaced[s : s + 1], (8, size)), 0, 1, stride=bins, stride_axis=0
        )
        tiles = []
        for b in range(bins):
            for k in range(XB // 8):
                shift = (bins * 8 * k - bins * half + b) % size
                apart = col // bins - sub - 8 * k
                near = (apart <= half) & (apart >= -half)
                tiles.append(jnp.where(near, first if shift == 0 else pltpu.roll(first, shift, 1), 0.0))
        hi, lo = halves(jnp.concatenate(tiles, axis=0))
        back_hi_ref[:, s * size : (s + 1) * size] = hi
        back_lo_ref[:, s * size : (s + 1) * size] = lo
    for at in range(2):
        for v in range(vregs):
            tiles = []
            for tile in range(16):
                at_slot, l = 2 * (tile // 8) + tile % 2, (tile // 2) % 4
                s = at_slot + v * EARLY
                if s < scales and spot_of(s) == (v, at_slot):
                    row = jnp.broadcast_to(fit_ref[at, s, l : l + 1, :], (bins, 128))
                    tiles.append(jnp.where(second_hot, row, 0.0))
                else:
                    tiles.append(jnp.zeros((bins, 128), F32))
            parts = thirds(jnp.concatenate(tiles, axis=0))
            table_ref[at, v] = nt(first_hot16, parts[0]) + nt(first_hot16, parts[1]) + nt(first_hot16, parts[2])


    e_row = lax.broadcasted_iota(jnp.int32, (128, 256), 0)
    e_col = lax.broadcasted_iota(jnp.int32, (128, 256), 1)
    place_hot = (e_row % 16 < 8) & (e_row // 16 == e_col // 32 - (lags - 1)) & (e_row % 8 == e_col % 8)
    place_hot = (place_hot & (e_row < 16 * lags)).astype(F32).astype(BF16)

    def coefficients(v, begin, end):
        arrived(parts_ref.at[v, 1:], recv_t.at[v])
        tables = [parts_ref[v, k] for k in range(chips)]
        while len(tables) > 1:
            tables = [tables[k] + tables[k + 1] for k in range(0, len(tables), 2)]
        total = tables[0] * area
        ahead = table_ref[0, v] * (total - table_ref[1, v])
        over = jnp.transpose(jnp.concatenate([ahead] * 16, axis=0))
        rows = []
        for s in range(begin, end):
            back = (128 - slot_rows(s, 0)) % 128
            value = ahead if back == 0 else pltpu.roll(ahead, back, 1)
            hi = value.astype(BF16).astype(F32)
            rows += [hi, value - hi]
        ahead_rows = mm(jnp.concatenate(rows, axis=0).astype(BF16), place_hot)
        for s in range(begin, end):
            behind = jnp.zeros((bins, 128), F32)
            for l in range(lags):
                at = slot_rows(s, l)
                behind = jnp.where(lane // 32 == lags - 1 - l, over[at : at + 8], behind)
            hi = behind.astype(BF16).astype(F32)
            tiles = []
            for at, value in ((0, hi), (1, behind - hi)):
                row = (2 * (s - begin) + at) * 8
                z = ahead_rows[row : row + 8]
                value = value.astype(BF16).astype(F32)
                for x in range(4):
                    near = (lane // 8) % 4 == x
                    tiles.append(
                        jnp.concatenate(
                            [jnp.where(near, z[:, :128] + value, 0.0), jnp.where(near, z[:, 128:], 0.0)], axis=1
                        )
                    )
            coef_ref[s] = jnp.concatenate(tiles, axis=0).astype(BF16)
        return total

    def backward(s, carry):
        coef = coef_ref[s][:, : 32 * (2 * lags - 1)]
        for g in range(0, groups, 2):
            t = mm(coef, moved_ref[s, g // 2])
            t = t[:32] + t[32:]
            t_ref[g * 32 : (g + 1) * 32, :] = t[:, :width]
            t_ref[(g + 1) * 32 : (g + 2) * 32, :] = t[:, width:]
        hi, lo = halves(masked(t_ref[...], mask_w_ref))
        p = mm(jnp.concatenate([hi[:, :256], hi[:, 128:]], axis=0), adj_ref[s])
        q = mm(jnp.concatenate([lo[:, :256], lo[:, 128:]], axis=0), adj_ref[s, :, :128])
        c = p[:, :128] + p[:, 128:] + q
        hi, lo = halves(jnp.concatenate([c[:size], c[size:]], axis=1))
        cg_hi_ref[s] = hi
        cg_lo_ref[s] = lo
        return carry

    totals = []
    for v, (begin, end) in enumerate(((0, EARLY), (EARLY, scales))):
        totals.append(coefficients(v, begin, end))
        steps(begin, end, backward, 0)
        deep = (end - begin) * size
        cg_hi = cg_hi_ref[begin:end].reshape(deep, chunk)
        cg_lo = cg_lo_ref[begin:end].reshape(deep, chunk)
        part = slice(begin * size, end * size)
        out = mm3((back_hi_ref[:, part], back_lo_ref[:, part]), (cg_hi, cg_lo))
        if v == 0:
            out_ref[...] = out
    out = out_ref[...] + out

    for k in range(count):
        block = out[8 * k : 8 * k + 8]
        largest = jnp.max(jnp.abs(block), axis=0, keepdims=True)
        largest = jnp.broadcast_to(jnp.max(largest, axis=1, keepdims=True), (8, 128))
        power = jnp.maximum(jnp.ceil(jnp.log2(jnp.maximum(largest, 1e-30)) + 0.001), -90.0)
        scale = jnp.exp2(15.0 - power) * (32766.0 / 32768.0)
        left = jnp.round(block[:, :128] * scale).astype(jnp.int32)
        right = jnp.round(block[:, 128:] * scale).astype(jnp.int32)
        grad_ref[k, :8] = left * 65536 + (right + 32768)
        grad_ref[k, 8:] = power[:1].astype(jnp.int32)

    for k in range(count - 1, 0, -1):
        other = flipped(k)
        remote(grad_ref.at[other], land_ref.at[k], send_g.at[0], recv_g.at[k // 8], other).start()
    land_ref[0] = grad_ref[pl.ds(me, 1)][0]

    hot = jnp.concatenate([first_hot16, jnp.zeros((128 - bins, 128), BF16)], axis=0)
    for v in range(vregs):
        parts = thirds(jnp.transpose(jnp.concatenate([totals[v]] * 16, axis=0)))
        picked = mm(parts[0], hot) + mm(parts[1], hot) + mm(parts[2], hot)
        for s in [s for s in range(scales) if spot_of(s)[0] == v]:
            for l in range(lags):
                at = slot_rows(s, l)
                value = jnp.sum(jnp.where(second_hot, picked[at : at + 8], 0.0), axis=0, keepdims=True)
                corr_ref[s, l : l + 1, :] = value[:, :pairs]

    for layer in range(count // 8):
        arrived(land_ref.at[max(8 * layer, 1) : 8 * layer + 8], recv_g.at[layer])
        for k in range(8 * layer, 8 * layer + 8):
            word = land_ref[k, :8]
            power = jnp.broadcast_to(land_ref[k, 8:], (8, 128)).astype(F32)
            scale = jnp.exp2(power - 15.0) * (32768.0 / 32766.0)
            at = pl.multiple_of(flipped(k) * chunk, 128)
            result_ref[:, pl.ds(at, 128)] = (word >> 16).astype(F32) * scale
            result_ref[:, pl.ds(at + 128, 128)] = ((word & 65535) - 32768).astype(F32) * scale

    arrived(wide_ref.at[1:], send_x.at[0])
    arrived(y_ref, send_y.at[0])
    for v in range(vregs):
        arrived(parts_ref.at[v, 1:], send_t.at[v])
    arrived(land_ref.at[1:], send_g.at[0])


def fast_device(lensing_maps, filter_taps, survey_mask, bin_pairs, target_corr, pair_weight):
    scales, tap_count = filter_taps.shape
    half = (tap_count - 1) // 2
    strip = lensing_maps[0]
    strip_rows, cols = strip.shape
    bins, sky = lax.axis_size("bin"), lax.axis_size("sky")
    count = bins * sky
    pairs, lags = pair_weight.shape[0], pair_weight.shape[2]
    chunk = cols // count
    width = chunk + 128
    size = bins * XB
    groups = size // 32
    vregs = 2
    spec = pl.BlockSpec(memory_space=pltpu.VMEM)
    dma = pltpu.SemaphoreType.DMA
    table = (vregs, bins, 128)
    result, corr = pl.pallas_call(
        functools.partial(fast_kernel, bins, sky, scales, lags, chunk, half, 1.0 / (strip_rows * sky * cols)),
        out_shape=(
            pltpu.VMEM((strip_rows, cols), F32),
            pltpu.VMEM((scales, lags, pairs), F32),
        ),
        in_specs=[pl.BlockSpec(memory_space=pl.ANY)] * 6,
        out_specs=(spec, spec),
        scratch_shapes=[
            pltpu.VMEM((strip_rows, cols), BF16),
            pltpu.VMEM(filter_taps.shape, F32),
            pltpu.VMEM(survey_mask.shape, jnp.int32),
            pltpu.VMEM((2, pairs), jnp.int32),
            pltpu.VMEM((scales, lags, pairs), F32),
            pltpu.VMEM((scales, lags, pairs), F32),
            pltpu.VMEM((strip_rows, cols + 128), BF16),
            pltpu.VMEM((count // 2, strip_rows, 2 * chunk + 128), BF16),
            pltpu.VMEM((count // 2, strip_rows, width), BF16),
            pltpu.VMEM((scales, size, 2 * width), BF16),
            pltpu.VMEM((8, 128), F32),
            pltpu.VMEM((sky, 8, 128), F32),
            pltpu.VMEM((sky, 8, width), F32),
            pltpu.VMEM((sky, 8, width), F32),
            pltpu.VMEM((scales, size, size), BF16),
            pltpu.VMEM((scales, size, size), BF16),
            pltpu.VMEM((size, scales * size), BF16),
            pltpu.VMEM((size, scales * size), BF16),
            pltpu.VMEM((scales, 256, 256), BF16),
            pltpu.VMEM((scales, 256, 256), BF16),
            pltpu.VMEM((8, 128), F32),
            pltpu.VMEM((2, scales, 8, 128), F32),
            pltpu.VMEM((8, 128), jnp.int32),
            pltpu.VMEM((2,) + table, F32),
            pltpu.VMEM((scales, size, width), BF16),
            pltpu.VMEM((scales, groups // 2, 32 * (2 * lags - 1), 2 * width), BF16),
            pltpu.VMEM((scales, 64, 256), BF16),
            pltpu.VMEM((size, width), F32),
            pltpu.VMEM((scales, size, chunk), BF16),
            pltpu.VMEM((scales, size, chunk), BF16),
            pltpu.VMEM((size, chunk), F32),
            pltpu.VMEM((count, strip_rows + 1, 128), jnp.int32),
            pltpu.VMEM((count, strip_rows + 1, 128), jnp.int32),
            pltpu.VMEM(table, F32),
            pltpu.VMEM(table, F32),
            pltpu.VMEM((vregs, count // 2, bins, 128), F32),
            dma((1,)), dma((count // 2,)), dma((count // 8,)), dma((1,)), dma((count // 8,)), dma((3,)), dma((3,)),
            dma((vregs,)), dma((vregs,)), dma((vregs,)), dma((vregs,)),
            dma((1,)), dma((count // 8,)), dma((6,)),
        ],
        compiler_params=pltpu.CompilerParams(
            collective_id=1, has_side_effects=True, vmem_limit_bytes=VMEM_LIMIT
        ),
    )(
        strip,
        filter_taps,
        survey_mask,
        bin_pairs.T,
        jnp.transpose(target_corr, (1, 2, 0)),
        jnp.transpose(pair_weight, (1, 2, 0)),
    )
    return (jnp.transpose(corr, (2, 0, 1)), result[None])


def fits(mesh, maps, taps, survey_mask, weight):
    bins, sky = mesh.shape["bin"], mesh.shape["sky"]
    rows, cols = maps.shape[1:]
    return (
        maps.shape[0] == bins == 8
        and rows == XB == 8 * sky
        and cols == 256 * bins * sky
        and survey_mask.shape == (sky, cols // 128)
        and EARLY < taps.shape[0] <= 6
        and taps.shape[1] == 17
        and weight.shape[0] <= 128
        and weight.shape[2] == 4
    )


def solution(mesh):
    placed = (P("bin", "sky", None), P(), P("sky", None), P(), P(), P())

    def step(lensing_maps, filter_taps, survey_mask, bin_pairs, target_corr, pair_weight):
        fast = fits(mesh, lensing_maps, filter_taps, survey_mask, pair_weight)
        return jax.shard_map(
            fast_device if fast else per_device,
            mesh=mesh,
            in_specs=placed,
            out_specs=(P(), P("bin", "sky", None)),
            check_vma=False,
        )(lensing_maps, filter_taps, survey_mask, bin_pairs, target_corr, pair_weight)

    return step
```

```python
import functools

import jax
import jax.numpy as jnp
from jax import lax
from jax.experimental import pallas as pl
from jax.experimental.pallas import tpu as pltpu
from jax.sharding import PartitionSpec as P

F32 = jnp.float32
BF16 = jnp.bfloat16
XB = 32
MESH = pl.DeviceIdType.MESH
VMEM_LIMIT = 60 * 1024 * 1024


def round_up(n, m):
    return -(-n // m) * m


def halves(value):
    hi = value.astype(BF16)
    lo = (value - hi.astype(F32)).astype(BF16)
    return hi, lo


def mm(a, b):
    return jnp.dot(a, b, preferred_element_type=F32)


def mm3(a, b):
    return mm(a[0], b[0]) + mm(a[0], b[1]) + mm(a[1], b[0])


def place(bins, sky):
    return lax.axis_index("bin") * sky + lax.axis_index("sky")


def greet(me, bins, sky):
    count = bins * sky
    barrier = pltpu.get_barrier_semaphore()

    def hello(k, carry):
        other = lax.rem(me + k, count)
        pl.semaphore_signal(
            barrier, inc=1, device_id=(other // sky, lax.rem(other, sky)), device_id_type=MESH
        )
        return carry

    lax.fori_loop(1, count, hello, 0)
    pl.semaphore_wait(barrier, count - 1)


def band(row, height, width, shift, out_width):
    full = pltpu.roll(
        jnp.broadcast_to(row, (height, width)), width - shift, 1, stride=1, stride_axis=0
    )
    return full[:, :out_width]


def same_row(count):
    left = lax.rem(lax.broadcasted_iota(jnp.int32, (count, count), 0), XB)
    right = lax.rem(lax.broadcasted_iota(jnp.int32, (count, count), 1), XB)
    return (left == right).astype(F32)


def step_kernel(
    bins, sky, scales, lags, groups, chunk, halo, tiles, half, area, src_of, dst_of,
    x_ref, mark_ref, tap_ref, pair_ref, fit_ref,
    result_ref, corr_ref,
    y_ref, marks_ref, hi_ref, lo_ref, g_ref, sums_ref, grad_ref,
    col_ref, adj_ref, part_ref, sky_ref, bin_in_ref, bin_ref,
    send_x, recv_x, send_m, recv_m, send_s, recv_s, send_b, recv_b, send_g, recv_g, own_sem, coef_ref,
):
    count = bins * sky
    strip_rows, width = y_ref.shape[1], y_ref.shape[2]
    pieces, part_width = grad_ref.shape[0], grad_ref.shape[3]
    span = adj_ref.shape[2]
    size = bins * XB
    rows = groups * XB
    my_bin, my_sky = lax.axis_index("bin"), lax.axis_index("sky")
    me = place(bins, sky)
    greet(me, bins, sky)

    def window_copy(other, slot):
        return pltpu.make_async_remote_copy(
            src_ref=src_of(x_ref, other),
            dst_ref=y_ref.at[slot],
            send_sem=send_x.at[other],
            recv_sem=recv_x.at[slot],
            device_id=(other // sky, lax.rem(other, sky)),
            device_id_type=MESH,
        )

    def along(axis, src, dst, send, recv, other, slot):
        return pltpu.make_async_remote_copy(
            src_ref=src,
            dst_ref=dst.at[slot],
            send_sem=send.at[other],
            recv_sem=recv.at[slot],
            device_id=(my_bin, other) if axis == "sky" else (other, my_sky),
            device_id_type=MESH,
        )

    def each(n, mine, act):
        def body(k, carry):
            act(lax.rem(mine + k, n))
            return carry

        lax.fori_loop(1, n, body, 0)

    each(sky, my_sky, lambda o: along("sky", mark_ref, marks_ref, send_m, recv_m, o, my_sky).start())
    each(count, me, lambda o: window_copy(o, me).start())
    own_mark = pltpu.make_async_copy(mark_ref, marks_ref.at[my_sky], own_sem.at[0])
    own_mark.start()
    own = pltpu.make_async_copy(src_of(x_ref, me), y_ref.at[me], own_sem.at[1])
    own.start()

    tall = tap_ref.shape[3]
    row_hi, row_lo, back_hi, back_lo = [], [], [], []
    narrow = round_up(rows + 2 * half + 1, 128)
    for s in range(scales):
        taps, turned = tap_ref[0, s], tap_ref[1, s]
        for at, part in enumerate(halves(band(turned[:, :width], width, width, half, width))):
            col_ref[at, s] = part
        for at, part in enumerate(
            halves(band(taps[:, :span], span, span, half + halo, part_width))
        ):
            adj_ref[at, s] = part
        a, b = halves(band(taps[:, :narrow], rows, narrow, half, rows))
        row_hi.append(a)
        row_lo.append(b)
        back = band(turned[:, :narrow], rows, narrow, half, rows)
        back_hi.append(back)
    row_hi = jnp.concatenate(row_hi, axis=0)
    row_lo = jnp.concatenate(row_lo, axis=0)
    back = halves(jnp.concatenate(back_hi, axis=1))
    diag = same_row(size)
    lanes = lax.broadcasted_iota(jnp.int32, (size, width), 1)
    owned = (lanes >= halo) & (lanes < halo + chunk)
    spot = lax.rem(lax.broadcasted_iota(jnp.int32, (bins, size), 1), XB)
    bin_row = lax.broadcasted_iota(jnp.int32, (bins, size), 0)

    pairs = fit_ref.shape[1]
    first = jnp.broadcast_to(pair_ref[:, 0:1], (pairs, size))
    second = jnp.broadcast_to(pair_ref[:, 1:2], (pairs, size))
    right_hot = lax.broadcasted_iota(jnp.int32, (pairs, size), 1) // XB == second
    weight = jnp.zeros((bins, size), F32)
    target = jnp.zeros((bins, size), F32)
    for i in range(bins):
        hot = right_hot & (first == i)
        weight_row = jnp.sum(jnp.where(hot, fit_ref[0], 0.0), axis=0, keepdims=True)
        target_row = jnp.sum(jnp.where(hot, fit_ref[1], 0.0), axis=0, keepdims=True)
        weight = jnp.where(bin_row == i, weight_row, weight)
        target = jnp.where(bin_row == i, target_row, target)
    sums_ref[...] = jnp.zeros_like(sums_ref)

    each(sky, my_sky, lambda o: along("sky", mark_ref, marks_ref, send_m, recv_m, o, o).wait())
    own_mark.wait()
    each(count, me, lambda o: window_copy(o, o).wait())
    own.wait()

    mark_width = mark_ref.shape[1]
    start = me * chunk - halo + 128
    marks = marks_ref[...].reshape(rows, mark_width)
    marks = pltpu.roll(marks, lax.rem(mark_width - start // 128, mark_width), 1)
    which = (lax.broadcasted_iota(jnp.int32, (rows, width), 1) + start) // 128 - start // 128
    mask = jnp.zeros((rows, width), F32)
    for t in range(tiles):
        mask = jnp.where(which == t, jnp.broadcast_to(marks[:, t : t + 1], (rows, width)), mask)
    masks = [
        jnp.concatenate([mask[g * XB : (g + 1) * XB]] * bins, axis=0) > 0 for g in range(groups)
    ]

    for b in range(bins):
        y = jnp.concatenate([y_ref[b * sky + k].astype(F32) for k in range(sky)], axis=0)
        y = y.astype(BF16)
        hi, lo = halves(mm(row_hi, y) + mm(row_lo, y))
        for s in range(scales):
            for g in range(groups):
                part = slice(s * rows + g * XB, s * rows + (g + 1) * XB)
                hi_ref[g, s, b * XB : (b + 1) * XB, :] = hi[part]
                lo_ref[g, s, b * XB : (b + 1) * XB, :] = lo[part]

    for g in range(groups):

        def forward(s, carry):
            matrix = (col_ref[0, s], col_ref[1, s])
            filtered = mm3((hi_ref[g, s], lo_ref[g, s]), matrix).astype(BF16).astype(F32)
            kept = jnp.where(masks[g], filtered, 0.0)
            g_ref[g, s] = kept.astype(BF16)
            left = jnp.where(owned, kept, 0.0).astype(BF16)
            for l in range(lags):
                right = kept if l == 0 else pltpu.roll(kept, width - l, 1)
                gram = lax.dot_general(
                    left, right.astype(BF16), (((1,), (1,)), ((), ())), preferred_element_type=F32
                )
                gram = jnp.sum((gram * diag).reshape(bins, XB, size), axis=1)
                sums_ref[s * lags + l] = sums_ref[s * lags + l] + gram
            return carry

        lax.fori_loop(0, scales, forward, 0)

    table = jnp.zeros((bins, size), F32)
    for at in range(scales * lags):
        value = sums_ref[at]
        for step in (16, 8, 4, 2, 1):
            value = value + pltpu.roll(value, size - step, 1)
        if at:
            value = pltpu.roll(value, at, 1)
        table = jnp.where(spot == at, value, table)

    part_ref[...] = table
    each(sky, my_sky, lambda o: along("sky", part_ref, sky_ref, send_s, recv_s, o, my_sky).start())
    sky_ref[pl.ds(my_sky, 1)] = table[None]
    each(sky, my_sky, lambda o: along("sky", part_ref, sky_ref, send_s, recv_s, o, o).wait())
    table = sky_ref[0]
    for k in range(1, sky):
        table = table + sky_ref[k]
    bin_in_ref[...] = table
    each(bins, my_bin, lambda o: along("bin", bin_in_ref, bin_ref, send_b, recv_b, o, my_bin).start())
    bin_ref[pl.ds(my_bin, 1)] = table[None]
    each(bins, my_bin, lambda o: along("bin", bin_in_ref, bin_ref, send_b, recv_b, o, o).wait())
    table = bin_ref[0]
    for k in range(1, bins):
        table = table + bin_ref[k]
    table = table * area

    picked = jnp.zeros((pairs, size), F32)
    for i in range(bins):
        picked = jnp.where(first == i, jnp.broadcast_to(table[i : i + 1], (pairs, size)), picked)
    picked = jnp.where(right_hot, picked, 0.0)
    step = size // 2
    while step >= XB:
        picked = picked + pltpu.roll(picked, step, 1)
        step //= 2
    corr_ref[...] = picked

    ahead = jnp.where(spot < scales * lags, weight * (table - target), 0.0)
    spread = jnp.broadcast_to(ahead[:, None, :], (bins, XB, size)).reshape(size, size)
    behind = jnp.sum(jnp.transpose(spread * diag).reshape(bins, XB, size), axis=1)

    def coefficient(values, at):
        value = jnp.where(spot == at, values, 0.0)
        value = pltpu.roll(value, lax.rem(size - at, size), 1)
        for step in (1, 2, 4, 8, 16):
            value = value + pltpu.roll(value, step, 1)
        return value

    def grad_copy(piece, other, slot):
        return pltpu.make_async_remote_copy(
            src_ref=grad_ref.at[piece, other],
            dst_ref=dst_of(result_ref, slot, piece),
            send_sem=send_g.at[piece, other],
            recv_sem=recv_g.at[piece, slot],
            device_id=(other // sky, lax.rem(other, sky)),
            device_id_type=MESH,
        )

    own_grads = []
    for piece in range(pieces):
        cut = slice(piece * part_width, piece * part_width + span)
        for g in range(groups):

            def backward(s, carry):
                maps = g_ref[g, s, :, cut].astype(F32)
                total_grad = jnp.zeros((size, span), F32)
                for shift in range(1 - lags, lags):
                    moved = maps if shift == 0 else pltpu.roll(maps, (span - shift) % span, 1)
                    moved = moved.astype(BF16)
                    at = s * (2 * lags - 1) + shift + lags - 1
                    if piece == 0:
                        if shift == 0:
                            coef = coefficient(ahead + behind, s * lags)
                        elif shift > 0:
                            coef = coefficient(ahead, s * lags + shift)
                        else:
                            coef = coefficient(behind, s * lags - shift)
                        if pieces > 1 or groups > 1:
                            coef_ref[at] = coef
                    else:
                        coef = coef_ref[at]
                    full = jnp.broadcast_to(coef[:, None, :], (bins, XB, size))
                    hi, lo = halves(full.reshape(size, size) * diag)
                    total_grad = total_grad + mm(hi, moved) + mm(lo, moved)
                total_grad = jnp.where(masks[g][:, cut], total_grad, 0.0)
                hi, lo = halves(mm3(halves(total_grad), (adj_ref[0, s], adj_ref[1, s])))
                hi_ref[g, s, :, :part_width] = hi
                lo_ref[g, s, :, :part_width] = lo
                return carry

            lax.fori_loop(0, scales, backward, 0)

        for b in range(bins):
            spots = [(g, s) for s in range(scales) for g in range(groups)]
            rows_of = slice(b * XB, (b + 1) * XB)
            hi = jnp.concatenate([hi_ref[g, s, rows_of, :part_width] for g, s in spots], axis=0)
            lo = jnp.concatenate([lo_ref[g, s, rows_of, :part_width] for g, s in spots], axis=0)
            total_rows = mm3(back, (hi, lo))
            for k in range(sky):
                at = b * sky + k
                grad_ref[piece, at] = total_rows[k * strip_rows : (k + 1) * strip_rows]

        each(count, me, lambda o: grad_copy(piece, o, me).start())
        own_grad = pltpu.make_async_copy(
            grad_ref.at[piece, me], dst_of(result_ref, me, piece), own_sem.at[2 + piece]
        )
        own_grad.start()
        own_grads.append(own_grad)
    for piece in range(pieces):
        each(count, me, lambda o: grad_copy(piece, o, o).wait())
        own_grads[piece].wait()


def per_device(lensing_maps, filter_taps, survey_mask, bin_pairs, target_corr, pair_weight):
    scales, tap_count = filter_taps.shape
    half = (tap_count - 1) // 2
    strip = lensing_maps[0]
    strip_rows, cols = strip.shape
    bins, sky = lax.axis_size("bin"), lax.axis_size("sky")
    count = bins * sky
    pairs, lags = pair_weight.shape[0], pair_weight.shape[2]
    row_count = strip_rows * sky
    groups = row_count // XB
    chunk = cols // count
    width = round_up(chunk + 2 * (2 * half + lags - 1), 128)
    halo = (width - chunk) // 2
    out_width = round_up(chunk, 128)
    tiles = width // 128 + 1
    size = bins * XB
    aligned = chunk % 128 == 0
    pieces = out_width // 128
    part_width = out_width // pieces
    span = width - (pieces - 1) * part_width

    windows = jnp.pad(strip, ((0, 0), (halo, halo)))
    if not aligned:
        windows = jnp.stack([windows[:, d * chunk : d * chunk + width] for d in range(count)])
    mark_width = round_up(survey_mask.shape[1] + 1 + tiles, 128)
    marks = jnp.pad(
        survey_mask.astype(F32), ((0, 0), (1, mark_width - survey_mask.shape[1] - 1))
    )
    marks = jnp.broadcast_to(marks, (strip_rows, mark_width))
    tall = max(width, round_up(row_count + 2 * half + 1, 128))
    taps = jnp.stack([filter_taps, filter_taps[:, ::-1]])
    taps = jnp.pad(taps, ((0, 0), (0, 0), (0, tall - tap_count)))[:, :, None, :]
    fit = jnp.stack([pair_weight, target_corr]).reshape(2, pairs, scales * lags)
    fit = jnp.tile(jnp.pad(fit, ((0, 0), (0, 0), (0, XB - scales * lags))), (1, 1, bins))

    if aligned:
        src_of = lambda ref, d: ref.at[:, pl.ds(pl.multiple_of(d * chunk, 128), width)]
        dst_of = lambda ref, d, p: ref.at[
            :, pl.ds(pl.multiple_of(d * chunk + p * part_width, 128), part_width)
        ]
        result_shape = (strip_rows, cols)
    else:
        src_of = lambda ref, d: ref.at[d]
        dst_of = lambda ref, d, p: ref.at[d]
        result_shape = (count, strip_rows, out_width)

    spec = pl.BlockSpec(memory_space=pltpu.VMEM)
    table_shape = (bins, size)
    dma = pltpu.SemaphoreType.DMA
    result, corr = pl.pallas_call(
        functools.partial(
            step_kernel, bins, sky, scales, lags, groups, chunk, halo, tiles, half,
            1.0 / (row_count * cols), src_of, dst_of,
        ),
        out_shape=(
            jax.ShapeDtypeStruct(result_shape, F32),
            jax.ShapeDtypeStruct((pairs, size), F32),
        ),
        in_specs=[spec] * 5,
        out_specs=(spec, spec),
        scratch_shapes=[
            pltpu.VMEM((count, strip_rows, width), BF16),
            pltpu.VMEM((sky, strip_rows, mark_width), F32),
            pltpu.VMEM((groups, scales, size, width), BF16),
            pltpu.VMEM((groups, scales, size, width), BF16),
            pltpu.VMEM((groups, scales, size, width), BF16),
            pltpu.VMEM((scales * lags,) + table_shape, F32),
            pltpu.VMEM((pieces, count, strip_rows, part_width), F32),
            pltpu.VMEM((2, scales, width, width), BF16),
            pltpu.VMEM((2, scales, span, part_width), BF16),
            pltpu.VMEM(table_shape, F32),
            pltpu.VMEM((sky,) + table_shape, F32),
            pltpu.VMEM(table_shape, F32),
            pltpu.VMEM((bins,) + table_shape, F32),
            dma((count,)), dma((count,)), dma((sky,)), dma((sky,)), dma((sky,)), dma((sky,)),
            dma((bins,)), dma((bins,)), dma((pieces, count)), dma((pieces, count)), dma((2 + pieces,)),
            pltpu.VMEM((scales * (2 * lags - 1),) + table_shape, F32),
        ],
        compiler_params=pltpu.CompilerParams(
            collective_id=1, has_side_effects=True, vmem_limit_bytes=VMEM_LIMIT
        ),
    )(windows, marks, taps, bin_pairs, fit)
    if not aligned:
        result = jnp.transpose(result[:, :, :chunk], (1, 0, 2)).reshape(strip_rows, cols)
    corr_table = corr[:, : scales * lags].reshape(pairs, scales, lags)
    return (corr_table, result[None])


def tables(bins, scales, lags):
    lane = lax.broadcasted_iota(jnp.int32, (bins, 128), 1)
    high, low = lane // 64, (lane // 8) % 2
    return lane, high, low, 2 * high + low


EARLY = 2


def spot_of(scale):
    return (0, scale) if scale < EARLY else (1, scale - EARLY)


def slot_rows(scale, lag):
    slot = spot_of(scale)[1]
    return 64 * (slot // 2) + 16 * lag + 8 * (slot % 2)


def thirds(value):
    hi = value.astype(BF16)
    rest = value - hi.astype(F32)
    mid = rest.astype(BF16)
    lo = (rest - mid.astype(F32)).astype(BF16)
    return hi, mid, lo


def nt(a, b):
    return lax.dot_general(a, b, (((1,), (1,)), ((), ())), preferred_element_type=F32)


def steps(begin, end, body, carry):
    for s in range(begin, end):
        carry = body(s, carry)
    return carry


def fast_kernel(
    bins, sky, scales, lags, chunk, half, area,
    x_hbm, tap_hbm, mask_hbm, pair_hbm, target_hbm, weight_hbm,
    result_ref, corr_ref,
    x_ref, tap_ref, mask_ref, pair_ref, target_ref, weight_ref,
    pad_ref, wide_ref, y_ref, cols_ref, mark_ref, marks_ref, mask_v_ref, mask_w_ref,
    row_hi_ref, row_lo_ref, back_hi_ref, back_lo_ref, fwd_ref, adj_ref,
    small_ref, fit_ref, pairs_ref, table_ref,
    g_ref, moved_ref, coef_ref, t_ref, cg_hi_ref, cg_lo_ref, out_ref, grad_ref, land_ref,
    part_ref, twin_ref, parts_ref,
    send_x, recv_x, recv_w, send_y, recv_y, send_m, recv_m, send_c, recv_c, send_t, recv_t, send_g, recv_g, in_sem,
):
    count = bins * sky
    cols = x_ref.shape[1]
    width = y_ref.shape[2]
    halo = (width - chunk) // 2
    pairs = pair_ref.shape[1]
    taps_n = tap_ref.shape[1]
    size = bins * XB
    groups = size // 32
    vregs = part_ref.shape[0]
    my_bin, my_sky = lax.axis_index("bin"), lax.axis_index("sky")
    me = place(bins, sky)

    barrier = pltpu.get_barrier_semaphore()

    bits = count.bit_length() - 1
    flips = [(1 - 2 * lax.rem(me // 2**i, 2)) * 2**i for i in range(bits)]

    def flipped(mask):
        other = me
        for i in range(bits):
            if (mask >> i) & 1:
                other = other + flips[i]
        return other

    def arrived(ref, sem):
        pltpu.make_async_copy(ref, ref, sem).wait()

    chips = count // 2
    far_first = range(chips - 1, 0, -1)

    def hello(other):
        pl.semaphore_signal(
            barrier, inc=1, device_id=(other // sky, lax.rem(other, sky)), device_id_type=MESH
        )

    hello(me + flips[0])
    for k in far_first:
        hello(flipped(2 * k))
    loads = [
        pltpu.make_async_copy(src, dst, in_sem.at[i])
        for i, (src, dst) in enumerate(
            (
                (x_hbm, x_ref), (mask_hbm, mask_ref), (tap_hbm, tap_ref),
                (pair_hbm, pair_ref), (target_hbm, target_ref), (weight_hbm, weight_ref),
            )
        )
    ]
    for load in loads:
        load.start()

    chip, core = me // 2, lax.rem(me, 2)
    twin = me + flips[0]
    wide = 2 * chunk + 2 * halo

    def remote(src, dst, send, recv, other):
        return pltpu.make_async_remote_copy(
            src_ref=src,
            dst_ref=dst,
            send_sem=send,
            recv_sem=recv,
            device_id=(other // sky, lax.rem(other, sky)),
            device_id_type=MESH,
        )

    def window_copy(k):
        other = flipped(2 * k)
        at = (1 - core) * chunk
        src = pad_ref.at[:, pl.ds(pl.multiple_of((other // 2) * 2 * chunk + at, 128), width)]
        dst = wide_ref.at[k, :, pl.ds(pl.multiple_of(at, 128), width)]
        return remote(src, dst, send_x.at[0], recv_x.at[k], other)

    def rest_copy(k):
        other = flipped(2 * k)
        at = core * width
        src = pad_ref.at[:, pl.ds(pl.multiple_of((other // 2) * 2 * chunk + at, 128), wide - width)]
        dst = wide_ref.at[k, :, pl.ds(pl.multiple_of(at, 128), wide - width)]
        return remote(src, dst, send_x.at[0], recv_w.at[k // 4], other)

    def twin_copy(k):
        src = wide_ref.at[k, :, pl.ds(pl.multiple_of((1 - core) * chunk, 128), width)]
        return remote(src, y_ref.at[k], send_y.at[0], recv_y.at[k // 4], twin)

    beside = me + flips[1]

    def mark_copy(n, slot, to):
        src = mark_ref if n < 2 else marks_ref.at[slot]
        return remote(src, marks_ref.at[slot], send_m.at[n], recv_m.at[n], to)

    loads[0].wait()
    loads[1].wait()
    moved_x = pltpu.roll(x_ref[...].astype(F32), halo, 1)
    edge = lax.broadcasted_iota(jnp.int32, (moved_x.shape[0], 128), 1) < halo
    pad_ref[:, :128] = jnp.where(edge, 0.0, moved_x[:, :128]).astype(BF16)
    pad_ref[:, 128:cols] = moved_x[:, 128:].astype(BF16)
    pad_ref[:, cols:] = jnp.where(edge, moved_x[:, :128], 0.0).astype(BF16)
    mark_ref[...] = jnp.zeros_like(mark_ref)
    mark_ref[:, : mask_ref.shape[1]] = jnp.broadcast_to(
        mask_ref[...].astype(F32), (mark_ref.shape[0], mask_ref.shape[1])
    )

    pl.semaphore_wait(barrier, count // 2)
    for k in far_first:
        window_copy(k).start()
    for k in far_first:
        rest_copy(k).start()
    mark_copy(0, my_sky, twin).start()
    mark_copy(1, my_sky, beside).start()
    at = pl.multiple_of(chip * 2 * chunk, 128)
    wide_ref[0] = pad_ref[:, pl.ds(at, wide)]
    twin_copy(0).start()
    marks_ref[pl.ds(my_sky, 1)] = mark_ref[...][None]

    for load in loads[2:]:
        load.wait()
    small_ref[...] = jnp.zeros_like(small_ref)
    small_ref[:scales, :taps_n] = tap_ref[...]
    tap_hi, tap_lo = halves(small_ref[...])
    tap_row = lax.broadcasted_iota(jnp.int32, (128, 256), 0)
    tap_col = lax.broadcasted_iota(jnp.int32, (128, 256), 1)
    real = tap_row < taps_n

    def spread(hot):
        hot = (hot & real).astype(F32).astype(BF16)
        return mm(tap_hi, hot) + mm(tap_lo, hot)

    straight = spread(tap_col == tap_row)
    turned = spread(tap_col == taps_n - 1 - tap_row)
    spaced = spread(tap_col == bins * (taps_n - 1 - tap_row))
    sub = lax.broadcasted_iota(jnp.int32, (bins, size), 0)
    col = lax.broadcasted_iota(jnp.int32, (bins, size), 1)
    turns = [pltpu.roll(straight, (XB * b - half) % size, 1) for b in range(bins)]
    for s in range(scales):
        reach = halo + half
        hi, lo = halves(band(turned[s : s + 1], 256, 256, reach, 128))
        fwd_ref[s, :, :128] = hi
        fwd_ref[s, :, 128:] = lo
        first = jnp.zeros((bins, size), F32)
        for b in range(bins):
            first = jnp.where(sub == b, jnp.broadcast_to(turns[b][s : s + 1], (bins, size)), first)
        tiles = [
            jnp.where(col // XB == sub, first if x == 0 else pltpu.roll(first, x, 1), 0.0)
            for x in range(XB)
        ]
        hi, lo = halves(jnp.concatenate(tiles, axis=0))
        row_hi_ref[s] = hi
        row_lo_ref[s] = lo

    lane, high, low, slot = tables(bins, scales, lags)
    pairs_ref[...] = jnp.full_like(pairs_ref, -1)
    pairs_ref[:2, :pairs] = pair_ref[...]
    fit_ref[...] = jnp.zeros_like(fit_ref)
    for s in range(scales):
        fit_ref[0, s, :lags, :pairs] = weight_ref[s]
        fit_ref[1, s, :lags, :pairs] = target_ref[s]
    bin_of = lax.broadcasted_iota(jnp.int32, (bins, 128), 0)
    first_hot = (pairs_ref[0:1, :] == bin_of).astype(F32)
    second_hot = pairs_ref[1:2, :] == bin_of
    first_hot16 = first_hot.astype(BF16)
    far = lax.rem(beside, sky)
    mark_copy(1, far, beside).wait()
    mark_copy(2, far, twin).start()
    mark_copy(0, lax.rem(twin, sky), twin).wait()
    mark_copy(2, lax.rem(beside + flips[0], sky), twin).wait()
    for k in range(sky):
        marks = pltpu.roll(marks_ref[k], 1, 1)
        marks = pltpu.roll(marks, lax.rem(128 - 2 * me, 128), 1)
        left, one, two, right = [jnp.broadcast_to(marks[:, t : t + 1], (8, 128)) for t in range(4)]
        lanes = lax.broadcasted_iota(jnp.int32, (8, 128), 1)
        mask_v_ref[k, :, :128] = one
        mask_v_ref[k, :, 128:256] = two
        mask_v_ref[k, :, 256:] = jnp.where(lanes < 64, right, left)
        mask_w_ref[k, :, :128] = jnp.where(lanes < 64, left, one)
        mask_w_ref[k, :, 128:256] = jnp.where(lanes < 64, one, two)
        mask_w_ref[k, :, 256:] = jnp.where(lanes < 64, two, right)

    def masked(value, ref):
        tall = size // sky
        return jnp.concatenate(
            [value[k * tall : (k + 1) * tall] * jnp.broadcast_to(ref[k, 0:1, :], (tall, width)) for k in range(sky)],
            axis=0,
        )

    def stacked(v):
        return jnp.concatenate(
            [v[:, :256], v[:, 128:], jnp.concatenate([v[:, 256:], v[:, :128]], axis=1)], axis=0
        )

    mine = pl.multiple_of(core * chunk, 128)

    def pass_on(layer):
        for k in range(4 * layer, 4 * layer + 4):
            if k:
                window_copy(k).wait_recv()
                twin_copy(k).start()

    def columns(layer):
        arrived(wide_ref.at[max(4 * layer, 1) : 4 * layer + 4, :, : wide - width], recv_w.at[layer])
        arrived(y_ref.at[4 * layer : 4 * layer + 4], recv_y.at[layer])
        first = (flipped(8 * layer) // 8) * 4
        rows = []
        for c in range(4):
            slot = 4 * layer + lax.rem(chip + c % 2, 2) + 2 * lax.rem(chip // 2 + c // 2, 2)
            direct = wide_ref[pl.ds(slot, 1), :, pl.ds(mine, width)][0].astype(F32)
            passed = y_ref[pl.ds(slot, 1)][0].astype(F32)
            rows.append(jnp.where(core == 0, direct, passed))
            rows.append(jnp.where(core == 1, direct, passed))
        y = stacked(jnp.concatenate(rows, axis=0).astype(BF16))
        tall = 2 * XB
        at = pl.multiple_of(first * 16, tall)
        for s in range(scales):
            p = mm(y, fwd_ref[s])
            f = p[:, :128] + p[:, 128:]
            hi, lo = halves(jnp.concatenate([f[:tall], f[tall : 2 * tall], f[2 * tall :]], axis=1))
            cols_ref[s, pl.ds(at, tall), :width] = hi
            cols_ref[s, pl.ds(at, tall), width:] = lo

    layers = count // 8
    pass_on(0)
    for layer in range(layers):
        if layer + 1 < layers:
            pass_on(layer + 1)
        columns(layer)

    def forward(s, carry):
        p = mm(row_hi_ref[s], cols_ref[s])
        q = mm(row_lo_ref[s], cols_ref[s, :, :width])
        f = p[:, :width] + p[:, width:] + q
        kept16 = masked(f, mask_v_ref).astype(BF16)
        g_ref[s] = kept16
        shifted = [kept16[:, l : l + chunk] for l in range(lags)]
        total = jnp.zeros((32, 128), F32)
        for g in range(groups):
            right = jnp.concatenate(
                [shifted[l][g * 32 + 16 * h : g * 32 + 16 * h + 16] for h in range(2) for l in range(lags)],
                axis=0,
            )
            total = total + nt(kept16[g * 32 : (g + 1) * 32, :chunk], right)
        z = jnp.zeros((bins, 128), F32)
        for x in range(4):
            z = jnp.where(slot == x, total[bins * x : bins * (x + 1)], z)
        z = z + pltpu.roll(z, 64, 1)
        z = z + jnp.where(low == 0, pltpu.roll(z, 120, 1), pltpu.roll(z, 8, 1))
        into = s if s < EARLY else s - EARLY
        return jnp.where(slot == into, z, carry)

    def core_copy(v):
        return pltpu.make_async_remote_copy(
            src_ref=part_ref.at[v],
            dst_ref=twin_ref.at[v],
            send_sem=send_c.at[v],
            recv_sem=recv_c.at[v],
            device_id=((me + flips[0]) // sky, lax.rem(me + flips[0], sky)),
            device_id_type=MESH,
        )

    def send_tables(v):
        core_copy(v).wait()
        parts_ref[v, 0] = part_ref[v] + twin_ref[v]
        for k in far_first:
            remote(parts_ref.at[v, 0], parts_ref.at[v, k], send_t.at[v], recv_t.at[v], flipped(2 * k)).start()

    zero = jnp.zeros((bins, 128), F32)
    part_ref[0] = steps(0, EARLY, forward, zero)
    core_copy(0).start()
    late = steps(EARLY, EARLY + 1, forward, zero)
    send_tables(0)
    part_ref[1] = steps(EARLY + 1, scales, forward, late)
    core_copy(1).start()

    def lagging(s, carry):
        kept = g_ref[s]
        for at in range(2 * lags - 1):
            cut = width - halo + (at - lags + 1)
            turn = jnp.concatenate([kept[:, cut:], kept[:, :cut]], axis=1)
            for g in range(groups):
                side = (g % 2) * width
                moved_ref[s, g // 2, at * 32 : (at + 1) * 32, side : side + width] = turn[g * 32 : (g + 1) * 32]
        return carry

    steps(0, 1, lagging, 0)
    send_tables(1)
    steps(1, scales, lagging, 0)

    for s in range(scales):
        hi, lo = halves(band(straight[s : s + 1], 256, 256, reach, 128))
        adj_ref[s, :, :128] = hi
        adj_ref[s, :, 128:] = lo
        first = pltpu.roll(
            jnp.broadcast_to(spaced[s : s + 1], (8, size)), 0, 1, stride=bins, stride_axis=0
        )
        tiles = []
        for b in range(bins):
            for k in range(XB // 8):
                shift = (bins * 8 * k - bins * half + b) % size
                apart = col // bins - sub - 8 * k
                near = (apart <= half) & (apart >= -half)
                tiles.append(jnp.where(near, first if shift == 0 else pltpu.roll(first, shift, 1), 0.0))
        hi, lo = halves(jnp.concatenate(tiles, axis=0))
        back_hi_ref[:, s * size : (s + 1) * size] = hi
        back_lo_ref[:, s * size : (s + 1) * size] = lo
    for at in range(2):
        for v in range(vregs):
            tiles = []
            for tile in range(16):
                at_slot, l = 2 * (tile // 8) + tile % 2, (tile // 2) % 4
                s = at_slot + v * EARLY
                if s < scales and spot_of(s) == (v, at_slot):
                    row = jnp.broadcast_to(fit_ref[at, s, l : l + 1, :], (bins, 128))
                    tiles.append(jnp.where(second_hot, row, 0.0))
                else:
                    tiles.append(jnp.zeros((bins, 128), F32))
            parts = thirds(jnp.concatenate(tiles, axis=0))
            table_ref[at, v] = nt(first_hot16, parts[0]) + nt(first_hot16, parts[1]) + nt(first_hot16, parts[2])


    e_row = lax.broadcasted_iota(jnp.int32, (128, 256), 0)
    e_col = lax.broadcasted_iota(jnp.int32, (128, 256), 1)
    place_hot = (e_row % 16 < 8) & (e_row // 16 == e_col // 32 - (lags - 1)) & (e_row % 8 == e_col % 8)
    place_hot = (place_hot & (e_row < 16 * lags)).astype(F32).astype(BF16)

    def coefficients(v, begin, end):
        arrived(parts_ref.at[v, 1:], recv_t.at[v])
        tables = [parts_ref[v, k] for k in range(chips)]
        while len(tables) > 1:
            tables = [tables[k] + tables[k + 1] for k in range(0, len(tables), 2)]
        total = tables[0] * area
        ahead = table_ref[0, v] * (total - table_ref[1, v])
        over = jnp.transpose(jnp.concatenate([ahead] * 16, axis=0))
        rows = []
        for s in range(begin, end):
            back = (128 - slot_rows(s, 0)) % 128
            value = ahead if back == 0 else pltpu.roll(ahead, back, 1)
            hi = value.astype(BF16).astype(F32)
            rows += [hi, value - hi]
        ahead_rows = mm(jnp.concatenate(rows, axis=0).astype(BF16), place_hot)
        for s in range(begin, end):
            behind = jnp.zeros((bins, 128), F32)
            for l in range(lags):
                at = slot_rows(s, l)
                behind = jnp.where(lane // 32 == lags - 1 - l, over[at : at + 8], behind)
            hi = behind.astype(BF16).astype(F32)
            tiles = []
            for at, value in ((0, hi), (1, behind - hi)):
                row = (2 * (s - begin) + at) * 8
                z = ahead_rows[row : row + 8]
                value = value.astype(BF16).astype(F32)
                for x in range(4):
                    near = (lane // 8) % 4 == x
                    tiles.append(
                        jnp.concatenate(
                            [jnp.where(near, z[:, :128] + value, 0.0), jnp.where(near, z[:, 128:], 0.0)], axis=1
                        )
                    )
            coef_ref[s] = jnp.concatenate(tiles, axis=0).astype(BF16)
        return total

    def backward(s, carry):
        coef = coef_ref[s][:, : 32 * (2 * lags - 1)]
        for g in range(0, groups, 2):
            t = mm(coef, moved_ref[s, g // 2])
            t = t[:32] + t[32:]
            t_ref[g * 32 : (g + 1) * 32, :] = t[:, :width]
            t_ref[(g + 1) * 32 : (g + 2) * 32, :] = t[:, width:]
        hi, lo = halves(masked(t_ref[...], mask_w_ref))
        p = mm(jnp.concatenate([hi[:, :256], hi[:, 128:]], axis=0), adj_ref[s])
        q = mm(jnp.concatenate([lo[:, :256], lo[:, 128:]], axis=0), adj_ref[s, :, :128])
        c = p[:, :128] + p[:, 128:] + q
        hi, lo = halves(jnp.concatenate([c[:size], c[size:]], axis=1))
        cg_hi_ref[s] = hi
        cg_lo_ref[s] = lo
        return carry

    totals = []
    for v, (begin, end) in enumerate(((0, EARLY), (EARLY, scales))):
        totals.append(coefficients(v, begin, end))
        steps(begin, end, backward, 0)
        deep = (end - begin) * size
        cg_hi = cg_hi_ref[begin:end].reshape(deep, chunk)
        cg_lo = cg_lo_ref[begin:end].reshape(deep, chunk)
        part = slice(begin * size, end * size)
        out = mm3((back_hi_ref[:, part], back_lo_ref[:, part]), (cg_hi, cg_lo))
        if v == 0:
            out_ref[...] = out
    out = out_ref[...] + out

    for k in range(count):
        block = out[8 * k : 8 * k + 8]
        largest = jnp.max(jnp.abs(block), axis=0, keepdims=True)
        largest = jnp.broadcast_to(jnp.max(largest, axis=1, keepdims=True), (8, 128))
        power = jnp.maximum(jnp.ceil(jnp.log2(jnp.maximum(largest, 1e-30)) + 0.001), -90.0)
        scale = jnp.exp2(15.0 - power) * (32766.0 / 32768.0)
        left = jnp.round(block[:, :128] * scale).astype(jnp.int32)
        right = jnp.round(block[:, 128:] * scale).astype(jnp.int32)
        grad_ref[k, :8] = left * 65536 + (right + 32768)
        grad_ref[k, 8:] = power[:1].astype(jnp.int32)

    for k in sorted(range(1, count), key=lambda k: (-(k % 8), -k)):
        other = flipped(k)
        remote(grad_ref.at[other], land_ref.at[k], send_g.at[0], recv_g.at[k // 8], other).start()
    land_ref[0] = grad_ref[pl.ds(me, 1)][0]

    hot = jnp.concatenate([first_hot16, jnp.zeros((128 - bins, 128), BF16)], axis=0)
    for v in range(vregs):
        parts = thirds(jnp.transpose(jnp.concatenate([totals[v]] * 16, axis=0)))
        picked = mm(parts[0], hot) + mm(parts[1], hot) + mm(parts[2], hot)
        for s in [s for s in range(scales) if spot_of(s)[0] == v]:
            for l in range(lags):
                at = slot_rows(s, l)
                value = jnp.sum(jnp.where(second_hot, picked[at : at + 8], 0.0), axis=0, keepdims=True)
                corr_ref[s, l : l + 1, :] = value[:, :pairs]

    for layer in range(count // 8):
        arrived(land_ref.at[max(8 * layer, 1) : 8 * layer + 8], recv_g.at[layer])
        for k in range(8 * layer, 8 * layer + 8):
            word = land_ref[k, :8]
            power = jnp.broadcast_to(land_ref[k, 8:], (8, 128)).astype(F32)
            scale = jnp.exp2(power - 15.0) * (32768.0 / 32766.0)
            at = pl.multiple_of(flipped(k) * chunk, 128)
            result_ref[:, pl.ds(at, 128)] = (word >> 16).astype(F32) * scale
            result_ref[:, pl.ds(at + 128, 128)] = ((word & 65535) - 32768).astype(F32) * scale

    arrived(wide_ref.at[1:], send_x.at[0])
    arrived(y_ref, send_y.at[0])
    for v in range(vregs):
        arrived(parts_ref.at[v, 1:], send_t.at[v])
    arrived(land_ref.at[1:], send_g.at[0])


def fast_device(lensing_maps, filter_taps, survey_mask, bin_pairs, target_corr, pair_weight):
    scales, tap_count = filter_taps.shape
    half = (tap_count - 1) // 2
    strip = lensing_maps[0]
    strip_rows, cols = strip.shape
    bins, sky = lax.axis_size("bin"), lax.axis_size("sky")
    count = bins * sky
    pairs, lags = pair_weight.shape[0], pair_weight.shape[2]
    chunk = cols // count
    width = chunk + 128
    size = bins * XB
    groups = size // 32
    vregs = 2
    spec = pl.BlockSpec(memory_space=pltpu.VMEM)
    dma = pltpu.SemaphoreType.DMA
    table = (vregs, bins, 128)
    result, corr = pl.pallas_call(
        functools.partial(fast_kernel, bins, sky, scales, lags, chunk, half, 1.0 / (strip_rows * sky * cols)),
        out_shape=(
            pltpu.VMEM((strip_rows, cols), F32),
            pltpu.VMEM((scales, lags, pairs), F32),
        ),
        in_specs=[pl.BlockSpec(memory_space=pl.ANY)] * 6,
        out_specs=(spec, spec),
        scratch_shapes=[
            pltpu.VMEM((strip_rows, cols), BF16),
            pltpu.VMEM(filter_taps.shape, F32),
            pltpu.VMEM(survey_mask.shape, jnp.int32),
            pltpu.VMEM((2, pairs), jnp.int32),
            pltpu.VMEM((scales, lags, pairs), F32),
            pltpu.VMEM((scales, lags, pairs), F32),
            pltpu.VMEM((strip_rows, cols + 128), BF16),
            pltpu.VMEM((count // 2, strip_rows, 2 * chunk + 128), BF16),
            pltpu.VMEM((count // 2, strip_rows, width), BF16),
            pltpu.VMEM((scales, size, 2 * width), BF16),
            pltpu.VMEM((8, 128), F32),
            pltpu.VMEM((sky, 8, 128), F32),
            pltpu.VMEM((sky, 8, width), F32),
            pltpu.VMEM((sky, 8, width), F32),
            pltpu.VMEM((scales, size, size), BF16),
            pltpu.VMEM((scales, size, size), BF16),
            pltpu.VMEM((size, scales * size), BF16),
            pltpu.VMEM((size, scales * size), BF16),
            pltpu.VMEM((scales, 256, 256), BF16),
            pltpu.VMEM((scales, 256, 256), BF16),
            pltpu.VMEM((8, 128), F32),
            pltpu.VMEM((2, scales, 8, 128), F32),
            pltpu.VMEM((8, 128), jnp.int32),
            pltpu.VMEM((2,) + table, F32),
            pltpu.VMEM((scales, size, width), BF16),
            pltpu.VMEM((scales, groups // 2, 32 * (2 * lags - 1), 2 * width), BF16),
            pltpu.VMEM((scales, 64, 256), BF16),
            pltpu.VMEM((size, width), F32),
            pltpu.VMEM((scales, size, chunk), BF16),
            pltpu.VMEM((scales, size, chunk), BF16),
            pltpu.VMEM((size, chunk), F32),
            pltpu.VMEM((count, strip_rows + 1, 128), jnp.int32),
            pltpu.VMEM((count, strip_rows + 1, 128), jnp.int32),
            pltpu.VMEM(table, F32),
            pltpu.VMEM(table, F32),
            pltpu.VMEM((vregs, count // 2, bins, 128), F32),
            dma((1,)), dma((count // 2,)), dma((count // 8,)), dma((1,)), dma((count // 8,)), dma((3,)), dma((3,)),
            dma((vregs,)), dma((vregs,)), dma((vregs,)), dma((vregs,)),
            dma((1,)), dma((count // 8,)), dma((6,)),
        ],
        compiler_params=pltpu.CompilerParams(
            collective_id=1, has_side_effects=True, vmem_limit_bytes=VMEM_LIMIT
        ),
    )(
        strip,
        filter_taps,
        survey_mask,
        bin_pairs.T,
        jnp.transpose(target_corr, (1, 2, 0)),
        jnp.transpose(pair_weight, (1, 2, 0)),
    )
    return (jnp.transpose(corr, (2, 0, 1)), result[None])


def fits(mesh, maps, taps, survey_mask, weight):
    bins, sky = mesh.shape["bin"], mesh.shape["sky"]
    rows, cols = maps.shape[1:]
    return (
        maps.shape[0] == bins == 8
        and rows == XB == 8 * sky
        and cols == 256 * bins * sky
        and survey_mask.shape == (sky, cols // 128)
        and EARLY < taps.shape[0] <= 6
        and taps.shape[1] == 17
        and weight.shape[0] <= 128
        and weight.shape[2] == 4
    )


def solution(mesh):
    placed = (P("bin", "sky", None), P(), P("sky", None), P(), P(), P())

    def step(lensing_maps, filter_taps, survey_mask, bin_pairs, target_corr, pair_weight):
        fast = fits(mesh, lensing_maps, filter_taps, survey_mask, pair_weight)
        return jax.shard_map(
            fast_device if fast else per_device,
            mesh=mesh,
            in_specs=placed,
            out_specs=(P(), P("bin", "sky", None)),
            check_vma=False,
        )(lensing_maps, filter_taps, survey_mask, bin_pairs, target_corr, pair_weight)

    return step
```
